32 devices in a mesh: grp: 2 (over x), seq: 16 (over z, y, core).
Axes of the slice: x: 2, y: 2, z: 4, core: 2. Of those that a mesh axis runs over, the one named last changes fastest.
Arguments:
- tokens: bfloat16 [4, 3072, 768], P('grp', 'seq'), may hold values from -6 to 6
- valid_len: int32 [4], P('grp'), may hold values from 768 to 3072, as said below
- query_weight: bfloat16 [768, 768], P(('grp', 'seq')), may hold values from -0.21875 to 0.21875
- query_bias: bfloat16 [768], P(('grp', 'seq')), may hold values from -3 to 3
- key_weight: bfloat16 [768, 768], P(('grp', 'seq')), may hold values from -0.21875 to 0.21875
- value_weight: bfloat16 [768, 768], P(('grp', 'seq')), may hold values from -0.21875 to 0.21875
- value_bias: bfloat16 [768], P(('grp', 'seq')), may hold values from -3 to 3
- output_weight: bfloat16 [768, 768], P(('grp', 'seq')), may hold values from -6 to 6
- output_bias: bfloat16 [768], P(('grp', 'seq')), may hold values from -3 to 3
- first_gain: bfloat16 [768], P(('grp', 'seq')), may hold values from 0.099609375 to 1.8984375
- first_shift: bfloat16 [768], P(('grp', 'seq')), may hold values from -3 to 3
- inner_weight: bfloat16 [768, 3072], P(('grp', 'seq')), may hold values from -0.21875 to 0.21875
- inner_bias: bfloat16 [3072], P(('grp', 'seq')), may hold values from -3 to 3
- outer_weight: bfloat16 [3072, 768], P(('grp', 'seq')), may hold values from -0.109375 to 0.109375
- outer_bias: bfloat16 [768], P(('grp', 'seq')), may hold values from -3 to 3
- second_gain: bfloat16 [768], P(('grp', 'seq')), may hold values from 0.099609375 to 1.8984375
- second_shift: bfloat16 [768], P(('grp', 'seq')), may hold values from -3 to 3
- grad_out: bfloat16 [4, 3072, 768], P('grp', 'seq'), may hold values from -6 to 6
Outputs:
- layer_output: bfloat16 [4, 3072, 768], P('grp', 'seq')
- dtokens: bfloat16 [4, 3072, 768], P('grp', 'seq')
- dquery_weight: float32 [768, 768], P('seq')
- dquery_bias: float32 [768], P('seq')
- dkey_weight: float32 [768, 768], P('seq')
- dvalue_weight: float32 [768, 768], P('seq')
- dvalue_bias: float32 [768], P('seq')
- doutput_weight: float32 [768, 768], P('seq')
- doutput_bias: float32 [768], P('seq')
- dfirst_gain: float32 [768], P('seq')
- dfirst_shift: float32 [768], P('seq')
- dinner_weight: float32 [768, 3072], P('seq')
- dinner_bias: float32 [3072], P('seq')
- douter_weight: float32 [3072, 768], P('seq')
- douter_bias: float32 [768], P('seq')
- dsecond_gain: float32 [768], P('seq')
- dsecond_shift: float32 [768], P('seq')
The draws below stay inside these ranges and needn't reach their ends.
Inputs may be any that keep to these rules, and one draw needn't show every extreme that they name: Sequence n takes only its first valid_len[n] positions as keys; in every draw some sequence takes all 3072.
All inputs are finite; a program needn't handle non-finite values.
Results may differ from the reference program's by a relative error of at most 0.023.
Values may be sent and summed in bfloat16 or wider, within the bound.
No kernel may reach another device: no remote copies, remote signals or barrier semaphores. Data moves between devices by JAX's collectives and lax.ppermute only.
A program may use at most 320 MiB of HBM per device.

```python
import jax
import jax.numpy as jnp
from jax import lax

D = 768
HEADS = 12
HEAD = 64
FF = 3072
LEN = 3072
SEQS = 4
QBLOCK = 512


def draw_valid_len(key, part):
    first_key, second_key = jax.random.split(key)
    lengths = jax.random.randint(first_key, (SEQS,), LEN // 4, LEN + 1)
    chosen = jax.random.randint(second_key, (), 0, SEQS)
    return jnp.where(jnp.arange(SEQS) == chosen, LEN, lengths).astype(jnp.int32)


def levels(key, shape, cuts, smallest, high):
    loudness = 1.0
    for dim, shards_of in cuts:
        steps = jax.random.uniform(jax.random.fold_in(jax.random.fold_in(key, 6), dim), (shards_of,), jnp.float32, smallest / len(cuts), high / len(cuts))
        loudness = loudness * jnp.repeat(jnp.exp(steps), shape[dim] // shards_of).reshape((-1,) + (1,) * (len(shape) - 1 - dim))
    return loudness


def bell_draw(stream_key, extent, deviation, limit, cuts=(), dtype=jnp.bfloat16):
    array = deviation * jax.random.normal(stream_key, extent, jnp.float32)
    if cuts:
        array = array * levels(stream_key, extent, cuts, -0.22, 0.18)
    return jnp.clip(array, -limit, limit).astype(dtype)


def setup_inputs(seed: int = 0) -> dict:
    key_of = jax.random.split(jax.random.key(seed), 19)
    return {
        "tokens": bell_draw(key_of[0], (SEQS, LEN, D), 1.0, 6.0, ((0, 2), (1, 16))),
        "valid_len": draw_valid_len(jax.random.fold_in(key_of[18], 71), 0),
        "query_weight": bell_draw(key_of[2], (D, D), D ** -0.5, 0.21875, ((0, 32),)),
        "query_bias": bell_draw(key_of[3], (D,), 0.5, 3.0, ((0, 32),)),
        "key_weight": bell_draw(key_of[4], (D, D), D ** -0.5, 0.21875, ((0, 32),)),
        "value_weight": bell_draw(key_of[5], (D, D), D ** -0.5, 0.21875, ((0, 32),)),
        "value_bias": bell_draw(key_of[6], (D,), 0.5, 3.0, ((0, 32),)),
        "output_weight": bell_draw(key_of[7], (D, D), 1.0, 6.0, ((0, 32),)),
        "output_bias": bell_draw(key_of[8], (D,), 0.5, 3.0, ((0, 32),)),
        "first_gain": jnp.clip(1.0 + 0.18 * jax.random.normal(key_of[9], (D,), jnp.float32), 0.099609375, 1.8984375).astype(jnp.bfloat16),
        "first_shift": bell_draw(key_of[10], (D,), 0.5, 3.0, ((0, 32),)),
        "inner_weight": bell_draw(key_of[11], (D, FF), D ** -0.5, 0.21875, ((0, 32),)),
        "inner_bias": bell_draw(key_of[12], (FF,), 0.5, 3.0, ((0, 32),)),
        "outer_weight": bell_draw(key_of[13], (FF, D), FF ** -0.5, 0.109375, ((0, 32),)),
        "outer_bias": bell_draw(key_of[14], (D,), 0.5, 3.0, ((0, 32),)),
        "second_gain": jnp.clip(1.0 + 0.18 * jax.random.normal(key_of[15], (D,), jnp.float32), 0.099609375, 1.8984375).astype(jnp.bfloat16),
        "second_shift": bell_draw(key_of[16], (D,), 0.5, 3.0, ((0, 32),)),
        "grad_out": bell_draw(key_of[17], (SEQS, LEN, D), 1.0, 6.0, ((0, 2), (1, 16))),
    }


@jax.custom_vjp
def low(v):
    return lax.optimization_barrier(v.astype(jnp.bfloat16)).astype(jnp.float32)

@jax.custom_vjp
def low_back(v):
    return v

def low_keep(v):
    return (low(v), None)

def low_pass(kept, grad):
    return (grad,)

def back_keep(v):
    return (v, None)

def back_low(kept, grad):
    return (low(grad),)
low.defvjp(low_keep, low_pass)
low_back.defvjp(back_keep, back_low)
highest = lax.Precision.HIGHEST
score_scale = 0.125
epsilon = 1e-12
masked_score = -1e+30

def matmul(left_side, right_side):
    return jnp.dot(left_side, right_side, precision=highest)

def layer_norm(hidden, norm_gain, norm_shift):
    centred = hidden - lax.optimization_barrier(jnp.mean(hidden, axis=-1, keepdims=True))
    spread = lax.optimization_barrier(jnp.mean(centred * centred, axis=-1, keepdims=True))
    return centred * lax.rsqrt(spread + epsilon) * norm_gain + norm_shift

def attend_rows(query_rows, key_rows, value_rows, key_valid):
    raw_scores = jnp.einsum('qhd,khd->hqk', query_rows, key_rows, precision=highest) * score_scale
    scores = low_back(jnp.where(key_valid[None, None, :], raw_scores, masked_score))
    weights = low(jax.nn.softmax(scores, axis=-1))
    return jnp.einsum('hqk,khd->qhd', weights, value_rows, precision=highest)

def sequence_forward(params, inputs, valid_count):
    query_weight, query_bias, key_weight, value_weight, value_bias, output_weight, output_bias, first_gain, first_shift, inner_weight, inner_bias, outer_weight, outer_bias, second_gain, second_shift = params
    length = inputs.shape[0]
    queries = low(low_back(matmul(inputs, query_weight) + query_bias)).reshape(length, HEADS, HEAD)
    key_rows = low(low_back(matmul(inputs, key_weight))).reshape(length, HEADS, HEAD)
    value_rows = low(low_back(matmul(inputs, value_weight) + value_bias)).reshape(length, HEADS, HEAD)
    key_valid = jnp.arange(length) < valid_count
    query_blocks = queries.reshape(length // QBLOCK, QBLOCK, HEADS, HEAD)

    def one_block(query_rows):
        return attend_rows(query_rows, key_rows, value_rows, key_valid)
    context = lax.map(jax.checkpoint(one_block), query_blocks).reshape(length, HEADS * HEAD)
    context = low(low_back(context))
    attn_out = low_back(matmul(context, output_weight) + output_bias)
    first_out = low(layer_norm(inputs + attn_out, first_gain, first_shift))
    inner_pre = low_back(matmul(first_out, inner_weight) + inner_bias)
    active = low(jax.nn.gelu(inner_pre, approximate=False))
    outer_out = low_back(matmul(active, outer_weight) + outer_bias)
    return layer_norm(first_out + outer_out, second_gain, second_shift)

def reference(tokens, valid_len, query_weight, query_bias, key_weight, value_weight, value_bias, output_weight, output_bias, first_gain, first_shift, inner_weight, inner_bias, outer_weight, outer_bias, second_gain, second_shift, grad_out):
    params = tuple((weight.astype(jnp.float32) for weight in (query_weight, query_bias, key_weight, value_weight, value_bias, output_weight, output_bias, first_gain, first_shift, inner_weight, inner_bias, outer_weight, outer_bias, second_gain, second_shift)))
    inputs = tokens.astype(jnp.float32)

    def forward(layer_params, layer_inputs):

        def one_sequence(sequence_pair):
            return sequence_forward(layer_params, sequence_pair[0], sequence_pair[1])
        return lax.map(one_sequence, (layer_inputs, valid_len))
    layer_out, pullback = jax.vjp(forward, params, inputs)
    gradients, dinputs = pullback(grad_out.astype(jnp.float32))
    return (layer_out.astype(jnp.bfloat16), dinputs.astype(jnp.bfloat16), gradients[0], gradients[1], gradients[2], gradients[3], gradients[4], gradients[5], gradients[6], gradients[7], gradients[8], gradients[9], gradients[10], gradients[11], gradients[12], gradients[13], gradients[14])
```

```python
from functools import partial

import jax
import jax.numpy as jnp
from jax import lax
from jax.sharding import PartitionSpec as P

HEADS = 12
HEAD = 64
HEAD_GROUPS = 4
GROUP_WIDTH = HEADS * HEAD // HEAD_GROUPS

score_scale = 0.125
epsilon = 1e-12
masked_score = -1e30


def log2_of(size):
    return size.bit_length() - 1


def flip(value, axis, size, mask):
    return lax.ppermute(value, axis, [(i, i ^ mask) for i in range(size)])


def in_order(mine, theirs, bit):
    return jnp.where(bit == 0, jnp.stack([mine, theirs]), jnp.stack([theirs, mine]))


def pick(pair, bit):
    return jnp.where(bit == 0, pair[0], pair[1])


def layer_norm(hidden, norm_gain, norm_shift):
    centred = hidden - jnp.mean(hidden, axis=-1, keepdims=True)
    spread = jnp.mean(centred * centred, axis=-1, keepdims=True)
    return centred * lax.rsqrt(spread + epsilon) * norm_gain + norm_shift


def dot(left, right):
    return jnp.dot(left, right, preferred_element_type=jnp.float32)


def dot_t(left, right):
    return lax.dot_general(left, right, (((1,), (1,)), ((), ())), preferred_element_type=jnp.float32)


def t_dot(left, right):
    return lax.dot_general(left, right, (((0,), (0,)), ((), ())), preferred_element_type=jnp.float32)


def column_sums(matrix):
    return jnp.sum(matrix.astype(jnp.float32), axis=0)


def attend_forward(queries, keys, values, bias):
    context, peaks = [], []
    for h in range(GROUP_WIDTH // HEAD):
        cols = slice(h * HEAD, (h + 1) * HEAD)
        scores = dot_t(queries[:, cols], keys[:, cols]) * score_scale + bias
        log_total = jax.nn.logsumexp(scores, axis=-1, keepdims=True)
        probs = jnp.exp(scores - log_total).astype(jnp.bfloat16)
        context.append(dot(probs, values[:, cols]))
        peaks.append(log_total)
    return jnp.concatenate(context, axis=1), peaks


def attend_backward(queries, keys, values, bias, peaks, context, dcontext):
    dq, dk, dv = [], [], []
    for h in range(GROUP_WIDTH // HEAD):
        cols = slice(h * HEAD, (h + 1) * HEAD)
        scores = dot_t(queries[:, cols], keys[:, cols]) * score_scale + bias
        probs = jnp.exp(scores - peaks[h])
        dprobs = dot_t(dcontext[:, cols], values[:, cols])
        delta = jnp.sum(dcontext[:, cols].astype(jnp.float32) * context[:, cols], axis=1, keepdims=True)
        dscores = (probs * (dprobs - delta)).astype(jnp.bfloat16)
        dq.append(dot(dscores, keys[:, cols]) * score_scale)
        dk.append(t_dot(dscores, queries[:, cols]) * score_scale)
        dv.append(t_dot(probs.astype(jnp.bfloat16), dcontext[:, cols]))
    return tuple(jnp.concatenate(part, axis=1) for part in (dq, dk, dv))


def per_device(
    seq_size,
    grp_size,
    tokens,
    valid_len,
    query_weight,
    query_bias,
    key_weight,
    value_weight,
    value_bias,
    output_weight,
    output_bias,
    first_gain,
    first_shift,
    inner_weight,
    inner_bias,
    outer_weight,
    outer_bias,
    second_gain,
    second_shift,
    grad_out,
):
    bf16 = jnp.bfloat16
    rows, width = tokens.shape[1:]
    feed = inner_weight.shape[1]
    shard = query_weight.shape[0]
    HI, ZO, YO = seq_size // 2, seq_size // 4, 2
    extra_bits = [1 << b for b in range(2, log2_of(ZO))]
    part_bits = [1] + extra_bits
    me = lax.axis_index("seq")
    grp = lax.axis_index("grp")
    z1 = me // HI
    z0 = (me // ZO) % 2
    y0 = (me // YO) % 2
    head_group = 2 * z0 + y0
    my_part = me % 2 + 2 * ((me // 4) % max(ZO // 4, 1))
    n_parts = seq_size // 8

    def sflip(value, mask):
        return flip(value, "seq", seq_size, mask)

    packed = jnp.concatenate(
        [
            jnp.concatenate([inner_weight[:, i * width : (i + 1) * width] for i in range(feed // width)], axis=0),
            outer_weight,
            output_weight,
        ],
        axis=0,
    )
    gathered = lax.all_gather(packed, ("grp", "seq"), axis=0, tiled=False)

    x_mine = pick(tokens, z1)
    x_sent = pick(tokens, 1 - z1)
    half_width = width // 2
    x_pair = in_order(x_mine, sflip(x_sent, HI), z1)
    xa, xb = x_pair[:, :, :half_width], x_pair[:, :, half_width:]
    ra, rb = sflip(xa, YO), sflip(xb, ZO)
    xa, xb = in_order(xa, ra, y0), in_order(xb, rb, z0)
    ra, rb = sflip(xa, ZO), sflip(xb, YO)
    xa, xb = in_order(xa, ra, z0), in_order(xb, rb, y0)
    x_all = jnp.concatenate([xa.transpose(2, 0, 1, 3, 4), xb.transpose(2, 1, 0, 3, 4)], axis=-1)
    x_all = x_all.reshape(8 * rows, width)

    smalls = jnp.concatenate(
        [query_bias, value_bias, output_bias, first_gain, first_shift, outer_bias, second_gain, second_shift, inner_bias]
    )
    small_rows = 32 - shard if shard == 24 else 8
    grouped = jnp.stack([query_weight, key_weight, value_weight]).reshape(3, shard, HEAD_GROUPS, GROUP_WIDTH)
    grouped = grouped.transpose(2, 1, 0, 3).reshape(HEAD_GROUPS, shard, 3 * GROUP_WIDTH)
    small_block = jnp.zeros((small_rows * 3 * GROUP_WIDTH,), bf16).at[: smalls.shape[0]].set(smalls)
    small_block = jnp.broadcast_to(small_block.reshape(1, small_rows, -1), (HEAD_GROUPS, small_rows, 3 * GROUP_WIDTH))
    grouped = jnp.concatenate([grouped, small_block], axis=1)

    def group_block(k):
        return lax.dynamic_index_in_dim(grouped, head_group ^ k, 0, keepdims=False)

    w0 = group_block(0)
    w1 = sflip(group_block(1), YO)
    w2 = sflip(group_block(2), ZO)
    w3 = sflip(group_block(3), ZO | YO)
    w_all = in_order(in_order(w0, w1, y0), in_order(w2, w3, y0), z0)
    w_all = in_order(w_all, sflip(w_all, HI), z1)
    names = ["z1", "z0", "y0"]
    for b in extra_bits:
        w_all = in_order(w_all, sflip(w_all, b), (me // b) % 2)
        names = ["e%d" % b] + names
    for b in range(log2_of(grp_size)):
        w_all = in_order(w_all, flip(w_all, "grp", grp_size, 1 << b), (grp >> b) % 2)
        names = ["g%d" % b] + names
    w_all = in_order(w_all, sflip(w_all, 1), me % 2)
    names = ["c"] + names
    wanted = ["g%d" % b for b in reversed(range(log2_of(grp_size)))] + ["z1", "z0"]
    wanted += ["e%d" % b for b in reversed(extra_bits)] + ["y0", "c"]
    n = len(names)
    w_all = w_all.transpose(*[names.index(w) for w in wanted], n, n + 1)
    w_all = w_all.reshape(grp_size * seq_size, shard + small_rows, 3 * GROUP_WIDTH)
    small_all = w_all[:, shard:].reshape(grp_size * seq_size, -1)[:, : smalls.shape[0]]
    vectors = [small_all[:, i * shard : (i + 1) * shard].reshape(-1).astype(jnp.float32) for i in range(8)]
    q_bias, v_bias, o_bias, gain1, shift1, out_bias, gain2, shift2 = vectors
    in_bias = small_all[:, 8 * shard :].reshape(-1).astype(jnp.float32)
    w_all = w_all[:, :shard].reshape(width, 3 * GROUP_WIDTH)

    def own_columns(vector):
        return lax.dynamic_slice_in_dim(vector, head_group * GROUP_WIDTH, GROUP_WIDTH)

    qkv_bias = jnp.concatenate([own_columns(q_bias), jnp.zeros((GROUP_WIDTH,), jnp.float32), own_columns(v_bias)])
    qkv = (dot(x_all, w_all) + qkv_bias).astype(bf16)
    queries = qkv[:, :GROUP_WIDTH]
    kv = qkv[:, GROUP_WIDTH:][None]
    for b in part_bits:
        bit = (me // b) % 2
        theirs = sflip(kv, b)
        kv = jnp.where(bit == 0, jnp.concatenate([kv, theirs]), jnp.concatenate([theirs, kv]))
    kv = kv.reshape(-1, 2 * GROUP_WIDTH)
    keys, values = kv[:, :GROUP_WIDTH], kv[:, GROUP_WIDTH:]

    part = jnp.arange(n_parts, dtype=jnp.int32)
    part_device = part % 2 + 4 * (part // 2)
    member = jnp.arange(8, dtype=jnp.int32)
    member_device = (member // 4) * HI + ((member // 2) % 2) * ZO + (member % 2) * YO
    device = part_device[:, None] + member_device[None, :]
    position = (device[:, :, None] * rows + jnp.arange(rows, dtype=jnp.int32)).reshape(-1)
    bias = jnp.where(position < pick(valid_len, z1), 0.0, masked_score)[None, :]

    context_full, peaks = attend_forward(queries, keys, values, bias)

    teams = [
        [a * HI + b * ZO + c * YO + q for a in range(2) for b in range(2) for c in range(2)]
        for q in [i % 2 + 4 * (i // 2) for i in range(n_parts)]
    ]

    def exchange(blocks):
        return lax.all_to_all(blocks, "seq", 0, 0, axis_index_groups=teams, tiled=True)

    context = exchange(context_full.astype(bf16).reshape(8, rows, GROUP_WIDTH))
    context = context.reshape(2, HEAD_GROUPS, rows, GROUP_WIDTH).transpose(0, 2, 1, 3).reshape(2 * rows, width)

    n_dev = grp_size * seq_size
    inner_rows = shard * (feed // width)
    inner_all = gathered[:, :inner_rows].reshape(n_dev, feed // width, shard, width)
    inner_all = inner_all.transpose(0, 2, 1, 3).reshape(width, feed)
    outer_all = gathered[:, inner_rows : inner_rows + outer_weight.shape[0]].reshape(feed, width)
    output_all = gathered[:, inner_rows + outer_weight.shape[0] :].reshape(width, width)

    home = tokens.reshape(2 * rows, width)
    cotangent = grad_out.reshape(2 * rows, width)
    hidden_one = home.astype(jnp.float32) + dot(context, output_all) + o_bias
    norm_one, norm_back_one = jax.vjp(layer_norm, hidden_one, gain1, shift1)
    first_out = norm_one.astype(bf16)
    inner_pre = dot(first_out, inner_all) + in_bias
    active_full, gelu_back = jax.vjp(partial(jax.nn.gelu, approximate=False), inner_pre)
    active = active_full.astype(bf16)
    hidden_two = first_out.astype(jnp.float32) + dot(active, outer_all) + out_bias
    layer_out, norm_back_two = jax.vjp(layer_norm, hidden_two, gain2, shift2)
    dhidden_two, dsecond_gain, dsecond_shift = norm_back_two(cotangent.astype(jnp.float32))
    douter = dhidden_two.astype(bf16)
    douter_weight = t_dot(active, douter)
    dinner = gelu_back(dot_t(douter, outer_all))[0].astype(bf16)
    dinner_weight = t_dot(first_out, dinner)
    dfirst = dhidden_two + dot_t(dinner, inner_all)
    dhidden_one, dfirst_gain, dfirst_shift = norm_back_one(dfirst)
    dattend = dhidden_one.astype(bf16)
    doutput_weight = t_dot(context, dattend)
    dcontext = dot_t(dattend, output_all).astype(bf16)
    dcontext = dcontext.reshape(2, rows, HEAD_GROUPS, GROUP_WIDTH).transpose(0, 2, 1, 3)
    dcontext = exchange(dcontext.reshape(8, rows, GROUP_WIDTH)).reshape(8 * rows, GROUP_WIDTH)

    out_rows = width // seq_size
    small_grads = [
        column_sums(dattend),
        dfirst_gain,
        dfirst_shift,
        column_sums(douter),
        dsecond_gain,
        dsecond_shift,
    ]
    small_grads = jnp.concatenate(
        [g.reshape(seq_size, out_rows) for g in small_grads] + [column_sums(dinner).reshape(seq_size, -1)], axis=1
    )
    n_small = small_grads.shape[1]
    small_grads = jnp.pad(small_grads, ((0, 0), (0, 8 * width - n_small))).reshape(seq_size, 8, width)
    dinner_blocks = dinner_weight.reshape(seq_size, out_rows, feed // width, width).transpose(0, 2, 1, 3)
    grads = jnp.concatenate(
        [
            dinner_blocks.reshape(seq_size, -1, width).astype(bf16),
            douter_weight.reshape(seq_size, -1, width).astype(bf16),
            doutput_weight.reshape(seq_size, -1, width).astype(bf16),
            small_grads.astype(bf16),
        ],
        axis=1,
    )
    grads = lax.psum_scatter(grads, "seq", scatter_dimension=0, tiled=False)
    for b in range(log2_of(grp_size)):
        grads = (grads.astype(jnp.float32) + flip(grads, "grp", grp_size, 1 << b).astype(jnp.float32)).astype(bf16)
    grads = grads.astype(jnp.float32)
    r1 = out_rows * (feed // width)
    r2 = r1 + feed // seq_size
    r3 = r2 + out_rows
    dinner_weight = grads[:r1].reshape(feed // width, out_rows, width).transpose(1, 0, 2).reshape(out_rows, feed)
    douter_weight = grads[r1:r2]
    doutput_weight = grads[r2:r3]
    small = grads[r3:].reshape(-1)[:n_small]
    doutput_bias, dfirst_gain, dfirst_shift, douter_bias, dsecond_gain, dsecond_shift = (
        small[i * out_rows : (i + 1) * out_rows] for i in range(6)
    )
    dinner_bias = small[6 * out_rows :]

    dqueries, dkeys, dvalues = attend_backward(queries, keys, values, bias, peaks, context_full, dcontext)
    dkv = jnp.concatenate([dkeys, dvalues], axis=1).reshape(n_parts, 8 * rows, 2 * GROUP_WIDTH)
    for b in reversed(part_bits):
        bit = (me // b) % 2
        n_now = dkv.shape[0] // 2
        low, high = dkv[:n_now], dkv[n_now:]
        sent = jnp.where(bit == 0, high, low).astype(bf16)
        dkv = jnp.where(bit == 0, low, high) + sflip(sent, b).astype(jnp.float32)
    dqkv = jnp.concatenate([dqueries.astype(bf16), dkv[0].astype(bf16)], axis=1)

    dx = dot_t(dqkv, w_all).reshape(2, 2, 2, rows, width)
    da, db = dx[..., :half_width], dx[..., half_width:]

    def halve(low, high, bit, mask):
        sent = jnp.where(bit == 0, high, low).astype(bf16)
        return jnp.where(bit == 0, low, high) + sflip(sent, mask).astype(jnp.float32)

    da = halve(da[:, :, 0], da[:, :, 1], y0, YO)
    db = halve(db[:, 0], db[:, 1], z0, ZO)
    da = halve(da[:, 0], da[:, 1], z0, ZO)
    db = halve(db[:, 0], db[:, 1], y0, YO)
    dx = jnp.concatenate([da, db], axis=-1)
    mine = pick(dx, z1)
    theirs = sflip(pick(dx, 1 - z1).astype(bf16), HI).astype(jnp.float32)
    dtokens = dhidden_one.reshape(2, rows, width) + in_order(mine, theirs, z1)

    dw = t_dot(x_all, dqkv)
    dbias = column_sums(dqkv)
    dw = dw.reshape(seq_size, out_rows, 3 * GROUP_WIDTH)
    dw = jnp.concatenate([dw, jnp.broadcast_to(dbias, (seq_size, 8, 3 * GROUP_WIDTH))], axis=1)
    block = dw.shape[1]
    n_extra = 1 << len(extra_bits)
    dw = dw.reshape(2, 2, 2, n_extra, 2, 1, block, 3 * GROUP_WIDTH)[:, :, :, :, :, 0]
    dw = dw.reshape(2, 2, n_extra, 2, 2, block, 3 * GROUP_WIDTH)
    dw = halve(dw[:, :, :, :, 0], dw[:, :, :, :, 1], me % 2, 1)
    for b in reversed(extra_bits):
        m = dw.shape[2] // 2
        dw = halve(dw[:, :, :m], dw[:, :, m:], (me // b) % 2, b)
    dw = dw[:, :, 0]
    dw = halve(dw[0], dw[1], z1, HI)
    for b in range(log2_of(grp_size)):
        dw = dw + flip(dw.astype(bf16), "grp", grp_size, 1 << b).astype(jnp.float32)
    dw = dw.astype(bf16).reshape(HEAD_GROUPS, block, 3 * GROUP_WIDTH)

    def row_block(k):
        return lax.dynamic_index_in_dim(dw, head_group ^ k, 0, keepdims=False)

    w0 = row_block(0)
    w1 = sflip(row_block(1), YO)
    w2 = sflip(row_block(2), ZO)
    w3 = sflip(row_block(3), ZO | YO)
    dw = in_order(in_order(w0, w1, y0), in_order(w2, w3, y0), z0).reshape(HEAD_GROUPS, block, 3, GROUP_WIDTH)
    dw = dw.astype(jnp.float32).transpose(2, 1, 0, 3).reshape(3, block, width)
    dquery_weight, dkey_weight, dvalue_weight = dw[0, :out_rows], dw[1, :out_rows], dw[2, :out_rows]
    dquery_bias = lax.dynamic_slice_in_dim(dw[0, out_rows], me * out_rows, out_rows)
    dvalue_bias = lax.dynamic_slice_in_dim(dw[2, out_rows], me * out_rows, out_rows)

    return (
        layer_out.astype(bf16).reshape(2, rows, width),
        dtokens.astype(bf16),
        dquery_weight,
        dquery_bias,
        dkey_weight,
        dvalue_weight,
        dvalue_bias,
        doutput_weight,
        doutput_bias,
        dfirst_gain,
        dfirst_shift,
        dinner_weight,
        dinner_bias,
        douter_weight,
        douter_bias,
        dsecond_gain,
        dsecond_shift,
    )


def solution(mesh):
    in_specs = (
        P("grp", "seq", None),
        P("grp"),
        P(("grp", "seq"), None),
        P(("grp", "seq")),
        P(("grp", "seq"), None),
        P(("grp", "seq"), None),
        P(("grp", "seq")),
        P(("grp", "seq"), None),
        P(("grp", "seq")),
        P(("grp", "seq")),
        P(("grp", "seq")),
        P(("grp", "seq"), None),
        P(("grp", "seq")),
        P(("grp", "seq"), None),
        P(("grp", "seq")),
        P(("grp", "seq")),
        P(("grp", "seq")),
        P("grp", "seq", None),
    )
    out_specs = (
        P("grp", "seq", None),
        P("grp", "seq", None),
        P("seq", None),
        P("seq"),
        P("seq", None),
        P("seq", None),
        P("seq"),
        P("seq", None),
        P("seq"),
        P("seq"),
        P("seq"),
        P("seq", None),
        P("seq"),
        P("seq", None),
        P("seq"),
        P("seq"),
        P("seq"),
    )
    body = partial(per_device, mesh.shape["seq"], mesh.shape["grp"])
    return jax.shard_map(
        body, mesh=mesh, in_specs=in_specs, out_specs=out_specs, check_vma=False
    )
```

```python
from functools import partial

import jax
import jax.numpy as jnp
from jax import lax
from jax.experimental import pallas as pl
from jax.experimental.pallas import tpu as pltpu
from jax.sharding import PartitionSpec as P

HEADS = 12
HEAD = 64
HEAD_GROUPS = 4
GROUP_WIDTH = HEADS * HEAD // HEAD_GROUPS
NH = HEADS // HEAD_GROUPS
BF16 = jnp.bfloat16
F32 = jnp.float32

score_scale = 0.125
epsilon = 1e-12
masked_score = -1e30


def log2_of(size):
    return size.bit_length() - 1


def flip(value, axis, size, mask):
    return lax.ppermute(value, axis, [(i, i ^ mask) for i in range(size)])


def in_order(mine, theirs, bit):
    return jnp.where(bit == 0, jnp.stack([mine, theirs]), jnp.stack([theirs, mine]))


def pick(pair, bit):
    return jnp.where(bit == 0, pair[0], pair[1])


def layer_norm(hidden, norm_gain, norm_shift):
    centred = hidden - jnp.mean(hidden, axis=-1, keepdims=True)
    spread = jnp.mean(centred * centred, axis=-1, keepdims=True)
    return centred * lax.rsqrt(spread + epsilon) * norm_gain + norm_shift


def dot(left, right):
    return jnp.dot(left, right, preferred_element_type=jnp.float32)


def dot_t(left, right):
    return lax.dot_general(left, right, (((1,), (1,)), ((), ())), preferred_element_type=jnp.float32)


def t_dot(left, right):
    return lax.dot_general(left, right, (((0,), (0,)), ((), ())), preferred_element_type=jnp.float32)


def column_sums(matrix):
    return jnp.sum(matrix.astype(jnp.float32), axis=0)


def thirds(x):
    hi=x.astype(BF16)
    r=x-hi.astype(F32)
    mid=r.astype(BF16)
    lo=(r-mid.astype(F32)).astype(BF16)
    return hi,mid,lo

def fwd_body(q_ref, kv_ref, kb_ref, c_ref, cf_ref, st_ref, kt, va, oacc, lacc, *, bq):
    i=pl.program_id(0); h=pl.program_id(1)
    W=NH*HEAD
    @pl.when((i==0)&(h==0))
    def _():
        tail=kb_ref[:,HEAD:]
        for g in range(NH):
            ka=jnp.concatenate([kv_ref[:,g*HEAD:(g+1)*HEAD],tail],axis=1)
            kt[g]=ka.T
            va[g]=jnp.concatenate([kv_ref[:,W+g*HEAD:W+(g+1)*HEAD],tail],axis=1)
    one=jnp.where(lax.broadcasted_iota(jnp.int32,(bq,HEAD),1)==0,1.0,0.0).astype(BF16)
    def head(g):
        qa=jnp.concatenate([q_ref[:,g*HEAD:(g+1)*HEAD],one],axis=1)
        s=dot(qa,kt[g])
        m=jnp.max(s,axis=1,keepdims=True)
        p=jnp.exp(s-m).astype(BF16)
        o=dot(p,va[g])
        l=o[:,HEAD+1:HEAD+2]
        oacc[g]=o/l
        lacc[g]=jnp.broadcast_to(m+jnp.log(l),(bq,128))
    for g in range(NH):
        @pl.when(h==g)
        def _(): head(g)
    @pl.when(h==NH-1)
    def _():
        c=jnp.concatenate([oacc[g][:,:HEAD] for g in range(NH)],axis=1)
        c_ref[...]=c.astype(BF16)
        cf_ref[...]=c
        lane=lax.broadcasted_iota(jnp.int32,(bq,128),1)
        st=lacc[0]
        for g in range(1,NH): st=jnp.where(lane==g,lacc[g],st)
        st_ref[...]=st

def attend_forward(q,kv,kb,bq=256):
    n,W=q.shape; L=kv.shape[0]
    return pl.pallas_call(partial(fwd_body,bq=bq),
        grid=(n//bq,NH),
        in_specs=[pl.BlockSpec((bq,W),lambda i,h:(i,0)),pl.BlockSpec((L,2*W),lambda i,h:(0,0)),pl.BlockSpec((L,128),lambda i,h:(0,0))],
        out_specs=[pl.BlockSpec((bq,W),lambda i,h:(i,0)),pl.BlockSpec((bq,W),lambda i,h:(i,0)),pl.BlockSpec((bq,128),lambda i,h:(i,0))],
        out_shape=[jax.ShapeDtypeStruct((n,W),BF16),jax.ShapeDtypeStruct((n,W),F32),jax.ShapeDtypeStruct((n,128),F32)],
        scratch_shapes=[pltpu.VMEM((NH,128,L),BF16),pltpu.VMEM((NH,L,128),BF16),pltpu.VMEM((NH,bq,128),F32),pltpu.VMEM((NH,bq,128),F32)],
        name="attend_forward",
    )(q,kv,kb)

def bwd_body(q_ref, kv_ref, kb_ref, cf_ref, st_ref, dc_ref, dq_ref, dkv_ref, qt, qn, dct, dcn, dqt, dk, dv, *, bk, nk):
    j=pl.program_id(0); h=pl.program_id(1)
    W=NH*HEAD
    n=q_ref.shape[0]
    @pl.when((j==0)&(h==0))
    def _():
        lane=lax.broadcasted_iota(jnp.int32,(n,HEAD),1)
        def tail(x,first):
            hi,mid,lo=thirds(-x)
            z=jnp.where(lane==1,hi.astype(F32),jnp.where(lane==2,mid.astype(F32),jnp.where(lane==3,lo.astype(F32),0.0)))
            return jnp.where(lane==0,first,z).astype(BF16)
        for g in range(NH):
            cols=slice(g*HEAD,(g+1)*HEAD)
            qa=jnp.concatenate([q_ref[:,cols],tail(st_ref[:,g:g+1],1.0)],axis=1)
            qn[g]=qa
            qt[g]=qa.T
            d=dc_ref[:,cols]
            delta=jnp.sum(d.astype(F32)*cf_ref[:,cols],axis=1,keepdims=True)
            da=jnp.concatenate([d,tail(delta,0.0)],axis=1)
            dcn[g]=da
            dct[g]=da.T
        dqt[...]=jnp.zeros_like(dqt)
    tail=kb_ref[:,HEAD:]
    def head(g):
        k=kv_ref[:,g*HEAD:(g+1)*HEAD]
        ka=jnp.concatenate([k,tail],axis=1)
        va=jnp.concatenate([kv_ref[:,W+g*HEAD:W+(g+1)*HEAD],tail],axis=1)
        p=jnp.exp(dot(ka,qt[g]))
        dp=dot(va,dct[g])
        ds=(p*dp).astype(BF16)
        dv[g]=dot(p.astype(BF16),dcn[g])
        dk[g]=dot(ds,qn[g])
        dqt[g]=dqt[g]+t_dot(ka,ds)[:HEAD]
    for g in range(NH):
        @pl.when(h==g)
        def _(): head(g)
    @pl.when(h==NH-1)
    def _():
        dkv_ref[...]=jnp.concatenate([dk[g][:,:HEAD] for g in range(NH)]+[dv[g][:,:HEAD] for g in range(NH)],axis=1)
    @pl.when((h==NH-1)&(j==nk-1))
    def _():
        for g in range(NH):
            dq_ref[:,g*HEAD:(g+1)*HEAD]=(dqt[g].T*0.125).astype(BF16)

def attend_backward(q,kv,kb,cf,st,dc,bk=512):
    n,W=q.shape; L=kv.shape[0]; nk=L//bk
    full=lambda a: pl.BlockSpec(a.shape,lambda j,h:(0,0))
    return pl.pallas_call(partial(bwd_body,bk=bk,nk=nk),
        grid=(nk,NH),
        in_specs=[full(q),pl.BlockSpec((bk,2*W),lambda j,h:(j,0)),pl.BlockSpec((bk,128),lambda j,h:(j,0)),full(cf),full(st),full(dc)],
        out_specs=[pl.BlockSpec((n,W),lambda j,h:(0,0)),pl.BlockSpec((bk,2*W),lambda j,h:(j,0))],
        out_shape=[jax.ShapeDtypeStruct((n,W),BF16),jax.ShapeDtypeStruct((L,2*W),F32)],
        scratch_shapes=[pltpu.VMEM((NH,128,n),BF16),pltpu.VMEM((NH,n,128),BF16),pltpu.VMEM((NH,128,n),BF16),pltpu.VMEM((NH,n,128),BF16),
            pltpu.VMEM((NH,HEAD,n),F32),pltpu.VMEM((NH,bk,128),F32),pltpu.VMEM((NH,bk,128),F32)],
        name="attend_backward",
    )(q,kv,kb,cf,st,dc)


def per_device(
    seq_size,
    grp_size,
    tokens,
    valid_len,
    query_weight,
    query_bias,
    key_weight,
    value_weight,
    value_bias,
    output_weight,
    output_bias,
    first_gain,
    first_shift,
    inner_weight,
    inner_bias,
    outer_weight,
    outer_bias,
    second_gain,
    second_shift,
    grad_out,
):
    bf16 = jnp.bfloat16
    rows, width = tokens.shape[1:]
    feed = inner_weight.shape[1]
    shard = query_weight.shape[0]
    HI, ZO, YO = seq_size // 2, seq_size // 4, 2
    extra_bits = [1 << b for b in range(2, log2_of(ZO))]
    part_bits = [1] + extra_bits
    me = lax.axis_index("seq")
    grp = lax.axis_index("grp")
    z1 = me // HI
    z0 = (me // ZO) % 2
    y0 = (me // YO) % 2
    head_group = 2 * z0 + y0
    my_part = me % 2 + 2 * ((me // 4) % max(ZO // 4, 1))
    n_parts = seq_size // 8

    def sflip(value, mask):
        return flip(value, "seq", seq_size, mask)

    packed = jnp.concatenate(
        [
            jnp.concatenate([inner_weight[:, i * width : (i + 1) * width] for i in range(feed // width)], axis=0),
            outer_weight,
            output_weight,
        ],
        axis=0,
    )
    gathered = lax.all_gather(packed, ("grp", "seq"), axis=0, tiled=False)

    x_mine = pick(tokens, z1)
    x_sent = pick(tokens, 1 - z1)
    half_width = width // 2
    x_pair = in_order(x_mine, sflip(x_sent, HI), z1)
    xa, xb = x_pair[:, :, :half_width], x_pair[:, :, half_width:]
    ra, rb = sflip(xa, YO), sflip(xb, ZO)
    xa, xb = in_order(xa, ra, y0), in_order(xb, rb, z0)
    ra, rb = sflip(xa, ZO), sflip(xb, YO)
    xa, xb = in_order(xa, ra, z0), in_order(xb, rb, y0)
    x_all = jnp.concatenate([xa.transpose(2, 0, 1, 3, 4), xb.transpose(2, 1, 0, 3, 4)], axis=-1)
    x_all = x_all.reshape(8 * rows, width)

    smalls = jnp.concatenate(
        [query_bias, value_bias, output_bias, first_gain, first_shift, outer_bias, second_gain, second_shift, inner_bias]
    )
    small_rows = 32 - shard if shard == 24 else 8
    grouped = jnp.stack([query_weight, key_weight, value_weight]).reshape(3, shard, HEAD_GROUPS, GROUP_WIDTH)
    grouped = grouped.transpose(2, 1, 0, 3).reshape(HEAD_GROUPS, shard, 3 * GROUP_WIDTH)
    small_block = jnp.zeros((small_rows * 3 * GROUP_WIDTH,), bf16).at[: smalls.shape[0]].set(smalls)
    small_block = jnp.broadcast_to(small_block.reshape(1, small_rows, -1), (HEAD_GROUPS, small_rows, 3 * GROUP_WIDTH))
    grouped = jnp.concatenate([grouped, small_block], axis=1)

    def group_block(k):
        return lax.dynamic_index_in_dim(grouped, head_group ^ k, 0, keepdims=False)

    w0 = group_block(0)
    w1 = sflip(group_block(1), YO)
    w2 = sflip(group_block(2), ZO)
    w3 = sflip(group_block(3), ZO | YO)
    w_all = in_order(in_order(w0, w1, y0), in_order(w2, w3, y0), z0)
    w_all = in_order(w_all, sflip(w_all, HI), z1)
    names = ["z1", "z0", "y0"]
    for b in extra_bits:
        w_all = in_order(w_all, sflip(w_all, b), (me // b) % 2)
        names = ["e%d" % b] + names
    for b in range(log2_of(grp_size)):
        w_all = in_order(w_all, flip(w_all, "grp", grp_size, 1 << b), (grp >> b) % 2)
        names = ["g%d" % b] + names
    w_all = in_order(w_all, sflip(w_all, 1), me % 2)
    names = ["c"] + names
    wanted = ["g%d" % b for b in reversed(range(log2_of(grp_size)))] + ["z1", "z0"]
    wanted += ["e%d" % b for b in reversed(extra_bits)] + ["y0", "c"]
    n = len(names)
    w_all = w_all.transpose(*[names.index(w) for w in wanted], n, n + 1)
    w_all = w_all.reshape(grp_size * seq_size, shard + small_rows, 3 * GROUP_WIDTH)
    small_all = w_all[:, shard:].reshape(grp_size * seq_size, -1)[:, : smalls.shape[0]]
    vectors = [small_all[:, i * shard : (i + 1) * shard].reshape(-1).astype(jnp.float32) for i in range(8)]
    q_bias, v_bias, o_bias, gain1, shift1, out_bias, gain2, shift2 = vectors
    in_bias = small_all[:, 8 * shard :].reshape(-1).astype(jnp.float32)
    w_all = w_all[:, :shard].reshape(width, 3 * GROUP_WIDTH)

    def own_columns(vector):
        return lax.dynamic_slice_in_dim(vector, head_group * GROUP_WIDTH, GROUP_WIDTH)

    qkv_bias = jnp.concatenate([own_columns(q_bias), jnp.zeros((GROUP_WIDTH,), jnp.float32), own_columns(v_bias)])
    qkv = dot(x_all, w_all) + qkv_bias
    queries = (qkv[:, :GROUP_WIDTH] * score_scale).astype(bf16)
    kv = qkv[:, GROUP_WIDTH:].astype(bf16)[None]
    for b in part_bits:
        bit = (me // b) % 2
        theirs = sflip(kv, b)
        kv = jnp.where(bit == 0, jnp.concatenate([kv, theirs]), jnp.concatenate([theirs, kv]))
    kv = kv.reshape(-1, 2 * GROUP_WIDTH)

    part = jnp.arange(n_parts, dtype=jnp.int32)
    part_device = part % 2 + 4 * (part // 2)
    member = jnp.arange(8, dtype=jnp.int32)
    member_device = (member // 4) * HI + ((member // 2) % 2) * ZO + (member % 2) * YO
    device = part_device[:, None] + member_device[None, :]
    position = (device[:, :, None] * rows + jnp.arange(rows, dtype=jnp.int32)).reshape(-1)
    bias = jnp.where(position < pick(valid_len, z1), 0.0, masked_score)[:, None]
    lane = jnp.arange(128, dtype=jnp.int32)[None, :]
    key_tail = jnp.where(lane == HEAD, bias, jnp.where((lane > HEAD) & (lane < HEAD + 4), 1.0, 0.0)).astype(bf16)

    context, context_full, stats = attend_forward(queries, kv, key_tail)

    teams = [
        [a * HI + b * ZO + c * YO + q for a in range(2) for b in range(2) for c in range(2)]
        for q in [i % 2 + 4 * (i // 2) for i in range(n_parts)]
    ]

    def exchange(blocks):
        return lax.all_to_all(blocks, "seq", 0, 0, axis_index_groups=teams, tiled=True)

    context = exchange(context.reshape(8, rows, GROUP_WIDTH))
    context = context.reshape(2, HEAD_GROUPS, rows, GROUP_WIDTH).transpose(0, 2, 1, 3).reshape(2 * rows, width)

    n_dev = grp_size * seq_size
    inner_rows = shard * (feed // width)
    inner_all = gathered[:, :inner_rows].reshape(n_dev, feed // width, shard, width)
    inner_all = inner_all.transpose(0, 2, 1, 3).reshape(width, feed)
    outer_all = gathered[:, inner_rows : inner_rows + outer_weight.shape[0]].reshape(feed, width)
    output_all = gathered[:, inner_rows + outer_weight.shape[0] :].reshape(width, width)

    home = tokens.reshape(2 * rows, width)
    cotangent = grad_out.reshape(2 * rows, width)
    hidden_one = home.astype(jnp.float32) + dot(context, output_all) + o_bias
    norm_one, norm_back_one = jax.vjp(layer_norm, hidden_one, gain1, shift1)
    first_out = norm_one.astype(bf16)
    inner_pre = dot(first_out, inner_all) + in_bias
    active_full, gelu_back = jax.vjp(partial(jax.nn.gelu, approximate=False), inner_pre)
    active = active_full.astype(bf16)
    hidden_two = first_out.astype(jnp.float32) + dot(active, outer_all) + out_bias
    layer_out, norm_back_two = jax.vjp(layer_norm, hidden_two, gain2, shift2)
    dhidden_two, dsecond_gain, dsecond_shift = norm_back_two(cotangent.astype(jnp.float32))
    douter = dhidden_two.astype(bf16)
    douter_weight = t_dot(active, douter)
    dinner = gelu_back(dot_t(douter, outer_all))[0].astype(bf16)
    dinner_weight = t_dot(first_out, dinner)
    dfirst = dhidden_two + dot_t(dinner, inner_all)
    dhidden_one, dfirst_gain, dfirst_shift = norm_back_one(dfirst)
    dattend = dhidden_one.astype(bf16)
    doutput_weight = t_dot(context, dattend)
    dcontext = dot_t(dattend, output_all).astype(bf16)
    dcontext = dcontext.reshape(2, rows, HEAD_GROUPS, GROUP_WIDTH).transpose(0, 2, 1, 3)
    dcontext = exchange(dcontext.reshape(8, rows, GROUP_WIDTH)).reshape(8 * rows, GROUP_WIDTH)

    out_rows = width // seq_size
    small_grads = [
        column_sums(dattend),
        dfirst_gain,
        dfirst_shift,
        column_sums(douter),
        dsecond_gain,
        dsecond_shift,
    ]
    small_grads = jnp.concatenate(
        [g.reshape(seq_size, out_rows) for g in small_grads] + [column_sums(dinner).reshape(seq_size, -1)], axis=1
    )
    n_small = small_grads.shape[1]
    small_grads = jnp.pad(small_grads, ((0, 0), (0, 8 * width - n_small))).reshape(seq_size, 8, width)
    dinner_blocks = dinner_weight.reshape(seq_size, out_rows, feed // width, width).transpose(0, 2, 1, 3)
    grads = jnp.concatenate(
        [
            dinner_blocks.reshape(seq_size, -1, width).astype(bf16),
            douter_weight.reshape(seq_size, -1, width).astype(bf16),
            doutput_weight.reshape(seq_size, -1, width).astype(bf16),
            small_grads.astype(bf16),
        ],
        axis=1,
    )
    grads = lax.psum_scatter(grads, "seq", scatter_dimension=0, tiled=False)
    for b in range(log2_of(grp_size)):
        grads = (grads.astype(jnp.float32) + flip(grads, "grp", grp_size, 1 << b).astype(jnp.float32)).astype(bf16)
    grads = grads.astype(jnp.float32)
    r1 = out_rows * (feed // width)
    r2 = r1 + feed // seq_size
    r3 = r2 + out_rows
    dinner_weight = grads[:r1].reshape(feed // width, out_rows, width).transpose(1, 0, 2).reshape(out_rows, feed)
    douter_weight = grads[r1:r2]
    doutput_weight = grads[r2:r3]
    small = grads[r3:].reshape(-1)[:n_small]
    doutput_bias, dfirst_gain, dfirst_shift, douter_bias, dsecond_gain, dsecond_shift = (
        small[i * out_rows : (i + 1) * out_rows] for i in range(6)
    )
    dinner_bias = small[6 * out_rows :]

    dqueries, dkv = attend_backward(queries, kv, key_tail, context_full, stats, dcontext)
    dkv = dkv.reshape(n_parts, 8 * rows, 2 * GROUP_WIDTH)
    for b in reversed(part_bits):
        bit = (me // b) % 2
        n_now = dkv.shape[0] // 2
        low, high = dkv[:n_now], dkv[n_now:]
        sent = jnp.where(bit == 0, high, low).astype(bf16)
        dkv = jnp.where(bit == 0, low, high) + sflip(sent, b).astype(jnp.float32)
    dqkv = jnp.concatenate([dqueries, dkv[0].astype(bf16)], axis=1)

    dx = dot_t(dqkv, w_all).reshape(2, 2, 2, rows, width)
    da, db = dx[..., :half_width], dx[..., half_width:]

    def halve(low, high, bit, mask):
        sent = jnp.where(bit == 0, high, low).astype(bf16)
        return jnp.where(bit == 0, low, high) + sflip(sent, mask).astype(jnp.float32)

    da = halve(da[:, :, 0], da[:, :, 1], y0, YO)
    db = halve(db[:, 0], db[:, 1], z0, ZO)
    da = halve(da[:, 0], da[:, 1], z0, ZO)
    db = halve(db[:, 0], db[:, 1], y0, YO)
    dx = jnp.concatenate([da, db], axis=-1)
    mine = pick(dx, z1)
    theirs = sflip(pick(dx, 1 - z1).astype(bf16), HI).astype(jnp.float32)
    dtokens = dhidden_one.reshape(2, rows, width) + in_order(mine, theirs, z1)

    dw = t_dot(x_all, dqkv)
    dbias = column_sums(dqkv)
    dw = dw.reshape(seq_size, out_rows, 3 * GROUP_WIDTH)
    dw = jnp.concatenate([dw, jnp.broadcast_to(dbias, (seq_size, 8, 3 * GROUP_WIDTH))], axis=1)
    block = dw.shape[1]
    n_extra = 1 << len(extra_bits)
    dw = dw.reshape(2, 2, 2, n_extra, 2, 1, block, 3 * GROUP_WIDTH)[:, :, :, :, :, 0]
    dw = dw.reshape(2, 2, n_extra, 2, 2, block, 3 * GROUP_WIDTH)
    dw = halve(dw[:, :, :, :, 0], dw[:, :, :, :, 1], me % 2, 1)
    for b in reversed(extra_bits):
        m = dw.shape[2] // 2
        dw = halve(dw[:, :, :m], dw[:, :, m:], (me // b) % 2, b)
    dw = dw[:, :, 0]
    dw = halve(dw[0], dw[1], z1, HI)
    for b in range(log2_of(grp_size)):
        dw = dw + flip(dw.astype(bf16), "grp", grp_size, 1 << b).astype(jnp.float32)
    dw = dw.astype(bf16).reshape(HEAD_GROUPS, block, 3 * GROUP_WIDTH)

    def row_block(k):
        return lax.dynamic_index_in_dim(dw, head_group ^ k, 0, keepdims=False)

    w0 = row_block(0)
    w1 = sflip(row_block(1), YO)
    w2 = sflip(row_block(2), ZO)
    w3 = sflip(row_block(3), ZO | YO)
    dw = in_order(in_order(w0, w1, y0), in_order(w2, w3, y0), z0).reshape(HEAD_GROUPS, block, 3, GROUP_WIDTH)
    dw = dw.astype(jnp.float32).transpose(2, 1, 0, 3).reshape(3, block, width)
    dquery_weight, dkey_weight, dvalue_weight = dw[0, :out_rows], dw[1, :out_rows], dw[2, :out_rows]
    dquery_bias = lax.dynamic_slice_in_dim(dw[0, out_rows], me * out_rows, out_rows)
    dvalue_bias = lax.dynamic_slice_in_dim(dw[2, out_rows], me * out_rows, out_rows)

    return (
        layer_out.astype(bf16).reshape(2, rows, width),
        dtokens.astype(bf16),
        dquery_weight,
        dquery_bias,
        dkey_weight,
        dvalue_weight,
        dvalue_bias,
        doutput_weight,
        doutput_bias,
        dfirst_gain,
        dfirst_shift,
        dinner_weight,
        dinner_bias,
        douter_weight,
        douter_bias,
        dsecond_gain,
        dsecond_shift,
    )


def solution(mesh):
    in_specs = (
        P("grp", "seq", None),
        P("grp"),
        P(("grp", "seq"), None),
        P(("grp", "seq")),
        P(("grp", "seq"), None),
        P(("grp", "seq"), None),
        P(("grp", "seq")),
        P(("grp", "seq"), None),
        P(("grp", "seq")),
        P(("grp", "seq")),
        P(("grp", "seq")),
        P(("grp", "seq"), None),
        P(("grp", "seq")),
        P(("grp", "seq"), None),
        P(("grp", "seq")),
        P(("grp", "seq")),
        P(("grp", "seq")),
        P("grp", "seq", None),
    )
    out_specs = (
        P("grp", "seq", None),
        P("grp", "seq", None),
        P("seq", None),
        P("seq"),
        P("seq", None),
        P("seq", None),
        P("seq"),
        P("seq", None),
        P("seq"),
        P("seq"),
        P("seq"),
        P("seq", None),
        P("seq"),
        P("seq", None),
        P("seq"),
        P("seq"),
        P("seq"),
    )
    body = partial(per_device, mesh.shape["seq"], mesh.shape["grp"])
    return jax.shard_map(
        body, mesh=mesh, in_specs=in_specs, out_specs=out_specs, check_vma=False
    )
```

```python
from functools import partial

import jax
import jax.numpy as jnp
from jax import lax
from jax.experimental import pallas as pl
from jax.experimental.pallas import tpu as pltpu
from jax.sharding import PartitionSpec as P

HEADS = 12
HEAD = 64
HEAD_GROUPS = 4
GROUP_WIDTH = HEADS * HEAD // HEAD_GROUPS
NH = HEADS // HEAD_GROUPS
BF16 = jnp.bfloat16
F32 = jnp.float32

score_scale = 0.125
epsilon = 1e-12
masked_score = -1e30


def log2_of(size):
    return size.bit_length() - 1


def flip(value, axis, size, mask):
    return lax.ppermute(value, axis, [(i, i ^ mask) for i in range(size)])


def in_order(mine, theirs, bit):
    return jnp.where(bit == 0, jnp.stack([mine, theirs]), jnp.stack([theirs, mine]))


def pick(pair, bit):
    return jnp.where(bit == 0, pair[0], pair[1])


def layer_norm(hidden, norm_gain, norm_shift):
    centred = hidden - jnp.mean(hidden, axis=-1, keepdims=True)
    spread = jnp.mean(centred * centred, axis=-1, keepdims=True)
    return centred * lax.rsqrt(spread + epsilon) * norm_gain + norm_shift


def dot(left, right):
    return jnp.dot(left, right, preferred_element_type=jnp.float32)


def dot_t(left, right):
    return lax.dot_general(left, right, (((1,), (1,)), ((), ())), preferred_element_type=jnp.float32)


def t_dot(left, right):
    return lax.dot_general(left, right, (((0,), (0,)), ((), ())), preferred_element_type=jnp.float32)


def column_sums(matrix):
    return jnp.sum(matrix.astype(jnp.float32), axis=0)


def thirds(x):
    hi=x.astype(BF16)
    r=x-hi.astype(F32)
    mid=r.astype(BF16)
    lo=(r-mid.astype(F32)).astype(BF16)
    return hi,mid,lo

def fwd_body(q_ref, kv_ref, kb_ref, c_ref, cf_ref, st_ref, kt, va, oacc, lacc, *, bq):
    i=pl.program_id(0); h=pl.program_id(1)
    W=NH*HEAD
    @pl.when((i==0)&(h==0))
    def _():
        tail=kb_ref[:,HEAD:]
        for g in range(NH):
            ka=jnp.concatenate([kv_ref[:,g*HEAD:(g+1)*HEAD],tail],axis=1)
            kt[g]=ka.T
            va[g]=jnp.concatenate([kv_ref[:,W+g*HEAD:W+(g+1)*HEAD],tail],axis=1)
    one=jnp.where(lax.broadcasted_iota(jnp.int32,(bq,HEAD),1)==0,1.0,0.0).astype(BF16)
    def head(g):
        qa=jnp.concatenate([q_ref[:,g*HEAD:(g+1)*HEAD],one],axis=1)
        s=dot(qa,kt[g])
        m=jnp.max(s,axis=1,keepdims=True)
        p=jnp.exp(s-m).astype(BF16)
        o=dot(p,va[g])
        l=o[:,HEAD+1:HEAD+2]
        oacc[g]=o/l
        lacc[g]=jnp.broadcast_to(m+jnp.log(l),(bq,128))
    for g in range(NH):
        @pl.when(h==g)
        def _(): head(g)
    @pl.when(h==NH-1)
    def _():
        c=jnp.concatenate([oacc[g][:,:HEAD] for g in range(NH)],axis=1)
        c_ref[...]=c.astype(BF16)
        cf_ref[...]=c
        lane=lax.broadcasted_iota(jnp.int32,(bq,128),1)
        st=lacc[0]
        for g in range(1,NH): st=jnp.where(lane==g,lacc[g],st)
        st_ref[...]=st

def attend_forward(q,kv,kb,bq=256):
    n,W=q.shape; L=kv.shape[0]
    return pl.pallas_call(partial(fwd_body,bq=bq),
        grid=(n//bq,NH),
        in_specs=[pl.BlockSpec((bq,W),lambda i,h:(i,0)),pl.BlockSpec((L,2*W),lambda i,h:(0,0)),pl.BlockSpec((L,128),lambda i,h:(0,0))],
        out_specs=[pl.BlockSpec((bq,W),lambda i,h:(i,0)),pl.BlockSpec((bq,W),lambda i,h:(i,0)),pl.BlockSpec((bq,128),lambda i,h:(i,0))],
        out_shape=[jax.ShapeDtypeStruct((n,W),BF16),jax.ShapeDtypeStruct((n,W),F32),jax.ShapeDtypeStruct((n,128),F32)],
        scratch_shapes=[pltpu.VMEM((NH,128,L),BF16),pltpu.VMEM((NH,L,128),BF16),pltpu.VMEM((NH,bq,128),F32),pltpu.VMEM((NH,bq,128),F32)],
        name="attend_forward",
    )(q,kv,kb)

def bwd_body(q_ref, kv_ref, kb_ref, cf_ref, st_ref, dc_ref, dq_ref, dkv_ref, qt, qn, dct, dcn, dqt, dk, dv, *, bk, nk):
    j=pl.program_id(0); h=pl.program_id(1)
    W=NH*HEAD
    n=q_ref.shape[0]
    @pl.when((j==0)&(h==0))
    def _():
        lane=lax.broadcasted_iota(jnp.int32,(n,HEAD),1)
        def tail(x,first):
            hi,mid,lo=thirds(-x)
            z=jnp.where(lane==1,hi.astype(F32),jnp.where(lane==2,mid.astype(F32),jnp.where(lane==3,lo.astype(F32),0.0)))
            return jnp.where(lane==0,first,z).astype(BF16)
        for g in range(NH):
            cols=slice(g*HEAD,(g+1)*HEAD)
            qa=jnp.concatenate([q_ref[:,cols],tail(st_ref[:,g:g+1],1.0)],axis=1)
            qn[g]=qa
            qt[g]=qa.T
            d=dc_ref[:,cols]
            delta=jnp.sum(d.astype(F32)*cf_ref[:,cols],axis=1,keepdims=True)
            da=jnp.concatenate([d,tail(delta,0.0)],axis=1)
            dcn[g]=da
            dct[g]=da.T
        dqt[...]=jnp.zeros_like(dqt)
    tail=kb_ref[:,HEAD:]
    def head(g):
        k=kv_ref[:,g*HEAD:(g+1)*HEAD]
        ka=jnp.concatenate([k,tail],axis=1)
        va=jnp.concatenate([kv_ref[:,W+g*HEAD:W+(g+1)*HEAD],tail],axis=1)
        p=jnp.exp(dot(ka,qt[g]))
        dp=dot(va,dct[g])
        ds=(p*dp).astype(BF16)
        dv[g]=dot(p.astype(BF16),dcn[g])
        dk[g]=dot(ds,qn[g])
        dqt[g]=dqt[g]+t_dot(ka,ds)[:HEAD]
    for g in range(NH):
        @pl.when(h==g)
        def _(): head(g)
    @pl.when(h==NH-1)
    def _():
        dkv_ref[...]=jnp.concatenate([dk[g][:,:HEAD] for g in range(NH)]+[dv[g][:,:HEAD] for g in range(NH)],axis=1)
    @pl.when((h==NH-1)&(j==nk-1))
    def _():
        for g in range(NH):
            dq_ref[:,g*HEAD:(g+1)*HEAD]=(dqt[g].T*0.125).astype(BF16)

def attend_backward(q,kv,kb,cf,st,dc,bk=512):
    n,W=q.shape; L=kv.shape[0]; nk=L//bk
    full=lambda a: pl.BlockSpec(a.shape,lambda j,h:(0,0))
    return pl.pallas_call(partial(bwd_body,bk=bk,nk=nk),
        grid=(nk,NH),
        in_specs=[full(q),pl.BlockSpec((bk,2*W),lambda j,h:(j,0)),pl.BlockSpec((bk,128),lambda j,h:(j,0)),full(cf),full(st),full(dc)],
        out_specs=[pl.BlockSpec((n,W),lambda j,h:(0,0)),pl.BlockSpec((bk,2*W),lambda j,h:(j,0))],
        out_shape=[jax.ShapeDtypeStruct((n,W),BF16),jax.ShapeDtypeStruct((L,2*W),F32)],
        scratch_shapes=[pltpu.VMEM((NH,128,n),BF16),pltpu.VMEM((NH,n,128),BF16),pltpu.VMEM((NH,128,n),BF16),pltpu.VMEM((NH,n,128),BF16),
            pltpu.VMEM((NH,HEAD,n),F32),pltpu.VMEM((NH,bk,128),F32),pltpu.VMEM((NH,bk,128),F32)],
        name="attend_backward",
    )(q,kv,kb,cf,st,dc)


def weight_grads_body(y_ref, dz_ref, a_ref, do_ref, ctx_ref, da_ref, vec_ref, out_ref, *, chips):
    width = y_ref.shape[1]
    r_in, r_ctx = width // chips, ctx_ref.shape[1] // chips
    r_out = a_ref.shape[1] // chips
    for j in range(2):
        grad = t_dot(y_ref[...], dz_ref[:, j * width : (j + 1) * width]).astype(BF16)
        for q in range(chips):
            out_ref[q, j * r_in : (j + 1) * r_in] = grad[q * r_in : (q + 1) * r_in]
        grad = t_dot(a_ref[:, j * width : (j + 1) * width], do_ref[...]).astype(BF16)
        half = chips // 2
        for q in range(half):
            out_ref[j * half + q, 2 * r_in : 2 * r_in + r_out] = grad[q * r_out : (q + 1) * r_out]
    first = 2 * r_in + r_out
    grad = t_dot(ctx_ref[...], da_ref[...]).astype(BF16)
    for q in range(chips):
        out_ref[q, first : first + r_ctx] = grad[q * r_ctx : (q + 1) * r_ctx]
    own = vec_ref.shape[0]
    n = da_ref.shape[0] // 2
    ones = jnp.ones((16, y_ref.shape[0]), BF16)
    sums = [dot(ones[:, :n], da_ref[:n])[:1], dot(ones[:, :n], do_ref[:n])[:1]]
    sums += [dot(ones, dz_ref[:, j * width : (j + 1) * width])[:1] for j in range(2)]
    small = jnp.concatenate([vec_ref[...]] + sums, axis=0).astype(BF16)
    for q in range(chips):
        out_ref[q, first + r_ctx : first + r_ctx + own + 4] = small


def weight_grads(y, dz, a, do, ctx, da, vec, chips):
    width = y.shape[1]
    total = 2 * width // chips + a.shape[1] // chips + ctx.shape[1] // chips + vec.shape[0] + 4
    return pl.pallas_call(
        partial(weight_grads_body, chips=chips),
        out_shape=jax.ShapeDtypeStruct((chips, total, width), BF16),
        name="weight_grads",
    )(y, dz, a, do, ctx, da, vec)


def per_device(
    seq_size,
    grp_size,
    tokens,
    valid_len,
    query_weight,
    query_bias,
    key_weight,
    value_weight,
    value_bias,
    output_weight,
    output_bias,
    first_gain,
    first_shift,
    inner_weight,
    inner_bias,
    outer_weight,
    outer_bias,
    second_gain,
    second_shift,
    grad_out,
):
    bf16 = jnp.bfloat16
    rows, width = tokens.shape[1:]
    feed = inner_weight.shape[1]
    shard = query_weight.shape[0]
    HI, ZO, YO = seq_size // 2, seq_size // 4, 2
    extra_bits = [1 << b for b in range(2, log2_of(ZO))]
    part_bits = [1] + extra_bits
    me = lax.axis_index("seq")
    grp = lax.axis_index("grp")
    z1 = me // HI
    z0 = (me // ZO) % 2
    y0 = (me // YO) % 2
    head_group = 2 * z0 + y0
    my_part = me % 2 + 2 * ((me // 4) % max(ZO // 4, 1))
    n_parts = seq_size // 8

    def sflip(value, mask):
        return flip(value, "seq", seq_size, mask)

    core = me % 2
    chips = seq_size // 2
    piece = feed // seq_size
    n_dev = grp_size * seq_size
    half_feed = feed // 2
    split = inner_weight.reshape(shard, chips, 2, piece)
    split = [split[:, :, i].reshape(shard, 2, width).transpose(1, 0, 2).reshape(2 * shard, width) for i in range(2)]
    near = jnp.concatenate([pick(split, 1 - core), output_weight], axis=0)
    far = sflip(near, 1)
    outer_far = lax.ppermute(
        outer_weight,
        ("grp", "seq"),
        [(d, d ^ (1 | grp_size) if d % 2 != (d // grp_size) % 2 else d) for d in range(n_dev)],
    )
    inner_pair = in_order(pick(split, core).reshape(2, shard, width), far[: 2 * shard].reshape(2, shard, width), core)
    packed = jnp.concatenate(
        [
            inner_pair.transpose(1, 0, 2, 3).reshape(4 * shard, width),
            outer_far,
            in_order(output_weight, far[2 * shard :], core).reshape(2 * shard, width),
        ],
        axis=0,
    )
    same_core = [[2 * d + i for d in range(n_dev // 2)] for i in range(2)]
    gathered = lax.all_gather(packed, ("grp", "seq"), axis=0, tiled=False, axis_index_groups=same_core)

    x_mine = pick(tokens, z1)
    x_sent = pick(tokens, 1 - z1)
    half_width = width // 2
    x_pair = in_order(x_mine, sflip(x_sent, HI), z1)
    xa, xb = x_pair[:, :, :half_width], x_pair[:, :, half_width:]
    ra, rb = sflip(xa, YO), sflip(xb, ZO)
    xa, xb = in_order(xa, ra, y0), in_order(xb, rb, z0)
    ra, rb = sflip(xa, ZO), sflip(xb, YO)
    xa, xb = in_order(xa, ra, z0), in_order(xb, rb, y0)
    x_all = jnp.concatenate([xa.transpose(2, 0, 1, 3, 4), xb.transpose(2, 1, 0, 3, 4)], axis=-1)
    x_all = x_all.reshape(8 * rows, width)

    smalls = jnp.concatenate(
        [query_bias, value_bias, output_bias, first_gain, first_shift, outer_bias, second_gain, second_shift, inner_bias]
    )
    small_rows = 32 - shard if shard == 24 else 8
    grouped = jnp.stack([query_weight, key_weight, value_weight]).reshape(3, shard, HEAD_GROUPS, GROUP_WIDTH)
    grouped = grouped.transpose(2, 1, 0, 3).reshape(HEAD_GROUPS, shard, 3 * GROUP_WIDTH)
    small_block = jnp.zeros((small_rows * 3 * GROUP_WIDTH,), bf16).at[: smalls.shape[0]].set(smalls)
    small_block = jnp.broadcast_to(small_block.reshape(1, small_rows, -1), (HEAD_GROUPS, small_rows, 3 * GROUP_WIDTH))
    grouped = jnp.concatenate([grouped, small_block], axis=1)

    def group_block(k):
        return lax.dynamic_index_in_dim(grouped, head_group ^ k, 0, keepdims=False)

    w0 = group_block(0)
    w1 = sflip(group_block(1), YO)
    w2 = sflip(group_block(2), ZO)
    w3 = sflip(group_block(3), ZO | YO)
    w_all = in_order(in_order(w0, w1, y0), in_order(w2, w3, y0), z0)
    w_all = in_order(w_all, sflip(w_all, HI), z1)
    names = ["z1", "z0", "y0"]
    for b in extra_bits:
        w_all = in_order(w_all, sflip(w_all, b), (me // b) % 2)
        names = ["e%d" % b] + names
    for b in range(log2_of(grp_size)):
        w_all = in_order(w_all, flip(w_all, "grp", grp_size, 1 << b), (grp >> b) % 2)
        names = ["g%d" % b] + names
    w_all = in_order(w_all, sflip(w_all, 1), me % 2)
    names = ["c"] + names
    wanted = ["g%d" % b for b in reversed(range(log2_of(grp_size)))] + ["z1", "z0"]
    wanted += ["e%d" % b for b in reversed(extra_bits)] + ["y0", "c"]
    n = len(names)
    w_all = w_all.transpose(*[names.index(w) for w in wanted], n, n + 1)
    w_all = w_all.reshape(grp_size * seq_size, shard + small_rows, 3 * GROUP_WIDTH)
    small_all = w_all[:, shard:].reshape(grp_size * seq_size, -1)[:, : smalls.shape[0]]
    vectors = [small_all[:, i * shard : (i + 1) * shard].reshape(-1).astype(jnp.float32) for i in range(8)]
    q_bias, v_bias, o_bias, gain1, shift1, out_bias, gain2, shift2 = vectors
    in_bias = small_all[:, 8 * shard :].reshape(-1).astype(jnp.float32)
    w_all = w_all[:, :shard].reshape(width, 3 * GROUP_WIDTH)

    def own_columns(vector):
        return lax.dynamic_slice_in_dim(vector, head_group * GROUP_WIDTH, GROUP_WIDTH)

    qkv_bias = jnp.concatenate([own_columns(q_bias), jnp.zeros((GROUP_WIDTH,), jnp.float32), own_columns(v_bias)])
    qkv = dot(x_all, w_all) + qkv_bias
    queries = (qkv[:, :GROUP_WIDTH] * score_scale).astype(bf16)
    kv = qkv[:, GROUP_WIDTH:].astype(bf16)[None]
    for b in part_bits:
        bit = (me // b) % 2
        theirs = sflip(kv, b)
        kv = jnp.where(bit == 0, jnp.concatenate([kv, theirs]), jnp.concatenate([theirs, kv]))
    kv = kv.reshape(-1, 2 * GROUP_WIDTH)

    part = jnp.arange(n_parts, dtype=jnp.int32)
    part_device = part % 2 + 4 * (part // 2)
    member = jnp.arange(8, dtype=jnp.int32)
    member_device = (member // 4) * HI + ((member // 2) % 2) * ZO + (member % 2) * YO
    device = part_device[:, None] + member_device[None, :]
    position = (device[:, :, None] * rows + jnp.arange(rows, dtype=jnp.int32)).reshape(-1)
    bias = jnp.where(position < pick(valid_len, z1), 0.0, masked_score)[:, None]
    lane = jnp.arange(128, dtype=jnp.int32)[None, :]
    key_tail = jnp.where(lane == HEAD, bias, jnp.where((lane > HEAD) & (lane < HEAD + 4), 1.0, 0.0)).astype(bf16)

    context, context_full, stats = attend_forward(queries, kv, key_tail)

    teams = [
        [a * HI + b * ZO + c * YO + q for a in range(2) for b in range(2) for c in range(2)]
        for q in [i % 2 + 4 * (i // 2) for i in range(n_parts)]
    ]

    def exchange(blocks):
        return lax.all_to_all(blocks, "seq", 0, 0, axis_index_groups=teams, tiled=True)

    context = exchange(context.reshape(8, rows, GROUP_WIDTH))
    context = context.reshape(2, HEAD_GROUPS, rows, GROUP_WIDTH).transpose(0, 2, 1, 3).reshape(2 * rows, width)

    inner_lo = gathered[:, : 2 * shard].reshape(width, width)
    inner_hi = gathered[:, 2 * shard : 4 * shard].reshape(width, width)
    outer_end = 4 * shard + outer_weight.shape[0]
    outer_all = gathered[:, 4 * shard : outer_end].reshape(-1, 2, grp_size // 2, outer_weight.shape[0], width)
    outer_all = outer_all.transpose(0, 2, 1, 3, 4).reshape(half_feed, width)
    output_all = gathered[:, outer_end:].reshape(width, width)
    outer_lo, outer_hi = outer_all[:width], outer_all[width:]
    in_bias = pick(in_bias.reshape(chips, 2, piece).transpose(1, 0, 2).reshape(2, half_feed), core)

    home = tokens.reshape(2 * rows, width)
    cotangent = grad_out.reshape(2 * rows, width)
    hidden_one = home.astype(jnp.float32) + dot(context, output_all) + o_bias
    norm_one, norm_back_one = jax.vjp(layer_norm, hidden_one, gain1, shift1)
    first_out = norm_one.astype(bf16)
    n_own = 2 * rows
    both_first = jnp.concatenate([first_out, sflip(first_out, 1)], axis=0)

    def gelu_pair(pre):
        full, back = jax.vjp(partial(jax.nn.gelu, approximate=False), pre)
        return full.astype(bf16), back(jnp.ones_like(pre))[0]

    inner_all = jnp.concatenate([inner_lo, inner_hi], axis=1)
    active, slope = gelu_pair(dot(both_first, inner_all) + in_bias)
    outer_part = dot(active, outer_all)
    outer_sum = outer_part[:n_own] + sflip(outer_part[n_own:].astype(bf16), 1).astype(jnp.float32)
    hidden_two = first_out.astype(jnp.float32) + outer_sum + out_bias
    layer_out, norm_back_two = jax.vjp(layer_norm, hidden_two, gain2, shift2)
    dhidden_two, dsecond_gain, dsecond_shift = norm_back_two(cotangent.astype(jnp.float32))
    douter = dhidden_two.astype(bf16)
    both_douter = jnp.concatenate([douter, sflip(douter, 1)], axis=0)
    dinner = (dot_t(both_douter, outer_all) * slope).astype(bf16)
    dfirst_part = dot_t(dinner, inner_all)
    dfirst = dhidden_two + dfirst_part[:n_own] + sflip(dfirst_part[n_own:].astype(bf16), 1).astype(jnp.float32)
    dhidden_one, dfirst_gain, dfirst_shift = norm_back_one(dfirst)
    dattend = dhidden_one.astype(bf16)
    dcontext = dot_t(dattend, output_all).astype(bf16)
    dcontext = dcontext.reshape(2, rows, HEAD_GROUPS, GROUP_WIDTH).transpose(0, 2, 1, 3)
    dcontext = exchange(dcontext.reshape(8, rows, GROUP_WIDTH)).reshape(8 * rows, GROUP_WIDTH)

    out_rows = width // seq_size
    ctx_split = context.reshape(n_own, chips, 2, out_rows)
    ctx_split = [ctx_split[:, :, i].reshape(n_own, width // 2) for i in range(2)]
    both_ctx = jnp.concatenate([pick(ctx_split, core), sflip(pick(ctx_split, 1 - core), 1)], axis=0)
    both_dattend = jnp.concatenate([dattend, sflip(dattend, 1)], axis=0)
    vectors = jnp.stack([dfirst_gain, dfirst_shift, dsecond_gain, dsecond_shift])
    grads = weight_grads(both_first, dinner, active, both_douter, both_ctx, both_dattend, vectors, chips)
    chip_groups = [[2 * q + i for q in range(chips)] for i in range(2)]
    grads = lax.psum_scatter(grads, "seq", scatter_dimension=0, tiled=False, axis_index_groups=chip_groups)
    for b in range(log2_of(grp_size)):
        grads = (grads.astype(jnp.float32) + flip(grads, "grp", grp_size, 1 << b).astype(jnp.float32)).astype(bf16)
    r1 = 4 * out_rows
    r2 = r1 + piece
    r3 = r2 + out_rows
    inner_grad = grads[:r1].reshape(2, 2, out_rows, width)
    inner_grad = [inner_grad[:, i] for i in range(2)]
    far = sflip(jnp.concatenate([pick(inner_grad, 1 - core).reshape(2 * out_rows, width), grads[r3:]], axis=0), 1)
    dinner_weight = in_order(pick(inner_grad, core), far[: 2 * out_rows].reshape(2, out_rows, width), core)
    dinner_weight = dinner_weight.transpose(2, 0, 1, 3).reshape(out_rows, 2, chips, piece).transpose(0, 2, 1, 3)
    dinner_weight = dinner_weight.reshape(out_rows, feed).astype(jnp.float32)
    douter_weight = grads[r1:r2].astype(jnp.float32)
    doutput_weight = grads[r2:r3].astype(jnp.float32)
    small = grads[r3:].astype(jnp.float32)
    both = lax.dynamic_slice_in_dim(small + far[2 * out_rows :].astype(jnp.float32), me * out_rows, out_rows, axis=1)
    dfirst_gain, dfirst_shift, dsecond_gain, dsecond_shift, doutput_bias, douter_bias = (both[i] for i in range(6))
    dinner_bias = lax.dynamic_slice_in_dim(small[6:8].reshape(half_feed), (me // 2) * piece, piece)

    dqueries, dkv = attend_backward(queries, kv, key_tail, context_full, stats, dcontext)
    dkv = dkv.reshape(n_parts, 8 * rows, 2 * GROUP_WIDTH)
    for b in reversed(part_bits):
        bit = (me // b) % 2
        n_now = dkv.shape[0] // 2
        low, high = dkv[:n_now], dkv[n_now:]
        sent = jnp.where(bit == 0, high, low).astype(bf16)
        dkv = jnp.where(bit == 0, low, high) + sflip(sent, b).astype(jnp.float32)
    dqkv = jnp.concatenate([dqueries, dkv[0].astype(bf16)], axis=1)

    dx = dot_t(dqkv, w_all).reshape(2, 2, 2, rows, width)
    da, db = dx[..., :half_width], dx[..., half_width:]

    def halve(low, high, bit, mask):
        sent = jnp.where(bit == 0, high, low).astype(bf16)
        return jnp.where(bit == 0, low, high) + sflip(sent, mask).astype(jnp.float32)

    da = halve(da[:, :, 0], da[:, :, 1], y0, YO)
    db = halve(db[:, 0], db[:, 1], z0, ZO)
    da = halve(da[:, 0], da[:, 1], z0, ZO)
    db = halve(db[:, 0], db[:, 1], y0, YO)
    dx = jnp.concatenate([da, db], axis=-1)
    mine = pick(dx, z1)
    theirs = sflip(pick(dx, 1 - z1).astype(bf16), HI).astype(jnp.float32)
    dtokens = dhidden_one.reshape(2, rows, width) + in_order(mine, theirs, z1)

    dw = t_dot(x_all, dqkv)
    dbias = column_sums(dqkv)
    dw = dw.reshape(seq_size, out_rows, 3 * GROUP_WIDTH)
    dw = jnp.concatenate([dw, jnp.broadcast_to(dbias, (seq_size, 8, 3 * GROUP_WIDTH))], axis=1)
    block = dw.shape[1]
    n_extra = 1 << len(extra_bits)
    dw = dw.reshape(2, 2, 2, n_extra, 2, 1, block, 3 * GROUP_WIDTH)[:, :, :, :, :, 0]
    dw = dw.reshape(2, 2, n_extra, 2, 2, block, 3 * GROUP_WIDTH)
    dw = halve(dw[:, :, :, :, 0], dw[:, :, :, :, 1], me % 2, 1)
    for b in reversed(extra_bits):
        m = dw.shape[2] // 2
        dw = halve(dw[:, :, :m], dw[:, :, m:], (me // b) % 2, b)
    dw = dw[:, :, 0]
    dw = halve(dw[0], dw[1], z1, HI)
    for b in range(log2_of(grp_size)):
        dw = dw + flip(dw.astype(bf16), "grp", grp_size, 1 << b).astype(jnp.float32)
    dw = dw.astype(bf16).reshape(HEAD_GROUPS, block, 3 * GROUP_WIDTH)

    def row_block(k):
        return lax.dynamic_index_in_dim(dw, head_group ^ k, 0, keepdims=False)

    w0 = row_block(0)
    w1 = sflip(row_block(1), YO)
    w2 = sflip(row_block(2), ZO)
    w3 = sflip(row_block(3), ZO | YO)
    dw = in_order(in_order(w0, w1, y0), in_order(w2, w3, y0), z0).reshape(HEAD_GROUPS, block, 3, GROUP_WIDTH)
    dw = dw.astype(jnp.float32).transpose(2, 1, 0, 3).reshape(3, block, width)
    dquery_weight, dkey_weight, dvalue_weight = dw[0, :out_rows], dw[1, :out_rows], dw[2, :out_rows]
    dquery_bias = lax.dynamic_slice_in_dim(dw[0, out_rows], me * out_rows, out_rows)
    dvalue_bias = lax.dynamic_slice_in_dim(dw[2, out_rows], me * out_rows, out_rows)

    return (
        layer_out.astype(bf16).reshape(2, rows, width),
        dtokens.astype(bf16),
        dquery_weight,
        dquery_bias,
        dkey_weight,
        dvalue_weight,
        dvalue_bias,
        doutput_weight,
        doutput_bias,
        dfirst_gain,
        dfirst_shift,
        dinner_weight,
        dinner_bias,
        douter_weight,
        douter_bias,
        dsecond_gain,
        dsecond_shift,
    )


def solution(mesh):
    in_specs = (
        P("grp", "seq", None),
        P("grp"),
        P(("grp", "seq"), None),
        P(("grp", "seq")),
        P(("grp", "seq"), None),
        P(("grp", "seq"), None),
        P(("grp", "seq")),
        P(("grp", "seq"), None),
        P(("grp", "seq")),
        P(("grp", "seq")),
        P(("grp", "seq")),
        P(("grp", "seq"), None),
        P(("grp", "seq")),
        P(("grp", "seq"), None),
        P(("grp", "seq")),
        P(("grp", "seq")),
        P(("grp", "seq")),
        P("grp", "seq", None),
    )
    out_specs = (
        P("grp", "seq", None),
        P("grp", "seq", None),
        P("seq", None),
        P("seq"),
        P("seq", None),
        P("seq", None),
        P("seq"),
        P("seq", None),
        P("seq"),
        P("seq"),
        P("seq"),
        P("seq", None),
        P("seq"),
        P("seq", None),
        P("seq"),
        P("seq"),
        P("seq"),
    )
    body = partial(per_device, mesh.shape["seq"], mesh.shape["grp"])
    return jax.shard_map(
        body, mesh=mesh, in_specs=in_specs, out_specs=out_specs, check_vma=False
    )
```

```python
from functools import partial

import jax
import jax.numpy as jnp
from jax import lax
from jax.experimental import pallas as pl
from jax.experimental.pallas import tpu as pltpu
from jax.sharding import PartitionSpec as P

HEADS = 12
HEAD = 64
HEAD_GROUPS = 4
GROUP_WIDTH = HEADS * HEAD // HEAD_GROUPS
NH = HEADS // HEAD_GROUPS
BF16 = jnp.bfloat16
F32 = jnp.float32

score_scale = 0.125
epsilon = 1e-12
masked_score = -1e30


def log2_of(size):
    return size.bit_length() - 1


def flip(value, axis, size, mask):
    return lax.ppermute(value, axis, [(i, i ^ mask) for i in range(size)])


def in_order(mine, theirs, bit):
    return jnp.where(bit == 0, jnp.stack([mine, theirs]), jnp.stack([theirs, mine]))


def pick(pair, bit):
    return jnp.where(bit == 0, pair[0], pair[1])


def layer_norm(hidden, norm_gain, norm_shift):
    centred = hidden - jnp.mean(hidden, axis=-1, keepdims=True)
    spread = jnp.mean(centred * centred, axis=-1, keepdims=True)
    return centred * lax.rsqrt(spread + epsilon) * norm_gain + norm_shift


def dot(left, right):
    return jnp.dot(left, right, preferred_element_type=jnp.float32)


def dot_t(left, right):
    return lax.dot_general(left, right, (((1,), (1,)), ((), ())), preferred_element_type=jnp.float32)


def t_dot(left, right):
    return lax.dot_general(left, right, (((0,), (0,)), ((), ())), preferred_element_type=jnp.float32)


def column_sums(matrix):
    return jnp.sum(matrix.astype(jnp.float32), axis=0)


def thirds(x):
    hi=x.astype(BF16)
    r=x-hi.astype(F32)
    mid=r.astype(BF16)
    lo=(r-mid.astype(F32)).astype(BF16)
    return hi,mid,lo

def fwd_body(q_ref, kv_ref, kb_ref, c_ref, cf_ref, st_ref, kt, va, oacc, lacc, *, bq):
    i=pl.program_id(0); h=pl.program_id(1)
    W=NH*HEAD
    @pl.when((i==0)&(h==0))
    def _():
        tail=kb_ref[:,HEAD:]
        for g in range(NH):
            ka=jnp.concatenate([kv_ref[:,g*HEAD:(g+1)*HEAD],tail],axis=1)
            kt[g]=ka.T
            va[g]=jnp.concatenate([kv_ref[:,W+g*HEAD:W+(g+1)*HEAD],tail],axis=1)
    one=jnp.where(lax.broadcasted_iota(jnp.int32,(bq,HEAD),1)==0,1.0,0.0).astype(BF16)
    def head(g):
        qa=jnp.concatenate([q_ref[:,g*HEAD:(g+1)*HEAD],one],axis=1)
        s=dot(qa,kt[g])
        m=jnp.max(s,axis=1,keepdims=True)
        p=jnp.exp(s-m).astype(BF16)
        o=dot(p,va[g])
        l=o[:,HEAD+1:HEAD+2]
        oacc[g]=o/l
        lacc[g]=jnp.broadcast_to(m+jnp.log(l),(bq,128))
    for g in range(NH):
        @pl.when(h==g)
        def _(): head(g)
    @pl.when(h==NH-1)
    def _():
        c=jnp.concatenate([oacc[g][:,:HEAD] for g in range(NH)],axis=1)
        c_ref[...]=c.astype(BF16)
        cf_ref[...]=c
        lane=lax.broadcasted_iota(jnp.int32,(bq,128),1)
        st=lacc[0]
        for g in range(1,NH): st=jnp.where(lane==g,lacc[g],st)
        st_ref[...]=st

def attend_forward(q,kv,kb,bq=256):
    n,W=q.shape; L=kv.shape[0]
    return pl.pallas_call(partial(fwd_body,bq=bq),
        grid=(n//bq,NH),
        in_specs=[pl.BlockSpec((bq,W),lambda i,h:(i,0)),pl.BlockSpec((L,2*W),lambda i,h:(0,0)),pl.BlockSpec((L,128),lambda i,h:(0,0))],
        out_specs=[pl.BlockSpec((bq,W),lambda i,h:(i,0)),pl.BlockSpec((bq,W),lambda i,h:(i,0)),pl.BlockSpec((bq,128),lambda i,h:(i,0))],
        out_shape=[jax.ShapeDtypeStruct((n,W),BF16),jax.ShapeDtypeStruct((n,W),F32),jax.ShapeDtypeStruct((n,128),F32)],
        scratch_shapes=[pltpu.VMEM((NH,128,L),BF16),pltpu.VMEM((NH,L,128),BF16),pltpu.VMEM((NH,bq,128),F32),pltpu.VMEM((NH,bq,128),F32)],
        cost_estimate=pl.CostEstimate(flops=16*n*L*W, transcendentals=NH*n*L, bytes_accessed=4*n*L),
        name="attend_forward",
    )(q,kv,kb)

def bwd_body(q_ref, kv_ref, kb_ref, cf_ref, st_ref, dc_ref, dq_ref, dkv_ref, qt, qn, dct, dcn, dqt, dk, dv, *, bk, nk):
    j=pl.program_id(0); h=pl.program_id(1)
    W=NH*HEAD
    n=q_ref.shape[0]
    @pl.when((j==0)&(h==0))
    def _():
        lane=lax.broadcasted_iota(jnp.int32,(n,HEAD),1)
        def tail(x,first):
            hi,mid,lo=thirds(-x)
            z=jnp.where(lane==1,hi.astype(F32),jnp.where(lane==2,mid.astype(F32),jnp.where(lane==3,lo.astype(F32),0.0)))
            return jnp.where(lane==0,first,z).astype(BF16)
        for g in range(NH):
            cols=slice(g*HEAD,(g+1)*HEAD)
            qa=jnp.concatenate([q_ref[:,cols],tail(st_ref[:,g:g+1],1.0)],axis=1)
            qn[g]=qa
            qt[g]=qa.T
            d=dc_ref[:,cols]
            delta=jnp.sum(d.astype(F32)*cf_ref[:,cols],axis=1,keepdims=True)
            da=jnp.concatenate([d,tail(delta,0.0)],axis=1)
            dcn[g]=da
            dct[g]=da.T
        dqt[...]=jnp.zeros_like(dqt)
    tail=kb_ref[:,HEAD:]
    def head(g):
        k=kv_ref[:,g*HEAD:(g+1)*HEAD]
        ka=jnp.concatenate([k,tail],axis=1)
        va=jnp.concatenate([kv_ref[:,W+g*HEAD:W+(g+1)*HEAD],tail],axis=1)
        p=jnp.exp(dot(ka,qt[g]))
        dp=dot(va,dct[g])
        ds=(p*dp).astype(BF16)
        dv[g]=dot(p.astype(BF16),dcn[g])
        dk[g]=dot(ds,qn[g])
        dqt[g]=dqt[g]+t_dot(ka,ds)[:HEAD]
    for g in range(NH):
        @pl.when(h==g)
        def _(): head(g)
    @pl.when(h==NH-1)
    def _():
        dkv_ref[...]=jnp.concatenate([dk[g][:,:HEAD] for g in range(NH)]+[dv[g][:,:HEAD] for g in range(NH)],axis=1)
    @pl.when((h==NH-1)&(j==nk-1))
    def _():
        for g in range(NH):
            dq_ref[:,g*HEAD:(g+1)*HEAD]=(dqt[g].T*0.125).astype(BF16)

def attend_backward(q,kv,kb,cf,st,dc,bk=512):
    n,W=q.shape; L=kv.shape[0]; nk=L//bk
    full=lambda a: pl.BlockSpec(a.shape,lambda j,h:(0,0))
    return pl.pallas_call(partial(bwd_body,bk=bk,nk=nk),
        grid=(nk,NH),
        in_specs=[full(q),pl.BlockSpec((bk,2*W),lambda j,h:(j,0)),pl.BlockSpec((bk,128),lambda j,h:(j,0)),full(cf),full(st),full(dc)],
        out_specs=[pl.BlockSpec((n,W),lambda j,h:(0,0)),pl.BlockSpec((bk,2*W),lambda j,h:(j,0))],
        out_shape=[jax.ShapeDtypeStruct((n,W),BF16),jax.ShapeDtypeStruct((L,2*W),F32)],
        scratch_shapes=[pltpu.VMEM((NH,128,n),BF16),pltpu.VMEM((NH,n,128),BF16),pltpu.VMEM((NH,128,n),BF16),pltpu.VMEM((NH,n,128),BF16),
            pltpu.VMEM((NH,HEAD,n),F32),pltpu.VMEM((NH,bk,128),F32),pltpu.VMEM((NH,bk,128),F32)],
        cost_estimate=pl.CostEstimate(flops=32*n*L*W, transcendentals=NH*n*L, bytes_accessed=4*n*L),
        name="attend_backward",
    )(q,kv,kb,cf,st,dc)


def weight_grads_body(y_ref, dz_ref, a_ref, do_ref, ctx_ref, da_ref, vec_ref, out_ref, *, chips):
    width = y_ref.shape[1]
    r_in, r_ctx = width // chips, ctx_ref.shape[1] // chips
    r_out = a_ref.shape[1] // chips
    for j in range(2):
        grad = t_dot(y_ref[...], dz_ref[:, j * width : (j + 1) * width]).astype(BF16)
        for q in range(chips):
            out_ref[q, j * r_in : (j + 1) * r_in] = grad[q * r_in : (q + 1) * r_in]
        grad = t_dot(a_ref[:, j * width : (j + 1) * width], do_ref[...]).astype(BF16)
        half = chips // 2
        for q in range(half):
            out_ref[j * half + q, 2 * r_in : 2 * r_in + r_out] = grad[q * r_out : (q + 1) * r_out]
    first = 2 * r_in + r_out
    grad = t_dot(ctx_ref[...], da_ref[...]).astype(BF16)
    for q in range(chips):
        out_ref[q, first : first + r_ctx] = grad[q * r_ctx : (q + 1) * r_ctx]
    own = vec_ref.shape[0]
    n = da_ref.shape[0] // 2
    ones = jnp.ones((16, y_ref.shape[0]), BF16)
    sums = [dot(ones[:, :n], da_ref[:n])[:1], dot(ones[:, :n], do_ref[:n])[:1]]
    sums += [dot(ones, dz_ref[:, j * width : (j + 1) * width])[:1] for j in range(2)]
    small = jnp.concatenate([vec_ref[...]] + sums, axis=0).astype(BF16)
    for q in range(chips):
        out_ref[q, first + r_ctx : first + r_ctx + own + 4] = small
        out_ref[q, first + r_ctx + own + 4 :] = jnp.zeros((out_ref.shape[1] - first - r_ctx - own - 4, width), BF16)


def weight_grads(y, dz, a, do, ctx, da, vec, chips, parts):
    width = y.shape[1]
    total = 2 * width // chips + a.shape[1] // chips + ctx.shape[1] // chips + vec.shape[0] + 4
    total = -(-total // (16 * parts)) * 16 * parts
    return pl.pallas_call(
        partial(weight_grads_body, chips=chips),
        out_shape=jax.ShapeDtypeStruct((chips, total, width), BF16),
        cost_estimate=pl.CostEstimate(
            flops=2 * width * (y.shape[0] * (2 * dz.shape[1] + ctx.shape[1])), transcendentals=0, bytes_accessed=15 * width * width * 2
        ),
        name="weight_grads",
    )(y, dz, a, do, ctx, da, vec)


def per_device(
    seq_size,
    grp_size,
    tokens,
    valid_len,
    query_weight,
    query_bias,
    key_weight,
    value_weight,
    value_bias,
    output_weight,
    output_bias,
    first_gain,
    first_shift,
    inner_weight,
    inner_bias,
    outer_weight,
    outer_bias,
    second_gain,
    second_shift,
    grad_out,
):
    bf16 = jnp.bfloat16
    rows, width = tokens.shape[1:]
    feed = inner_weight.shape[1]
    shard = query_weight.shape[0]
    HI, ZO, YO = seq_size // 2, seq_size // 4, 2
    extra_bits = [1 << b for b in range(2, log2_of(ZO))]
    part_bits = [1] + extra_bits
    me = lax.axis_index("seq")
    grp = lax.axis_index("grp")
    z1 = me // HI
    z0 = (me // ZO) % 2
    y0 = (me // YO) % 2
    head_group = 2 * z0 + y0
    my_part = me % 2 + 2 * ((me // 4) % max(ZO // 4, 1))
    n_parts = seq_size // 8

    def sflip(value, mask):
        return flip(value, "seq", seq_size, mask)

    core = me % 2
    chips = seq_size // 2
    piece = feed // seq_size
    n_dev = grp_size * seq_size
    half_feed = feed // 2
    split = inner_weight.reshape(shard, chips, 2, piece)
    split = [split[:, :, i].reshape(shard, 2, width).transpose(1, 0, 2).reshape(2 * shard, width) for i in range(2)]
    near = jnp.concatenate([pick(split, 1 - core), output_weight], axis=0)
    far = sflip(near, 1)
    outer_far = lax.ppermute(
        outer_weight,
        ("grp", "seq"),
        [(d, d ^ (1 | grp_size) if d % 2 != (d // grp_size) % 2 else d) for d in range(n_dev)],
    )
    inner_pair = in_order(pick(split, core).reshape(2, shard, width), far[: 2 * shard].reshape(2, shard, width), core)
    packed = jnp.concatenate(
        [
            inner_pair.transpose(1, 0, 2, 3).reshape(4 * shard, width),
            outer_far,
            in_order(output_weight, far[2 * shard :], core).reshape(2 * shard, width),
        ],
        axis=0,
    )
    chip_groups = [[2 * q + i for q in range(chips)] for i in range(2)]
    gathered = lax.all_gather(packed, "seq", axis=0, tiled=False, axis_index_groups=chip_groups)
    for b in range(log2_of(grp_size)):
        theirs = flip(gathered, "grp", grp_size, 1 << b)
        gathered = in_order(gathered, theirs, (grp >> b) % 2).reshape((-1,) + packed.shape)

    x_mine = pick(tokens, z1)
    x_sent = pick(tokens, 1 - z1)
    half_width = width // 2
    x_pair = in_order(x_mine, sflip(x_sent, HI), z1)
    xa, xb = x_pair[:, :, :half_width], x_pair[:, :, half_width:]
    ra, rb = sflip(xa, YO), sflip(xb, ZO)
    xa, xb = in_order(xa, ra, y0), in_order(xb, rb, z0)
    ra, rb = sflip(xa, ZO), sflip(xb, YO)
    xa, xb = in_order(xa, ra, z0), in_order(xb, rb, y0)
    x_all = jnp.concatenate([xa.transpose(2, 0, 1, 3, 4), xb.transpose(2, 1, 0, 3, 4)], axis=-1)
    x_all = x_all.reshape(8 * rows, width)

    smalls = jnp.concatenate(
        [query_bias, value_bias, output_bias, first_gain, first_shift, outer_bias, second_gain, second_shift, inner_bias]
    )
    small_rows = 32 - shard if shard == 24 else 8
    grouped = jnp.stack([query_weight, key_weight, value_weight]).reshape(3, shard, HEAD_GROUPS, GROUP_WIDTH)
    grouped = grouped.transpose(2, 1, 0, 3).reshape(HEAD_GROUPS, shard, 3 * GROUP_WIDTH)
    small_block = jnp.zeros((small_rows * 3 * GROUP_WIDTH,), bf16).at[: smalls.shape[0]].set(smalls)
    small_block = jnp.broadcast_to(small_block.reshape(1, small_rows, -1), (HEAD_GROUPS, small_rows, 3 * GROUP_WIDTH))
    grouped = jnp.concatenate([grouped, small_block], axis=1)

    def group_block(k):
        return lax.dynamic_index_in_dim(grouped, head_group ^ k, 0, keepdims=False)

    w0 = group_block(0)
    w1 = sflip(group_block(1), YO)
    w2 = sflip(group_block(2), ZO)
    w3 = sflip(group_block(3), ZO | YO)
    w_all = in_order(in_order(w0, w1, y0), in_order(w2, w3, y0), z0)
    w_all = in_order(w_all, sflip(w_all, HI), z1)
    names = ["z1", "z0", "y0"]
    for b in extra_bits:
        w_all = in_order(w_all, sflip(w_all, b), (me // b) % 2)
        names = ["e%d" % b] + names
    for b in range(log2_of(grp_size)):
        w_all = in_order(w_all, flip(w_all, "grp", grp_size, 1 << b), (grp >> b) % 2)
        names = ["g%d" % b] + names
    w_all = in_order(w_all, sflip(w_all, 1), me % 2)
    names = ["c"] + names
    wanted = ["g%d" % b for b in reversed(range(log2_of(grp_size)))] + ["z1", "z0"]
    wanted += ["e%d" % b for b in reversed(extra_bits)] + ["y0", "c"]
    n = len(names)
    w_all = w_all.transpose(*[names.index(w) for w in wanted], n, n + 1)
    w_all = w_all.reshape(grp_size * seq_size, shard + small_rows, 3 * GROUP_WIDTH)
    small_all = w_all[:, shard:].reshape(grp_size * seq_size, -1)[:, : smalls.shape[0]]
    vectors = [small_all[:, i * shard : (i + 1) * shard].reshape(-1).astype(jnp.float32) for i in range(8)]
    q_bias, v_bias, o_bias, gain1, shift1, out_bias, gain2, shift2 = vectors
    in_bias = small_all[:, 8 * shard :].reshape(-1).astype(jnp.float32)
    w_all = w_all[:, :shard].reshape(width, 3 * GROUP_WIDTH)

    def own_columns(vector):
        return lax.dynamic_slice_in_dim(vector, head_group * GROUP_WIDTH, GROUP_WIDTH)

    qkv_bias = jnp.concatenate([own_columns(q_bias), jnp.zeros((GROUP_WIDTH,), jnp.float32), own_columns(v_bias)])
    qkv = dot(x_all, w_all) + qkv_bias
    queries = (qkv[:, :GROUP_WIDTH] * score_scale).astype(bf16)
    kv = qkv[:, GROUP_WIDTH:].astype(bf16)[None]
    for b in part_bits:
        bit = (me // b) % 2
        theirs = sflip(kv, b)
        kv = jnp.where(bit == 0, jnp.concatenate([kv, theirs]), jnp.concatenate([theirs, kv]))
    kv = kv.reshape(-1, 2 * GROUP_WIDTH)

    part = jnp.arange(n_parts, dtype=jnp.int32)
    part_device = part % 2 + 4 * (part // 2)
    member = jnp.arange(8, dtype=jnp.int32)
    member_device = (member // 4) * HI + ((member // 2) % 2) * ZO + (member % 2) * YO
    device = part_device[:, None] + member_device[None, :]
    position = (device[:, :, None] * rows + jnp.arange(rows, dtype=jnp.int32)).reshape(-1)
    bias = jnp.where(position < pick(valid_len, z1), 0.0, masked_score)[:, None]
    lane = jnp.arange(128, dtype=jnp.int32)[None, :]
    key_tail = jnp.where(lane == HEAD, bias, jnp.where((lane > HEAD) & (lane < HEAD + 4), 1.0, 0.0)).astype(bf16)

    context, context_full, stats = attend_forward(queries, kv, key_tail)

    teams = [
        [a * HI + b * ZO + c * YO + q for a in range(2) for b in range(2) for c in range(2)]
        for q in [i % 2 + 4 * (i // 2) for i in range(n_parts)]
    ]

    def exchange(blocks):
        return lax.all_to_all(blocks, "seq", 0, 0, axis_index_groups=teams, tiled=True)

    context = exchange(context.reshape(8, rows, GROUP_WIDTH))
    context = context.reshape(2, HEAD_GROUPS, rows, GROUP_WIDTH).transpose(0, 2, 1, 3).reshape(2 * rows, width)

    inner_lo = gathered[:, : 2 * shard].reshape(width, width)
    inner_hi = gathered[:, 2 * shard : 4 * shard].reshape(width, width)
    outer_end = 4 * shard + outer_weight.shape[0]
    outer_all = gathered[:, 4 * shard : outer_end].reshape(-1, 2, grp_size // 2, outer_weight.shape[0], width)
    outer_all = outer_all.transpose(0, 2, 1, 3, 4).reshape(half_feed, width)
    output_all = gathered[:, outer_end:].reshape(width, width)
    outer_lo, outer_hi = outer_all[:width], outer_all[width:]
    in_bias = pick(in_bias.reshape(chips, 2, piece).transpose(1, 0, 2).reshape(2, half_feed), core)

    home = tokens.reshape(2 * rows, width)
    cotangent = grad_out.reshape(2 * rows, width)
    hidden_one = home.astype(jnp.float32) + dot(context, output_all) + o_bias
    norm_one, norm_back_one = jax.vjp(layer_norm, hidden_one, gain1, shift1)
    first_out = norm_one.astype(bf16)
    n_own = 2 * rows
    both_first = jnp.concatenate([first_out, sflip(first_out, 1)], axis=0)

    def gelu_pair(pre):
        full, back = jax.vjp(partial(jax.nn.gelu, approximate=False), pre)
        return full.astype(bf16), back(jnp.ones_like(pre))[0]

    inner_all = jnp.concatenate([inner_lo, inner_hi], axis=1)
    active, slope = gelu_pair(dot(both_first, inner_all) + in_bias)
    outer_part = dot(active, outer_all)
    outer_sum = outer_part[:n_own] + sflip(outer_part[n_own:].astype(bf16), 1).astype(jnp.float32)
    hidden_two = first_out.astype(jnp.float32) + outer_sum + out_bias
    layer_out, norm_back_two = jax.vjp(layer_norm, hidden_two, gain2, shift2)
    dhidden_two, dsecond_gain, dsecond_shift = norm_back_two(cotangent.astype(jnp.float32))
    douter = dhidden_two.astype(bf16)
    both_douter = jnp.concatenate([douter, sflip(douter, 1)], axis=0)
    dinner = (dot_t(both_douter, outer_all) * slope).astype(bf16)
    dfirst_part = dot_t(dinner, inner_all)
    dfirst = dhidden_two + dfirst_part[:n_own] + sflip(dfirst_part[n_own:].astype(bf16), 1).astype(jnp.float32)
    dhidden_one, dfirst_gain, dfirst_shift = norm_back_one(dfirst)
    dattend = dhidden_one.astype(bf16)
    dcontext = dot_t(dattend, output_all).astype(bf16)
    dcontext = dcontext.reshape(2, rows, HEAD_GROUPS, GROUP_WIDTH).transpose(0, 2, 1, 3)
    dcontext = exchange(dcontext.reshape(8, rows, GROUP_WIDTH)).reshape(8 * rows, GROUP_WIDTH)

    out_rows = width // seq_size
    ctx_split = context.reshape(n_own, chips, 2, out_rows)
    ctx_split = [ctx_split[:, :, i].reshape(n_own, width // 2) for i in range(2)]
    both_ctx = jnp.concatenate([pick(ctx_split, core), sflip(pick(ctx_split, 1 - core), 1)], axis=0)
    both_dattend = jnp.concatenate([dattend, sflip(dattend, 1)], axis=0)
    vectors = jnp.stack([dfirst_gain, dfirst_shift, dsecond_gain, dsecond_shift])
    grads = weight_grads(both_first, dinner, active, both_douter, both_ctx, both_dattend, vectors, chips, grp_size)
    grads = grads.reshape(chips, grp_size, -1, width)
    for b in reversed(range(log2_of(grp_size))):
        bit = (grp >> b) % 2
        n_half = grads.shape[1] // 2
        kept, sent = (lax.dynamic_slice_in_dim(grads, n_half * i, n_half, axis=1) for i in (bit, 1 - bit))
        grads = (kept.astype(jnp.float32) + flip(sent, "grp", grp_size, 1 << b).astype(jnp.float32)).astype(bf16)
    grads = lax.psum_scatter(grads[:, 0], "seq", scatter_dimension=0, tiled=False, axis_index_groups=chip_groups)
    for b in range(log2_of(grp_size)):
        grads = in_order(grads, flip(grads, "grp", grp_size, 1 << b), (grp >> b) % 2).reshape(-1, width)
    r1 = 4 * out_rows
    r2 = r1 + piece
    r3 = r2 + out_rows
    inner_grad = grads[:r1].reshape(2, 2, out_rows, width)
    inner_grad = [inner_grad[:, i] for i in range(2)]
    far = sflip(jnp.concatenate([pick(inner_grad, 1 - core).reshape(2 * out_rows, width), grads[r3 : r3 + 8]], axis=0), 1)
    dinner_weight = in_order(pick(inner_grad, core), far[: 2 * out_rows].reshape(2, out_rows, width), core)
    dinner_weight = dinner_weight.transpose(2, 0, 1, 3).reshape(out_rows, 2, chips, piece).transpose(0, 2, 1, 3)
    dinner_weight = dinner_weight.reshape(out_rows, feed).astype(jnp.float32)
    douter_weight = grads[r1:r2].astype(jnp.float32)
    doutput_weight = grads[r2:r3].astype(jnp.float32)
    small = grads[r3 : r3 + 8].astype(jnp.float32)
    both = lax.dynamic_slice_in_dim(small + far[2 * out_rows :].astype(jnp.float32), me * out_rows, out_rows, axis=1)
    dfirst_gain, dfirst_shift, dsecond_gain, dsecond_shift, doutput_bias, douter_bias = (both[i] for i in range(6))
    dinner_bias = lax.dynamic_slice_in_dim(small[6:8].reshape(half_feed), (me // 2) * piece, piece)

    dqueries, dkv = attend_backward(queries, kv, key_tail, context_full, stats, dcontext)
    dkv = dkv.reshape(n_parts, 8 * rows, 2 * GROUP_WIDTH)
    for b in reversed(part_bits):
        bit = (me // b) % 2
        n_now = dkv.shape[0] // 2
        low, high = dkv[:n_now], dkv[n_now:]
        sent = jnp.where(bit == 0, high, low).astype(bf16)
        dkv = jnp.where(bit == 0, low, high) + sflip(sent, b).astype(jnp.float32)
    dqkv = jnp.concatenate([dqueries, dkv[0].astype(bf16)], axis=1)

    dx = dot_t(dqkv, w_all).reshape(2, 2, 2, rows, width)
    da, db = dx[..., :half_width], dx[..., half_width:]

    def halve(low, high, bit, mask):
        sent = jnp.where(bit == 0, high, low).astype(bf16)
        return jnp.where(bit == 0, low, high) + sflip(sent, mask).astype(jnp.float32)

    da = halve(da[:, :, 0], da[:, :, 1], y0, YO)
    db = halve(db[:, 0], db[:, 1], z0, ZO)
    da = halve(da[:, 0], da[:, 1], z0, ZO)
    db = halve(db[:, 0], db[:, 1], y0, YO)
    dx = jnp.concatenate([da, db], axis=-1)
    mine = pick(dx, z1)
    theirs = sflip(pick(dx, 1 - z1).astype(bf16), HI).astype(jnp.float32)
    dtokens = dhidden_one.reshape(2, rows, width) + in_order(mine, theirs, z1)

    dw = t_dot(x_all, dqkv)
    dbias = column_sums(dqkv)
    dw = dw.reshape(seq_size, out_rows, 3 * GROUP_WIDTH)
    dw = jnp.concatenate([dw, jnp.broadcast_to(dbias, (seq_size, 8, 3 * GROUP_WIDTH))], axis=1)
    block = dw.shape[1]
    n_extra = 1 << len(extra_bits)
    dw = dw.reshape(2, 2, 2, n_extra, 2, 1, block, 3 * GROUP_WIDTH)[:, :, :, :, :, 0]
    dw = dw.reshape(2, 2, n_extra, 2, 2, block, 3 * GROUP_WIDTH)
    dw = halve(dw[:, :, :, :, 0], dw[:, :, :, :, 1], me % 2, 1)
    for b in reversed(extra_bits):
        m = dw.shape[2] // 2
        dw = halve(dw[:, :, :m], dw[:, :, m:], (me // b) % 2, b)
    dw = dw[:, :, 0]
    dw = halve(dw[0], dw[1], z1, HI)
    for b in range(log2_of(grp_size)):
        dw = dw + flip(dw.astype(bf16), "grp", grp_size, 1 << b).astype(jnp.float32)
    dw = dw.astype(bf16).reshape(HEAD_GROUPS, block, 3 * GROUP_WIDTH)

    def row_block(k):
        return lax.dynamic_index_in_dim(dw, head_group ^ k, 0, keepdims=False)

    w0 = row_block(0)
    w1 = sflip(row_block(1), YO)
    w2 = sflip(row_block(2), ZO)
    w3 = sflip(row_block(3), ZO | YO)
    dw = in_order(in_order(w0, w1, y0), in_order(w2, w3, y0), z0).reshape(HEAD_GROUPS, block, 3, GROUP_WIDTH)
    dw = dw.astype(jnp.float32).transpose(2, 1, 0, 3).reshape(3, block, width)
    dquery_weight, dkey_weight, dvalue_weight = dw[0, :out_rows], dw[1, :out_rows], dw[2, :out_rows]
    dquery_bias = lax.dynamic_slice_in_dim(dw[0, out_rows], me * out_rows, out_rows)
    dvalue_bias = lax.dynamic_slice_in_dim(dw[2, out_rows], me * out_rows, out_rows)

    return (
        layer_out.astype(bf16).reshape(2, rows, width),
        dtokens.astype(bf16),
        dquery_weight,
        dquery_bias,
        dkey_weight,
        dvalue_weight,
        dvalue_bias,
        doutput_weight,
        doutput_bias,
        dfirst_gain,
        dfirst_shift,
        dinner_weight,
        dinner_bias,
        douter_weight,
        douter_bias,
        dsecond_gain,
        dsecond_shift,
    )


def solution(mesh):
    in_specs = (
        P("grp", "seq", None),
        P("grp"),
        P(("grp", "seq"), None),
        P(("grp", "seq")),
        P(("grp", "seq"), None),
        P(("grp", "seq"), None),
        P(("grp", "seq")),
        P(("grp", "seq"), None),
        P(("grp", "seq")),
        P(("grp", "seq")),
        P(("grp", "seq")),
        P(("grp", "seq"), None),
        P(("grp", "seq")),
        P(("grp", "seq"), None),
        P(("grp", "seq")),
        P(("grp", "seq")),
        P(("grp", "seq")),
        P("grp", "seq", None),
    )
    out_specs = (
        P("grp", "seq", None),
        P("grp", "seq", None),
        P("seq", None),
        P("seq"),
        P("seq", None),
        P("seq", None),
        P("seq"),
        P("seq", None),
        P("seq"),
        P("seq"),
        P("seq"),
        P("seq", None),
        P("seq"),
        P("seq", None),
        P("seq"),
        P("seq"),
        P("seq"),
    )
    body = partial(per_device, mesh.shape["seq"], mesh.shape["grp"])
    return jax.shard_map(
        body, mesh=mesh, in_specs=in_specs, out_specs=out_specs, check_vma=False
    )
```

```python
from functools import partial

import jax
import jax.numpy as jnp
from jax import lax
from jax.experimental import pallas as pl
from jax.experimental.pallas import tpu as pltpu
from jax.sharding import PartitionSpec as P

HEADS = 12
HEAD = 64
HEAD_GROUPS = 4
GROUP_WIDTH = HEADS * HEAD // HEAD_GROUPS
NH = HEADS // HEAD_GROUPS
BF16 = jnp.bfloat16
F32 = jnp.float32

score_scale = 0.125
epsilon = 1e-12
masked_score = -1e30


def log2_of(size):
    return size.bit_length() - 1


def flip(value, axis, size, mask):
    return lax.ppermute(value, axis, [(i, i ^ mask) for i in range(size)])


def in_order(mine, theirs, bit):
    return jnp.where(bit == 0, jnp.stack([mine, theirs]), jnp.stack([theirs, mine]))


def pick(pair, bit):
    return jnp.where(bit == 0, pair[0], pair[1])


def layer_norm(hidden, norm_gain, norm_shift):
    centred = hidden - jnp.mean(hidden, axis=-1, keepdims=True)
    spread = jnp.mean(centred * centred, axis=-1, keepdims=True)
    return centred * lax.rsqrt(spread + epsilon) * norm_gain + norm_shift


def dot(left, right):
    return jnp.dot(left, right, preferred_element_type=jnp.float32)


def dot_t(left, right):
    return lax.dot_general(left, right, (((1,), (1,)), ((), ())), preferred_element_type=jnp.float32)


def t_dot(left, right):
    return lax.dot_general(left, right, (((0,), (0,)), ((), ())), preferred_element_type=jnp.float32)


def column_sums(matrix):
    return jnp.sum(matrix.astype(jnp.float32), axis=0)


def thirds(x):
    hi=x.astype(BF16)
    r=x-hi.astype(F32)
    mid=r.astype(BF16)
    lo=(r-mid.astype(F32)).astype(BF16)
    return hi,mid,lo

def fwd_body(q_ref, kv_ref, kb_ref, c_ref, cf_ref, st_ref, kt, va, oacc, lacc, *, bq):
    i=pl.program_id(0); h=pl.program_id(1)
    W=NH*HEAD
    @pl.when((i==0)&(h==0))
    def _():
        tail=kb_ref[:,HEAD:]
        for g in range(NH):
            ka=jnp.concatenate([kv_ref[:,g*HEAD:(g+1)*HEAD],tail],axis=1)
            kt[g]=ka.T
            va[g]=jnp.concatenate([kv_ref[:,W+g*HEAD:W+(g+1)*HEAD],tail],axis=1)
    one=jnp.where(lax.broadcasted_iota(jnp.int32,(bq,HEAD),1)==0,1.0,0.0).astype(BF16)
    def head(g):
        qa=jnp.concatenate([q_ref[:,g*HEAD:(g+1)*HEAD],one],axis=1)
        s=dot(qa,kt[g])
        m=jnp.max(s,axis=1,keepdims=True)
        p=jnp.exp(s-m).astype(BF16)
        o=dot(p,va[g])
        l=o[:,HEAD+1:HEAD+2]
        oacc[g]=o/l
        lacc[g]=jnp.broadcast_to(m+jnp.log(l),(bq,128))
    for g in range(NH):
        @pl.when(h==g)
        def _(): head(g)
    @pl.when(h==NH-1)
    def _():
        c=jnp.concatenate([oacc[g][:,:HEAD] for g in range(NH)],axis=1)
        c_ref[...]=c.astype(BF16)
        cf_ref[...]=c
        lane=lax.broadcasted_iota(jnp.int32,(bq,128),1)
        st=lacc[0]
        for g in range(1,NH): st=jnp.where(lane==g,lacc[g],st)
        st_ref[...]=st

def attend_forward(q,kv,kb,bq=256):
    n,W=q.shape; L=kv.shape[0]
    return pl.pallas_call(partial(fwd_body,bq=bq),
        grid=(n//bq,NH),
        in_specs=[pl.BlockSpec((bq,W),lambda i,h:(i,0)),pl.BlockSpec((L,2*W),lambda i,h:(0,0)),pl.BlockSpec((L,128),lambda i,h:(0,0))],
        out_specs=[pl.BlockSpec((bq,W),lambda i,h:(i,0)),pl.BlockSpec((bq,W),lambda i,h:(i,0)),pl.BlockSpec((bq,128),lambda i,h:(i,0))],
        out_shape=[jax.ShapeDtypeStruct((n,W),BF16),jax.ShapeDtypeStruct((n,W),F32),jax.ShapeDtypeStruct((n,128),F32)],
        scratch_shapes=[pltpu.VMEM((NH,128,L),BF16),pltpu.VMEM((NH,L,128),BF16),pltpu.VMEM((NH,bq,128),F32),pltpu.VMEM((NH,bq,128),F32)],
        cost_estimate=pl.CostEstimate(flops=16*n*L*W, transcendentals=NH*n*L, bytes_accessed=4*n*L),
        name="attend_forward",
    )(q,kv,kb)

def bwd_body(q_ref, kv_ref, kb_ref, cf_ref, st_ref, dc_ref, dq_ref, dkv_ref, qt, qn, dct, dcn, dqt, dk, dv, *, bk, nk):
    j=pl.program_id(0); h=pl.program_id(1)
    W=NH*HEAD
    n=q_ref.shape[0]
    @pl.when((j==0)&(h==0))
    def _():
        lane=lax.broadcasted_iota(jnp.int32,(n,HEAD),1)
        def tail(x,first):
            hi,mid,lo=thirds(-x)
            z=jnp.where(lane==1,hi.astype(F32),jnp.where(lane==2,mid.astype(F32),jnp.where(lane==3,lo.astype(F32),0.0)))
            return jnp.where(lane==0,first,z).astype(BF16)
        for g in range(NH):
            cols=slice(g*HEAD,(g+1)*HEAD)
            qa=jnp.concatenate([q_ref[:,cols],tail(st_ref[:,g:g+1],1.0)],axis=1)
            qn[g]=qa
            qt[g]=qa.T
            d=dc_ref[:,cols]
            delta=jnp.sum(d.astype(F32)*cf_ref[:,cols],axis=1,keepdims=True)
            da=jnp.concatenate([d,tail(delta,0.0)],axis=1)
            dcn[g]=da
            dct[g]=da.T
        dqt[...]=jnp.zeros_like(dqt)
    tail=kb_ref[:,HEAD:]
    def head(g):
        k=kv_ref[:,g*HEAD:(g+1)*HEAD]
        ka=jnp.concatenate([k,tail],axis=1)
        va=jnp.concatenate([kv_ref[:,W+g*HEAD:W+(g+1)*HEAD],tail],axis=1)
        p=jnp.exp(dot(ka,qt[g]))
        dp=dot(va,dct[g])
        ds=(p*dp).astype(BF16)
        dv[g]=dot(p.astype(BF16),dcn[g])
        dk[g]=dot(ds,qn[g])
        dqt[g]=dqt[g]+t_dot(ka,ds)[:HEAD]
    for g in range(NH):
        @pl.when(h==g)
        def _(): head(g)
    @pl.when(h==NH-1)
    def _():
        dkv_ref[...]=jnp.concatenate([dk[g][:,:HEAD] for g in range(NH)]+[dv[g][:,:HEAD] for g in range(NH)],axis=1)
    @pl.when((h==NH-1)&(j==nk-1))
    def _():
        for g in range(NH):
            dq_ref[:,g*HEAD:(g+1)*HEAD]=(dqt[g].T*0.125).astype(BF16)

def attend_backward(q,kv,kb,cf,st,dc,bk=512):
    n,W=q.shape; L=kv.shape[0]; nk=L//bk
    full=lambda a: pl.BlockSpec(a.shape,lambda j,h:(0,0))
    return pl.pallas_call(partial(bwd_body,bk=bk,nk=nk),
        grid=(nk,NH),
        in_specs=[full(q),pl.BlockSpec((bk,2*W),lambda j,h:(j,0)),pl.BlockSpec((bk,128),lambda j,h:(j,0)),full(cf),full(st),full(dc)],
        out_specs=[pl.BlockSpec((n,W),lambda j,h:(0,0)),pl.BlockSpec((bk,2*W),lambda j,h:(j,0))],
        out_shape=[jax.ShapeDtypeStruct((n,W),BF16),jax.ShapeDtypeStruct((L,2*W),F32)],
        scratch_shapes=[pltpu.VMEM((NH,128,n),BF16),pltpu.VMEM((NH,n,128),BF16),pltpu.VMEM((NH,128,n),BF16),pltpu.VMEM((NH,n,128),BF16),
            pltpu.VMEM((NH,HEAD,n),F32),pltpu.VMEM((NH,bk,128),F32),pltpu.VMEM((NH,bk,128),F32)],
        name="attend_backward",
    )(q,kv,kb,cf,st,dc)


def outer_grads_body(a_ref, do_ref, out_ref, *, chips):
    width = do_ref.shape[1]
    r_out = a_ref.shape[1] // chips
    half = chips // 2
    for j in range(2):
        grad = t_dot(a_ref[:, j * width : (j + 1) * width], do_ref[...]).astype(BF16)
        for q in range(half):
            out_ref[j * half + q] = grad[q * r_out : (q + 1) * r_out]


def outer_grads(a, do, chips):
    width = do.shape[1]
    return pl.pallas_call(
        partial(outer_grads_body, chips=chips),
        out_shape=jax.ShapeDtypeStruct((chips, a.shape[1] // chips, width), BF16),
        cost_estimate=pl.CostEstimate(
            flops=2 * a.shape[0] * a.shape[1] * width, transcendentals=0, bytes_accessed=7 * width * width * 2
        ),
        name="outer_grads",
    )(a, do)


def inner_grads_body(y_ref, dz_ref, ctx_ref, da_ref, do_ref, vec_ref, out_ref, *, chips):
    width = y_ref.shape[1]
    r_in, r_ctx = width // chips, ctx_ref.shape[1] // chips
    for j in range(2):
        grad = t_dot(y_ref[...], dz_ref[:, j * width : (j + 1) * width]).astype(BF16)
        for q in range(chips):
            out_ref[q, j * r_in : (j + 1) * r_in] = grad[q * r_in : (q + 1) * r_in]
    first = 2 * r_in
    grad = t_dot(ctx_ref[...], da_ref[...]).astype(BF16)
    for q in range(chips):
        out_ref[q, first : first + r_ctx] = grad[q * r_ctx : (q + 1) * r_ctx]
    n = do_ref.shape[0]
    ones = jnp.ones((16, y_ref.shape[0]), BF16)
    sums = [dot(ones[:, :n], da_ref[:n])[:1], dot(ones[:, :n], do_ref[...])[:1]]
    sums += [dot(ones, dz_ref[:, j * width : (j + 1) * width])[:1] for j in range(2)]
    small = jnp.concatenate([vec_ref[...]] + sums, axis=0).astype(BF16)
    for q in range(chips):
        out_ref[q, first + r_ctx :] = small


def inner_grads(y, dz, ctx, da, do, vec, chips):
    width = y.shape[1]
    total = 2 * width // chips + ctx.shape[1] // chips + vec.shape[0] + 4
    return pl.pallas_call(
        partial(inner_grads_body, chips=chips),
        out_shape=jax.ShapeDtypeStruct((chips, total, width), BF16),
        cost_estimate=pl.CostEstimate(
            flops=2 * width * y.shape[0] * (dz.shape[1] + ctx.shape[1]), transcendentals=0, bytes_accessed=8 * width * width * 2
        ),
        name="inner_grads",
    )(y, dz, ctx, da, do, vec)


def per_device(
    seq_size,
    grp_size,
    tokens,
    valid_len,
    query_weight,
    query_bias,
    key_weight,
    value_weight,
    value_bias,
    output_weight,
    output_bias,
    first_gain,
    first_shift,
    inner_weight,
    inner_bias,
    outer_weight,
    outer_bias,
    second_gain,
    second_shift,
    grad_out,
):
    bf16 = jnp.bfloat16
    rows, width = tokens.shape[1:]
    feed = inner_weight.shape[1]
    shard = query_weight.shape[0]
    HI, ZO, YO = seq_size // 2, seq_size // 4, 2
    extra_bits = [1 << b for b in range(2, log2_of(ZO))]
    part_bits = [1] + extra_bits
    me = lax.axis_index("seq")
    grp = lax.axis_index("grp")
    z1 = me // HI
    z0 = (me // ZO) % 2
    y0 = (me // YO) % 2
    head_group = 2 * z0 + y0
    my_part = me % 2 + 2 * ((me // 4) % max(ZO // 4, 1))
    n_parts = seq_size // 8

    def sflip(value, mask):
        return flip(value, "seq", seq_size, mask)

    chips = seq_size // 2
    x_mine = pick(tokens, z1)
    x_sent = pick(tokens, 1 - z1)
    half_width = width // 2
    x_theirs = sflip(x_sent, HI)
    x_pair = in_order(x_mine, x_theirs, z1)
    xa, xb = x_pair[:, :, :half_width], x_pair[:, :, half_width:]
    ra, rb = sflip(xa, YO), sflip(xb, ZO)
    xa, xb = in_order(xa, ra, y0), in_order(xb, rb, z0)
    ra, rb = sflip(xa, ZO), sflip(xb, YO)
    xa, xb = in_order(xa, ra, z0), in_order(xb, rb, y0)
    x_all = jnp.concatenate([xa.transpose(2, 0, 1, 3, 4), xb.transpose(2, 1, 0, 3, 4)], axis=-1)
    x_all = x_all.reshape(8 * rows, width)

    core = me % 2
    chips = seq_size // 2
    piece = feed // seq_size
    n_dev = grp_size * seq_size
    half_feed = feed // 2
    split = inner_weight.reshape(shard, chips, 2, piece)
    split = [split[:, :, i].reshape(shard, 2, width).transpose(1, 0, 2).reshape(2 * shard, width) for i in range(2)]
    near = jnp.concatenate([pick(split, 1 - core), output_weight], axis=0)
    far = sflip(near, 1)
    outer_far = lax.ppermute(
        outer_weight,
        ("grp", "seq"),
        [(d, d ^ (1 | grp_size) if d % 2 != (d // grp_size) % 2 else d) for d in range(n_dev)],
    )
    inner_pair = in_order(pick(split, core).reshape(2, shard, width), far[: 2 * shard].reshape(2, shard, width), core)
    packed = jnp.concatenate(
        [
            inner_pair.transpose(1, 0, 2, 3).reshape(4 * shard, width),
            outer_far,
            in_order(output_weight, far[2 * shard :], core).reshape(2 * shard, width),
        ],
        axis=0,
    )
    chip_groups = [[2 * q + i for q in range(chips)] for i in range(2)]
    gathered = lax.all_gather(packed, "seq", axis=0, tiled=False, axis_index_groups=chip_groups)
    for b in range(log2_of(grp_size)):
        theirs = flip(gathered, "grp", grp_size, 1 << b)
        gathered = in_order(gathered, theirs, (grp >> b) % 2).reshape((-1,) + packed.shape)

    smalls = jnp.concatenate(
        [query_bias, value_bias, output_bias, first_gain, first_shift, outer_bias, second_gain, second_shift, inner_bias]
    )
    small_rows = 32 - shard if shard == 24 else 8
    grouped = jnp.stack([query_weight, key_weight, value_weight]).reshape(3, shard, HEAD_GROUPS, GROUP_WIDTH)
    grouped = grouped.transpose(2, 1, 0, 3).reshape(HEAD_GROUPS, shard, 3 * GROUP_WIDTH)
    small_block = jnp.zeros((small_rows * 3 * GROUP_WIDTH,), bf16).at[: smalls.shape[0]].set(smalls)
    small_block = jnp.broadcast_to(small_block.reshape(1, small_rows, -1), (HEAD_GROUPS, small_rows, 3 * GROUP_WIDTH))
    grouped = jnp.concatenate([grouped, small_block], axis=1)
    grouped, _ = lax.optimization_barrier((grouped, x_theirs))

    def group_block(k):
        return lax.dynamic_index_in_dim(grouped, head_group ^ k, 0, keepdims=False)

    w0 = group_block(0)
    w1 = sflip(group_block(1), YO)
    w2 = sflip(group_block(2), ZO)
    w3 = sflip(group_block(3), ZO | YO)
    w_all = in_order(in_order(w0, w1, y0), in_order(w2, w3, y0), z0)
    w_all = in_order(w_all, sflip(w_all, HI), z1)
    names = ["z1", "z0", "y0"]
    for b in extra_bits:
        w_all = in_order(w_all, sflip(w_all, b), (me // b) % 2)
        names = ["e%d" % b] + names
    for b in range(log2_of(grp_size)):
        w_all = in_order(w_all, flip(w_all, "grp", grp_size, 1 << b), (grp >> b) % 2)
        names = ["g%d" % b] + names
    w_all = in_order(w_all, sflip(w_all, 1), me % 2)
    names = ["c"] + names
    wanted = ["g%d" % b for b in reversed(range(log2_of(grp_size)))] + ["z1", "z0"]
    wanted += ["e%d" % b for b in reversed(extra_bits)] + ["y0", "c"]
    n = len(names)
    w_all = w_all.transpose(*[names.index(w) for w in wanted], n, n + 1)
    w_all = w_all.reshape(grp_size * seq_size, shard + small_rows, 3 * GROUP_WIDTH)
    small_all = w_all[:, shard:].reshape(grp_size * seq_size, -1)[:, : smalls.shape[0]]
    vectors = [small_all[:, i * shard : (i + 1) * shard].reshape(-1).astype(jnp.float32) for i in range(8)]
    q_bias, v_bias, o_bias, gain1, shift1, out_bias, gain2, shift2 = vectors
    in_bias = small_all[:, 8 * shard :].reshape(-1).astype(jnp.float32)
    w_all = w_all[:, :shard].reshape(width, 3 * GROUP_WIDTH)

    def own_columns(vector):
        return lax.dynamic_slice_in_dim(vector, head_group * GROUP_WIDTH, GROUP_WIDTH)

    qkv_bias = jnp.concatenate([own_columns(q_bias), jnp.zeros((GROUP_WIDTH,), jnp.float32), own_columns(v_bias)])
    qkv = dot(x_all, w_all) + qkv_bias
    queries = (qkv[:, :GROUP_WIDTH] * score_scale).astype(bf16)
    kv = qkv[:, GROUP_WIDTH:].astype(bf16)[None]
    for b in part_bits:
        bit = (me // b) % 2
        theirs = sflip(kv, b)
        kv = jnp.where(bit == 0, jnp.concatenate([kv, theirs]), jnp.concatenate([theirs, kv]))
    kv = kv.reshape(-1, 2 * GROUP_WIDTH)

    part = jnp.arange(n_parts, dtype=jnp.int32)
    part_device = part % 2 + 4 * (part // 2)
    member = jnp.arange(8, dtype=jnp.int32)
    member_device = (member // 4) * HI + ((member // 2) % 2) * ZO + (member % 2) * YO
    device = part_device[:, None] + member_device[None, :]
    position = (device[:, :, None] * rows + jnp.arange(rows, dtype=jnp.int32)).reshape(-1)
    bias = jnp.where(position < pick(valid_len, z1), 0.0, masked_score)[:, None]
    lane = jnp.arange(128, dtype=jnp.int32)[None, :]
    key_tail = jnp.where(lane == HEAD, bias, jnp.where((lane > HEAD) & (lane < HEAD + 4), 1.0, 0.0)).astype(bf16)

    context, context_full, stats = attend_forward(queries, kv, key_tail)

    teams = [
        [a * HI + b * ZO + c * YO + q for a in range(2) for b in range(2) for c in range(2)]
        for q in [i % 2 + 4 * (i // 2) for i in range(n_parts)]
    ]

    def exchange(blocks):
        return lax.all_to_all(blocks, "seq", 0, 0, axis_index_groups=teams, tiled=True)

    context = exchange(context.reshape(8, rows, GROUP_WIDTH))
    context = context.reshape(2, HEAD_GROUPS, rows, GROUP_WIDTH).transpose(0, 2, 1, 3).reshape(2 * rows, width)

    inner_lo = gathered[:, : 2 * shard].reshape(width, width)
    inner_hi = gathered[:, 2 * shard : 4 * shard].reshape(width, width)
    outer_end = 4 * shard + outer_weight.shape[0]
    outer_all = gathered[:, 4 * shard : outer_end].reshape(-1, 2, grp_size // 2, outer_weight.shape[0], width)
    outer_all = outer_all.transpose(0, 2, 1, 3, 4).reshape(half_feed, width)
    output_all = gathered[:, outer_end:].reshape(width, width)
    outer_lo, outer_hi = outer_all[:width], outer_all[width:]
    in_bias = pick(in_bias.reshape(chips, 2, piece).transpose(1, 0, 2).reshape(2, half_feed), core)

    home = tokens.reshape(2 * rows, width)
    cotangent = grad_out.reshape(2 * rows, width)
    hidden_one = home.astype(jnp.float32) + dot(context, output_all) + o_bias
    norm_one, norm_back_one = jax.vjp(layer_norm, hidden_one, gain1, shift1)
    first_out = norm_one.astype(bf16)
    n_own = 2 * rows
    both_first = jnp.concatenate([first_out, sflip(first_out, 1)], axis=0)

    def gelu_pair(pre):
        full, back = jax.vjp(partial(jax.nn.gelu, approximate=False), pre)
        return full.astype(bf16), back(jnp.ones_like(pre))[0]

    inner_all = jnp.concatenate([inner_lo, inner_hi], axis=1)
    active, slope = gelu_pair(dot(both_first, inner_all) + in_bias)
    outer_part = dot(active, outer_all)
    outer_sum = outer_part[:n_own] + sflip(outer_part[n_own:].astype(bf16), 1).astype(jnp.float32)
    hidden_two = first_out.astype(jnp.float32) + outer_sum + out_bias
    layer_out, norm_back_two = jax.vjp(layer_norm, hidden_two, gain2, shift2)
    dhidden_two, dsecond_gain, dsecond_shift = norm_back_two(cotangent.astype(jnp.float32))
    douter = dhidden_two.astype(bf16)
    both_douter = jnp.concatenate([douter, sflip(douter, 1)], axis=0)

    def over_chips(blocks):
        return lax.psum_scatter(blocks, "seq", scatter_dimension=0, tiled=False, axis_index_groups=chip_groups)

    def over_groups(blocks):
        for b in range(log2_of(grp_size)):
            blocks = (blocks.astype(jnp.float32) + flip(blocks, "grp", grp_size, 1 << b).astype(jnp.float32)).astype(bf16)
        return blocks

    outer_blocks, both_douter = lax.optimization_barrier((outer_grads(active, both_douter, chips), both_douter))
    outer_sums = over_chips(outer_blocks)
    dinner = (dot_t(both_douter, outer_all) * slope).astype(bf16)
    dfirst_part = dot_t(dinner, inner_all)
    dfirst = dhidden_two + dfirst_part[:n_own] + sflip(dfirst_part[n_own:].astype(bf16), 1).astype(jnp.float32)
    dhidden_one, dfirst_gain, dfirst_shift = norm_back_one(dfirst)
    dattend = dhidden_one.astype(bf16)
    dcontext = dot_t(dattend, output_all).astype(bf16)
    dcontext = dcontext.reshape(2, rows, HEAD_GROUPS, GROUP_WIDTH).transpose(0, 2, 1, 3)
    dcontext = exchange(dcontext.reshape(8, rows, GROUP_WIDTH)).reshape(8 * rows, GROUP_WIDTH)

    out_rows = width // seq_size
    ctx_split = context.reshape(n_own, chips, 2, out_rows)
    ctx_split = [ctx_split[:, :, i].reshape(n_own, width // 2) for i in range(2)]
    both_ctx = jnp.concatenate([pick(ctx_split, core), sflip(pick(ctx_split, 1 - core), 1)], axis=0)
    both_dattend = jnp.concatenate([dattend, sflip(dattend, 1)], axis=0)
    vectors = jnp.stack([dfirst_gain, dfirst_shift, dsecond_gain, dsecond_shift])
    inner_blocks = inner_grads(both_first, dinner, both_ctx, both_dattend, douter, vectors, chips)
    inner_blocks, dcontext = lax.optimization_barrier((inner_blocks, dcontext))
    inner_sums = over_chips(inner_blocks)

    dqueries, dkv = attend_backward(queries, kv, key_tail, context_full, stats, dcontext)
    dkv = dkv.reshape(n_parts, 8 * rows, 2 * GROUP_WIDTH)
    for b in reversed(part_bits):
        bit = (me // b) % 2
        n_now = dkv.shape[0] // 2
        low, high = dkv[:n_now], dkv[n_now:]
        sent = jnp.where(bit == 0, high, low).astype(bf16)
        dkv = jnp.where(bit == 0, low, high) + sflip(sent, b).astype(jnp.float32)
    dqkv = jnp.concatenate([dqueries, dkv[0].astype(bf16)], axis=1)

    dqkv, outer_sums, inner_sums = lax.optimization_barrier((dqkv, outer_sums, inner_sums))

    dx = dot_t(dqkv, w_all).reshape(2, 2, 2, rows, width)
    da, db = dx[..., :half_width], dx[..., half_width:]

    def halve(low, high, bit, mask):
        sent = jnp.where(bit == 0, high, low).astype(bf16)
        return jnp.where(bit == 0, low, high) + sflip(sent, mask).astype(jnp.float32)

    da = halve(da[:, :, 0], da[:, :, 1], y0, YO)
    db = halve(db[:, 0], db[:, 1], z0, ZO)
    da = halve(da[:, 0], da[:, 1], z0, ZO)
    db = halve(db[:, 0], db[:, 1], y0, YO)
    dx = jnp.concatenate([da, db], axis=-1)
    mine = pick(dx, z1)
    theirs = sflip(pick(dx, 1 - z1).astype(bf16), HI).astype(jnp.float32)
    dtokens = dhidden_one.reshape(2, rows, width) + in_order(mine, theirs, z1)

    grads = over_groups(inner_sums)
    douter_weight = over_groups(outer_sums).astype(jnp.float32)
    r1 = 4 * out_rows
    r3 = r1 + out_rows
    inner_grad = grads[:r1].reshape(2, 2, out_rows, width)
    inner_grad = [inner_grad[:, i] for i in range(2)]
    far = sflip(jnp.concatenate([pick(inner_grad, 1 - core).reshape(2 * out_rows, width), grads[r3 : r3 + 8]], axis=0), 1)
    dinner_weight = in_order(pick(inner_grad, core), far[: 2 * out_rows].reshape(2, out_rows, width), core)
    dinner_weight = dinner_weight.transpose(2, 0, 1, 3).reshape(out_rows, 2, chips, piece).transpose(0, 2, 1, 3)
    dinner_weight = dinner_weight.reshape(out_rows, feed).astype(jnp.float32)
    doutput_weight = grads[r1:r3].astype(jnp.float32)
    small = grads[r3 : r3 + 8].astype(jnp.float32)
    both = lax.dynamic_slice_in_dim(small + far[2 * out_rows :].astype(jnp.float32), me * out_rows, out_rows, axis=1)
    dfirst_gain, dfirst_shift, dsecond_gain, dsecond_shift, doutput_bias, douter_bias = (both[i] for i in range(6))
    dinner_bias = lax.dynamic_slice_in_dim(small[6:8].reshape(half_feed), (me // 2) * piece, piece)

    dw = t_dot(x_all, dqkv)
    dbias = column_sums(dqkv)
    dw = dw.reshape(seq_size, out_rows, 3 * GROUP_WIDTH)
    dw = jnp.concatenate([dw, jnp.broadcast_to(dbias, (seq_size, 8, 3 * GROUP_WIDTH))], axis=1)
    block = dw.shape[1]
    n_extra = 1 << len(extra_bits)
    dw = dw.reshape(2, 2, 2, n_extra, 2, 1, block, 3 * GROUP_WIDTH)[:, :, :, :, :, 0]
    dw = dw.reshape(2, 2, n_extra, 2, 2, block, 3 * GROUP_WIDTH)
    dw = halve(dw[:, :, :, :, 0], dw[:, :, :, :, 1], me % 2, 1)
    for b in reversed(extra_bits):
        m = dw.shape[2] // 2
        dw = halve(dw[:, :, :m], dw[:, :, m:], (me // b) % 2, b)
    dw = dw[:, :, 0]
    dw = halve(dw[0], dw[1], z1, HI)
    for b in range(log2_of(grp_size)):
        dw = dw + flip(dw.astype(bf16), "grp", grp_size, 1 << b).astype(jnp.float32)
    dw = dw.astype(bf16).reshape(HEAD_GROUPS, block, 3 * GROUP_WIDTH)

    def row_block(k):
        return lax.dynamic_index_in_dim(dw, head_group ^ k, 0, keepdims=False)

    w0 = row_block(0)
    w1 = sflip(row_block(1), YO)
    w2 = sflip(row_block(2), ZO)
    w3 = sflip(row_block(3), ZO | YO)
    dw = in_order(in_order(w0, w1, y0), in_order(w2, w3, y0), z0).reshape(HEAD_GROUPS, block, 3, GROUP_WIDTH)
    dw = dw.astype(jnp.float32).transpose(2, 1, 0, 3).reshape(3, block, width)
    dquery_weight, dkey_weight, dvalue_weight = dw[0, :out_rows], dw[1, :out_rows], dw[2, :out_rows]
    dquery_bias = lax.dynamic_slice_in_dim(dw[0, out_rows], me * out_rows, out_rows)
    dvalue_bias = lax.dynamic_slice_in_dim(dw[2, out_rows], me * out_rows, out_rows)

    return (
        layer_out.astype(bf16).reshape(2, rows, width),
        dtokens.astype(bf16),
        dquery_weight,
        dquery_bias,
        dkey_weight,
        dvalue_weight,
        dvalue_bias,
        doutput_weight,
        doutput_bias,
        dfirst_gain,
        dfirst_shift,
        dinner_weight,
        dinner_bias,
        douter_weight,
        douter_bias,
        dsecond_gain,
        dsecond_shift,
    )


def solution(mesh):
    in_specs = (
        P("grp", "seq", None),
        P("grp"),
        P(("grp", "seq"), None),
        P(("grp", "seq")),
        P(("grp", "seq"), None),
        P(("grp", "seq"), None),
        P(("grp", "seq")),
        P(("grp", "seq"), None),
        P(("grp", "seq")),
        P(("grp", "seq")),
        P(("grp", "seq")),
        P(("grp", "seq"), None),
        P(("grp", "seq")),
        P(("grp", "seq"), None),
        P(("grp", "seq")),
        P(("grp", "seq")),
        P(("grp", "seq")),
        P("grp", "seq", None),
    )
    out_specs = (
        P("grp", "seq", None),
        P("grp", "seq", None),
        P("seq", None),
        P("seq"),
        P("seq", None),
        P("seq", None),
        P("seq"),
        P("seq", None),
        P("seq"),
        P("seq"),
        P("seq"),
        P("seq", None),
        P("seq"),
        P("seq", None),
        P("seq"),
        P("seq"),
        P("seq"),
    )
    body = partial(per_device, mesh.shape["seq"], mesh.shape["grp"])
    return jax.shard_map(
        body, mesh=mesh, in_specs=in_specs, out_specs=out_specs, check_vma=False
    )
```

```python
from functools import partial

import jax
import jax.numpy as jnp
from jax import lax
from jax.experimental import pallas as pl
from jax.experimental.pallas import tpu as pltpu
from jax.sharding import PartitionSpec as P

HEADS = 12
HEAD = 64
HEAD_GROUPS = 4
GROUP_WIDTH = HEADS * HEAD // HEAD_GROUPS
NH = HEADS // HEAD_GROUPS
BF16 = jnp.bfloat16
F32 = jnp.float32

score_scale = 0.125
epsilon = 1e-12
masked_score = -1e30


def log2_of(size):
    return size.bit_length() - 1


def flip(value, axis, size, mask):
    return lax.ppermute(value, axis, [(i, i ^ mask) for i in range(size)])


def in_order(mine, theirs, bit):
    return jnp.where(bit == 0, jnp.stack([mine, theirs]), jnp.stack([theirs, mine]))


def pick(pair, bit):
    return jnp.where(bit == 0, pair[0], pair[1])


def layer_norm(hidden, norm_gain, norm_shift):
    centred = hidden - jnp.mean(hidden, axis=-1, keepdims=True)
    spread = jnp.mean(centred * centred, axis=-1, keepdims=True)
    return centred * lax.rsqrt(spread + epsilon) * norm_gain + norm_shift


def dot(left, right):
    return jnp.dot(left, right, preferred_element_type=jnp.float32)


def dot_t(left, right):
    return lax.dot_general(left, right, (((1,), (1,)), ((), ())), preferred_element_type=jnp.float32)


def t_dot(left, right):
    return lax.dot_general(left, right, (((0,), (0,)), ((), ())), preferred_element_type=jnp.float32)


def column_sums(matrix):
    return jnp.sum(matrix.astype(jnp.float32), axis=0)


def thirds(x):
    hi=x.astype(BF16)
    r=x-hi.astype(F32)
    mid=r.astype(BF16)
    lo=(r-mid.astype(F32)).astype(BF16)
    return hi,mid,lo

def fwd_body(q_ref, kv_ref, kb_ref, c_ref, cf_ref, st_ref, kt, va, oacc, lacc, *, bq):
    i=pl.program_id(0); h=pl.program_id(1)
    W=NH*HEAD
    @pl.when((i==0)&(h==0))
    def _():
        tail=kb_ref[:,HEAD:]
        for g in range(NH):
            ka=jnp.concatenate([kv_ref[:,g*HEAD:(g+1)*HEAD],tail],axis=1)
            kt[g]=ka.T
            va[g]=jnp.concatenate([kv_ref[:,W+g*HEAD:W+(g+1)*HEAD],tail],axis=1)
    one=jnp.where(lax.broadcasted_iota(jnp.int32,(bq,HEAD),1)==0,1.0,0.0).astype(BF16)
    def head(g):
        qa=jnp.concatenate([q_ref[:,g*HEAD:(g+1)*HEAD],one],axis=1)
        s=dot(qa,kt[g])
        m=jnp.max(s,axis=1,keepdims=True)
        p=jnp.exp(s-m).astype(BF16)
        o=dot(p,va[g])
        l=o[:,HEAD+1:HEAD+2]
        oacc[g]=o/l
        lacc[g]=jnp.broadcast_to(m+jnp.log(l),(bq,128))
    for g in range(NH):
        @pl.when(h==g)
        def _(): head(g)
    @pl.when(h==NH-1)
    def _():
        c=jnp.concatenate([oacc[g][:,:HEAD] for g in range(NH)],axis=1)
        c_ref[...]=c.astype(BF16)
        cf_ref[...]=c
        lane=lax.broadcasted_iota(jnp.int32,(bq,128),1)
        st=lacc[0]
        for g in range(1,NH): st=jnp.where(lane==g,lacc[g],st)
        st_ref[...]=st

def attend_forward(q,kv,kb,bq=256):
    n,W=q.shape; L=kv.shape[0]
    return pl.pallas_call(partial(fwd_body,bq=bq),
        grid=(n//bq,NH),
        in_specs=[pl.BlockSpec((bq,W),lambda i,h:(i,0)),pl.BlockSpec((L,2*W),lambda i,h:(0,0)),pl.BlockSpec((L,128),lambda i,h:(0,0))],
        out_specs=[pl.BlockSpec((bq,W),lambda i,h:(i,0)),pl.BlockSpec((bq,W),lambda i,h:(i,0)),pl.BlockSpec((bq,128),lambda i,h:(i,0))],
        out_shape=[jax.ShapeDtypeStruct((n,W),BF16),jax.ShapeDtypeStruct((n,W),F32),jax.ShapeDtypeStruct((n,128),F32)],
        scratch_shapes=[pltpu.VMEM((NH,128,L),BF16),pltpu.VMEM((NH,L,128),BF16),pltpu.VMEM((NH,bq,128),F32),pltpu.VMEM((NH,bq,128),F32)],
        cost_estimate=pl.CostEstimate(flops=16*n*L*W, transcendentals=NH*n*L, bytes_accessed=4*n*L),
        name="attend_forward",
    )(q,kv,kb)

def bwd_body(bit_ref, q_ref, kv_ref, kb_ref, cf_ref, st_ref, dc_ref, dq_ref, sent_ref, kept_ref, qt, qn, dct, dcn, dqt, dk, dv, *, nk):
    j=pl.program_id(0); h=pl.program_id(1)
    W=NH*HEAD
    n=q_ref.shape[0]
    @pl.when((j==0)&(h==0))
    def _():
        pad=jnp.zeros((n,256-W),BF16)
        row=lax.broadcasted_iota(jnp.int32,(16,n),0)
        lane=lax.broadcasted_iota(jnp.int32,(8,W),1)
        head_row=lax.broadcasted_iota(jnp.int32,(8,W),0)
        pick=jnp.where((lane>=head_row*HEAD)&(lane<head_row*HEAD+HEAD),1.0,0.0).astype(BF16)
        prod=dc_ref[...].astype(F32)*cf_ref[...]
        hi,mid,lo=thirds(prod)
        deltas=dot_t(pick,hi)+dot_t(pick,mid)+dot_t(pick,lo)
        stats=st_ref[...].T
        q_t=jnp.concatenate([q_ref[...],pad],axis=1).T
        d_t=jnp.concatenate([dc_ref[...],pad],axis=1).T
        def tail(x,first):
            hi,mid,lo=(v.astype(F32) for v in thirds(-x))
            z=jnp.where(row==1,hi,jnp.where(row==2,mid,jnp.where(row==3,lo,0.0)))
            return jnp.where(row==0,first,z).astype(BF16)
        rest=jnp.zeros((HEAD-16,n),BF16)
        for g in range(NH):
            cols=slice(g*HEAD,(g+1)*HEAD)
            for t,x,first,dst in ((q_t,stats,1.0,qt),(d_t,deltas,0.0,dct)):
                dst[g,:HEAD]=t[cols]
                dst[g,HEAD:HEAD+16]=tail(x[g:g+1],first)
                dst[g,HEAD+16:]=rest
            qn[g]=q_ref[:,cols]
            dcn[g]=dc_ref[:,cols]
        dqt[...]=jnp.zeros_like(dqt)
    key_tail=kb_ref[:,HEAD:]
    def head(g):
        k=kv_ref[:,g*HEAD:(g+1)*HEAD]
        ka=jnp.concatenate([k,key_tail],axis=1)
        va=jnp.concatenate([kv_ref[:,W+g*HEAD:W+(g+1)*HEAD],key_tail],axis=1)
        p=jnp.exp(dot(ka,qt[g]))
        dp=dot(va,dct[g])
        ds=(p*dp).astype(BF16)
        dv[g]=dot(p.astype(BF16),dcn[g])
        dk[g]=dot(ds,qn[g])
        dqt[g]=dqt[g]+t_dot(ka,ds)[:HEAD]
    for g in range(NH):
        @pl.when(h==g)
        def _(): head(g)
    @pl.when(h==NH-1)
    def _():
        dkv=jnp.concatenate([dk[g] for g in range(NH)]+[dv[g] for g in range(NH)],axis=1)
        @pl.when(j<nk//2)
        def _():
            sent_ref[...]=dkv.astype(BF16)
        @pl.when(j>=nk//2)
        def _():
            kept_ref[...]=dkv
    @pl.when((h==NH-1)&(j==nk-1))
    def _():
        for g in range(NH):
            dq_ref[:,g*HEAD:(g+1)*HEAD]=(dqt[g].T*0.125).astype(BF16)

def attend_backward(q,kv,kb,cf,st,dc,bit,bk=768):
    n,W=q.shape; L=kv.shape[0]; nk=L//bk; half=nk//2
    full=lambda a: pl.BlockSpec(a.shape,lambda j,h,b:(0,0))
    key=lambda j,h,b:(jnp.where(j<half,(1-b[0])*half+j,b[0]*half+j-half),0)
    return pl.pallas_call(partial(bwd_body,nk=nk),
        grid_spec=pltpu.PrefetchScalarGridSpec(
            num_scalar_prefetch=1,
            grid=(nk,NH),
            in_specs=[full(q),pl.BlockSpec((bk,2*W),key),pl.BlockSpec((bk,128),key),full(cf),full(st),full(dc)],
            out_specs=[pl.BlockSpec((n,W),lambda j,h,b:(0,0)),
                pl.BlockSpec((bk,2*W),lambda j,h,b:(jnp.minimum(j,half-1),0)),
                pl.BlockSpec((bk,2*W),lambda j,h,b:(jnp.maximum(j-half,0),0))],
            scratch_shapes=[pltpu.VMEM((NH,2*HEAD,n),BF16),pltpu.VMEM((NH,n,HEAD),BF16),pltpu.VMEM((NH,2*HEAD,n),BF16),pltpu.VMEM((NH,n,HEAD),BF16),
                pltpu.VMEM((NH,HEAD,n),F32),pltpu.VMEM((NH,bk,HEAD),F32),pltpu.VMEM((NH,bk,HEAD),F32)]),
        out_shape=[jax.ShapeDtypeStruct((n,W),BF16),jax.ShapeDtypeStruct((L//2,2*W),BF16),jax.ShapeDtypeStruct((L//2,2*W),F32)],
        name="attend_backward",
    )(bit,q,kv,kb,cf,st,dc)


def weight_grads_body(y_ref, dz_ref, a_ref, do_ref, ctx_ref, da_ref, vec_ref, out_ref, *, chips):
    width = y_ref.shape[1]
    r_in, r_ctx = width // chips, ctx_ref.shape[1] // chips
    r_out = a_ref.shape[1] // chips
    for j in range(2):
        grad = t_dot(y_ref[...], dz_ref[:, j * width : (j + 1) * width]).astype(BF16)
        for q in range(chips):
            out_ref[q, j * r_in : (j + 1) * r_in] = grad[q * r_in : (q + 1) * r_in]
        grad = t_dot(a_ref[:, j * width : (j + 1) * width], do_ref[...]).astype(BF16)
        half = chips // 2
        for q in range(half):
            out_ref[j * half + q, 2 * r_in : 2 * r_in + r_out] = grad[q * r_out : (q + 1) * r_out]
    first = 2 * r_in + r_out
    grad = t_dot(ctx_ref[...], da_ref[...]).astype(BF16)
    for q in range(chips):
        out_ref[q, first : first + r_ctx] = grad[q * r_ctx : (q + 1) * r_ctx]
    own = vec_ref.shape[0]
    n = da_ref.shape[0] // 2
    ones = jnp.ones((16, y_ref.shape[0]), BF16)
    sums = [dot(ones[:, :n], da_ref[:n])[:1], dot(ones[:, :n], do_ref[:n])[:1]]
    sums += [dot(ones, dz_ref[:, j * width : (j + 1) * width])[:1] for j in range(2)]
    small = jnp.concatenate([vec_ref[...]] + sums, axis=0).astype(BF16)
    for q in range(chips):
        out_ref[q, first + r_ctx : first + r_ctx + own + 4] = small


def weight_grads(y, dz, a, do, ctx, da, vec, chips):
    width = y.shape[1]
    total = 2 * width // chips + a.shape[1] // chips + ctx.shape[1] // chips + vec.shape[0] + 4
    return pl.pallas_call(
        partial(weight_grads_body, chips=chips),
        out_shape=jax.ShapeDtypeStruct((chips, total, width), BF16),
        cost_estimate=pl.CostEstimate(
            flops=2 * width * y.shape[0] * (2 * dz.shape[1] + ctx.shape[1]), transcendentals=0, bytes_accessed=15 * width * width * 2
        ),
        name="weight_grads",
    )(y, dz, a, do, ctx, da, vec)


def per_device(
    seq_size,
    grp_size,
    tokens,
    valid_len,
    query_weight,
    query_bias,
    key_weight,
    value_weight,
    value_bias,
    output_weight,
    output_bias,
    first_gain,
    first_shift,
    inner_weight,
    inner_bias,
    outer_weight,
    outer_bias,
    second_gain,
    second_shift,
    grad_out,
):
    bf16 = jnp.bfloat16
    rows, width = tokens.shape[1:]
    feed = inner_weight.shape[1]
    shard = query_weight.shape[0]
    HI, ZO, YO = seq_size // 2, seq_size // 4, 2
    extra_bits = [1 << b for b in range(2, log2_of(ZO))]
    part_bits = [1] + extra_bits
    me = lax.axis_index("seq")
    grp = lax.axis_index("grp")
    z1 = me // HI
    z0 = (me // ZO) % 2
    y0 = (me // YO) % 2
    head_group = 2 * z0 + y0
    my_part = me % 2 + 2 * ((me // 4) % max(ZO // 4, 1))
    n_parts = seq_size // 8

    def sflip(value, mask):
        return flip(value, "seq", seq_size, mask)

    chips = seq_size // 2
    x_mine = pick(tokens, z1)
    x_sent = pick(tokens, 1 - z1)
    half_width = width // 2
    x_theirs = sflip(x_sent, HI)
    x_pair = in_order(x_mine, x_theirs, z1)
    xa, xb = x_pair[:, :, :half_width], x_pair[:, :, half_width:]
    ra, rb = sflip(xa, YO), sflip(xb, ZO)
    xa, xb = in_order(xa, ra, y0), in_order(xb, rb, z0)
    ra, rb = sflip(xa, ZO), sflip(xb, YO)
    xa, xb = in_order(xa, ra, z0), in_order(xb, rb, y0)
    x_all = jnp.concatenate([xa.transpose(2, 0, 1, 3, 4), xb.transpose(2, 1, 0, 3, 4)], axis=-1)
    x_all = x_all.reshape(8 * rows, width)

    core = me % 2
    chips = seq_size // 2
    piece = feed // seq_size
    n_dev = grp_size * seq_size
    half_feed = feed // 2
    split = inner_weight.reshape(shard, chips, 2, piece)
    split = [split[:, :, i].reshape(shard, 2, width).transpose(1, 0, 2).reshape(2 * shard, width) for i in range(2)]
    near = jnp.concatenate([pick(split, 1 - core), output_weight], axis=0)
    far = sflip(near, 1)
    outer_far = lax.ppermute(
        outer_weight,
        ("grp", "seq"),
        [(d, d ^ (1 | grp_size) if d % 2 != (d // grp_size) % 2 else d) for d in range(n_dev)],
    )
    inner_pair = in_order(pick(split, core).reshape(2, shard, width), far[: 2 * shard].reshape(2, shard, width), core)
    packed = jnp.concatenate(
        [
            inner_pair.transpose(1, 0, 2, 3).reshape(4 * shard, width),
            in_order(output_weight, far[2 * shard :], core).reshape(2 * shard, width),
            outer_far,
        ],
        axis=0,
    )
    chip_groups = [[2 * q + i for q in range(chips)] for i in range(2)]
    gathered = lax.all_gather(packed, "seq", axis=0, tiled=False, axis_index_groups=chip_groups)
    first_end = 6 * shard
    gathered = [gathered[:, :first_end], gathered[:, first_end:]]
    gathered = [[part[None]] for part in gathered]
    for b in range(log2_of(grp_size)):
        for part in gathered:
            part += [flip(part[i], "grp", grp_size, 1 << b) for i in range(len(part))]

    def gathered_rows(which, start, stop):
        parts = [x[0, :, start:stop] for x in gathered[which]]
        stacks = {i: x[None] for i, x in enumerate(parts)}
        for b in range(log2_of(grp_size)):
            bit = (grp >> b) % 2
            merged = {}
            for i in range(len(stacks) // 2):
                low, high = stacks[2 * i], stacks[2 * i + 1]
                merged[i] = jnp.where(bit == 0, jnp.concatenate([low, high]), jnp.concatenate([high, low]))
            stacks = merged
        return stacks[0].reshape((-1,) + parts[0].shape[1:])

    smalls = jnp.concatenate(
        [query_bias, value_bias, output_bias, first_gain, first_shift, outer_bias, second_gain, second_shift, inner_bias]
    )
    small_rows = 32 - shard if shard == 24 else 8
    grouped = jnp.stack([query_weight, key_weight, value_weight]).reshape(3, shard, HEAD_GROUPS, GROUP_WIDTH)
    grouped = grouped.transpose(2, 1, 0, 3).reshape(HEAD_GROUPS, shard, 3 * GROUP_WIDTH)
    small_block = jnp.zeros((small_rows * 3 * GROUP_WIDTH,), bf16).at[: smalls.shape[0]].set(smalls)
    small_block = jnp.broadcast_to(small_block.reshape(1, small_rows, -1), (HEAD_GROUPS, small_rows, 3 * GROUP_WIDTH))
    grouped = jnp.concatenate([grouped, small_block], axis=1)
    grouped, _ = lax.optimization_barrier((grouped, x_theirs))

    def group_block(k):
        return lax.dynamic_index_in_dim(grouped, head_group ^ k, 0, keepdims=False)

    w0 = group_block(0)
    w1 = sflip(group_block(1), YO)
    w2 = sflip(group_block(2), ZO)
    w3 = sflip(group_block(3), ZO | YO)
    w_all = in_order(in_order(w0, w1, y0), in_order(w2, w3, y0), z0)
    w_all = in_order(w_all, sflip(w_all, HI), z1)
    names = ["z1", "z0", "y0"]
    for b in extra_bits:
        w_all = in_order(w_all, sflip(w_all, b), (me // b) % 2)
        names = ["e%d" % b] + names
    for b in range(log2_of(grp_size)):
        w_all = in_order(w_all, flip(w_all, "grp", grp_size, 1 << b), (grp >> b) % 2)
        names = ["g%d" % b] + names
    w_all = in_order(w_all, sflip(w_all, 1), me % 2)
    names = ["c"] + names
    wanted = ["g%d" % b for b in reversed(range(log2_of(grp_size)))] + ["z1", "z0"]
    wanted += ["e%d" % b for b in reversed(extra_bits)] + ["y0", "c"]
    n = len(names)
    w_all = w_all.transpose(*[names.index(w) for w in wanted], n, n + 1)
    w_all = w_all.reshape(grp_size * seq_size, shard + small_rows, 3 * GROUP_WIDTH)
    small_all = w_all[:, shard:].reshape(grp_size * seq_size, -1)[:, : smalls.shape[0]]
    vectors = [small_all[:, i * shard : (i + 1) * shard].reshape(-1).astype(jnp.float32) for i in range(8)]
    q_bias, v_bias, o_bias, gain1, shift1, out_bias, gain2, shift2 = vectors
    in_bias = small_all[:, 8 * shard :].reshape(-1).astype(jnp.float32)
    w_all = w_all[:, :shard].reshape(width, 3 * GROUP_WIDTH)

    def own_columns(vector):
        return lax.dynamic_slice_in_dim(vector, head_group * GROUP_WIDTH, GROUP_WIDTH)

    qkv_bias = jnp.concatenate([own_columns(q_bias), jnp.zeros((GROUP_WIDTH,), jnp.float32), own_columns(v_bias)])
    qkv = dot(x_all, w_all) + qkv_bias
    queries = (qkv[:, :GROUP_WIDTH] * score_scale).astype(bf16)
    kv = qkv[:, GROUP_WIDTH:].astype(bf16)[None]
    for b in part_bits:
        bit = (me // b) % 2
        theirs = sflip(kv, b)
        kv = jnp.where(bit == 0, jnp.concatenate([kv, theirs]), jnp.concatenate([theirs, kv]))
    kv = kv.reshape(-1, 2 * GROUP_WIDTH)

    part = jnp.arange(n_parts, dtype=jnp.int32)
    part_device = part % 2 + 4 * (part // 2)
    member = jnp.arange(8, dtype=jnp.int32)
    member_device = (member // 4) * HI + ((member // 2) % 2) * ZO + (member % 2) * YO
    device = part_device[:, None] + member_device[None, :]
    position = (device[:, :, None] * rows + jnp.arange(rows, dtype=jnp.int32)).reshape(-1)
    bias = jnp.where(position < pick(valid_len, z1), 0.0, masked_score)[:, None]
    lane = jnp.arange(128, dtype=jnp.int32)[None, :]
    key_tail = jnp.where(lane == HEAD, bias, jnp.where((lane > HEAD) & (lane < HEAD + 4), 1.0, 0.0)).astype(bf16)

    context, context_full, stats = attend_forward(queries, kv, key_tail)

    teams = [
        [a * HI + b * ZO + c * YO + q for a in range(2) for b in range(2) for c in range(2)]
        for q in [i % 2 + 4 * (i // 2) for i in range(n_parts)]
    ]

    def exchange(blocks):
        return lax.all_to_all(blocks, "seq", 0, 0, axis_index_groups=teams, tiled=True)

    context = exchange(context.reshape(8, rows, GROUP_WIDTH))
    context = context.reshape(2, HEAD_GROUPS, rows, GROUP_WIDTH).transpose(0, 2, 1, 3).reshape(2 * rows, width)

    inner_lo = gathered_rows(0, 0, 2 * shard).reshape(width, width)
    inner_hi = gathered_rows(0, 2 * shard, 4 * shard).reshape(width, width)
    output_all = gathered_rows(0, 4 * shard, first_end).reshape(width, width)
    outer_all = gathered_rows(1, 0, outer_weight.shape[0])
    outer_all = outer_all.reshape(-1, 2, grp_size // 2, outer_weight.shape[0], width)
    outer_all = outer_all.transpose(0, 2, 1, 3, 4).reshape(half_feed, width)

    in_bias = pick(in_bias.reshape(chips, 2, piece).transpose(1, 0, 2).reshape(2, half_feed), core)

    home = tokens.reshape(2 * rows, width)
    cotangent = grad_out.reshape(2 * rows, width)
    hidden_one = home.astype(jnp.float32) + dot(context, output_all) + o_bias
    norm_one, norm_back_one = jax.vjp(layer_norm, hidden_one, gain1, shift1)
    first_out = norm_one.astype(bf16)
    n_own = 2 * rows
    both_first = jnp.concatenate([first_out, sflip(first_out, 1)], axis=0)

    def gelu_pair(pre):
        full, back = jax.vjp(partial(jax.nn.gelu, approximate=False), pre)
        return full.astype(bf16), back(jnp.ones_like(pre))[0]

    inner_all = jnp.concatenate([inner_lo, inner_hi], axis=1)
    active, slope = gelu_pair(dot(both_first, inner_all) + in_bias)
    outer_part = dot(active, outer_all)
    outer_sum = outer_part[:n_own] + sflip(outer_part[n_own:].astype(bf16), 1).astype(jnp.float32)
    hidden_two = first_out.astype(jnp.float32) + outer_sum + out_bias
    layer_out, norm_back_two = jax.vjp(layer_norm, hidden_two, gain2, shift2)
    dhidden_two, dsecond_gain, dsecond_shift = norm_back_two(cotangent.astype(jnp.float32))
    douter = dhidden_two.astype(bf16)
    both_douter = jnp.concatenate([douter, sflip(douter, 1)], axis=0)

    def over_chips(blocks):
        return lax.psum_scatter(blocks, "seq", scatter_dimension=0, tiled=False, axis_index_groups=chip_groups)

    def over_groups(blocks):
        for b in range(log2_of(grp_size)):
            blocks = (blocks.astype(jnp.float32) + flip(blocks, "grp", grp_size, 1 << b).astype(jnp.float32)).astype(bf16)
        return blocks

    dinner = (dot_t(both_douter, outer_all) * slope).astype(bf16)
    dfirst_part = dot_t(dinner, inner_all)
    dfirst = dhidden_two + dfirst_part[:n_own] + sflip(dfirst_part[n_own:].astype(bf16), 1).astype(jnp.float32)
    dhidden_one, dfirst_gain, dfirst_shift = norm_back_one(dfirst)
    dattend = dhidden_one.astype(bf16)
    dcontext = dot_t(dattend, output_all).astype(bf16)
    dcontext = dcontext.reshape(2, rows, HEAD_GROUPS, GROUP_WIDTH).transpose(0, 2, 1, 3)
    dcontext = exchange(dcontext.reshape(8, rows, GROUP_WIDTH)).reshape(8 * rows, GROUP_WIDTH)

    out_rows = width // seq_size
    ctx_split = context.reshape(n_own, chips, 2, out_rows)
    ctx_split = [ctx_split[:, :, i].reshape(n_own, width // 2) for i in range(2)]
    both_ctx = jnp.concatenate([pick(ctx_split, core), sflip(pick(ctx_split, 1 - core), 1)], axis=0)
    both_dattend = jnp.concatenate([dattend, sflip(dattend, 1)], axis=0)
    vectors = jnp.stack([dfirst_gain, dfirst_shift, dsecond_gain, dsecond_shift])
    grads = weight_grads(both_first, dinner, active, both_douter, both_ctx, both_dattend, vectors, chips)
    grads, dcontext = lax.optimization_barrier((grads, dcontext))
    grads = over_chips(grads)

    last = part_bits[-1]
    dqueries, sent, kept = attend_backward(
        queries, kv, key_tail, context_full, stats, dcontext, ((me // last) % 2).astype(jnp.int32).reshape(1)
    )
    dkv = (kept + sflip(sent, last).astype(jnp.float32)).reshape(n_parts // 2, 8 * rows, 2 * GROUP_WIDTH)
    for b in reversed(part_bits[:-1]):
        bit = (me // b) % 2
        n_now = dkv.shape[0] // 2
        low, high = dkv[:n_now], dkv[n_now:]
        sent = jnp.where(bit == 0, high, low).astype(bf16)
        dkv = jnp.where(bit == 0, low, high) + sflip(sent, b).astype(jnp.float32)
    dqkv = jnp.concatenate([dqueries, dkv[0].astype(bf16)], axis=1)

    dx = dot_t(dqkv, w_all).reshape(2, 2, 2, rows, width)
    da, db = dx[..., :half_width], dx[..., half_width:]

    def halve(low, high, bit, mask):
        sent = jnp.where(bit == 0, high, low).astype(bf16)
        return jnp.where(bit == 0, low, high) + sflip(sent, mask).astype(jnp.float32)

    da = halve(da[:, :, 0], da[:, :, 1], y0, YO)
    db = halve(db[:, 0], db[:, 1], z0, ZO)
    da = halve(da[:, 0], da[:, 1], z0, ZO)
    db = halve(db[:, 0], db[:, 1], y0, YO)
    dx = jnp.concatenate([da, db], axis=-1)
    mine = pick(dx, z1)
    theirs = sflip(pick(dx, 1 - z1).astype(bf16), HI).astype(jnp.float32)
    dtokens = dhidden_one.reshape(2, rows, width) + in_order(mine, theirs, z1)

    grads = over_groups(grads)
    r1 = 4 * out_rows
    r2 = r1 + piece
    r3 = r2 + out_rows
    inner_grad = grads[:r1].reshape(2, 2, out_rows, width)
    inner_grad = [inner_grad[:, i] for i in range(2)]
    far = sflip(jnp.concatenate([pick(inner_grad, 1 - core).reshape(2 * out_rows, width), grads[r3 : r3 + 8]], axis=0), 1)
    dinner_weight = in_order(pick(inner_grad, core), far[: 2 * out_rows].reshape(2, out_rows, width), core)
    dinner_weight = dinner_weight.transpose(2, 0, 1, 3).reshape(out_rows, 2, chips, piece).transpose(0, 2, 1, 3)
    dinner_weight = dinner_weight.reshape(out_rows, feed).astype(jnp.float32)
    douter_weight = grads[r1:r2].astype(jnp.float32)
    doutput_weight = grads[r2:r3].astype(jnp.float32)
    small = grads[r3 : r3 + 8].astype(jnp.float32)
    both = lax.dynamic_slice_in_dim(small + far[2 * out_rows :].astype(jnp.float32), me * out_rows, out_rows, axis=1)
    dfirst_gain, dfirst_shift, dsecond_gain, dsecond_shift, doutput_bias, douter_bias = (both[i] for i in range(6))
    dinner_bias = lax.dynamic_slice_in_dim(small[6:8].reshape(half_feed), (me // 2) * piece, piece)

    dw = t_dot(x_all, dqkv)
    dbias = column_sums(dqkv)
    dw = dw.reshape(seq_size, out_rows, 3 * GROUP_WIDTH)
    dw = jnp.concatenate([dw, jnp.broadcast_to(dbias, (seq_size, 8, 3 * GROUP_WIDTH))], axis=1)
    block = dw.shape[1]
    n_extra = 1 << len(extra_bits)
    dw = dw.reshape(2, 2, 2, n_extra, 2, 1, block, 3 * GROUP_WIDTH)[:, :, :, :, :, 0]
    dw = dw.reshape(2, 2, n_extra, 2, 2, block, 3 * GROUP_WIDTH)
    dw = halve(dw[:, :, :, :, 0], dw[:, :, :, :, 1], me % 2, 1)
    for b in reversed(extra_bits):
        m = dw.shape[2] // 2
        dw = halve(dw[:, :, :m], dw[:, :, m:], (me // b) % 2, b)
    dw = dw[:, :, 0]
    dw = halve(dw[0], dw[1], z1, HI)
    for b in range(log2_of(grp_size)):
        dw = dw + flip(dw.astype(bf16), "grp", grp_size, 1 << b).astype(jnp.float32)
    dw = dw.astype(bf16).reshape(HEAD_GROUPS, block, 3 * GROUP_WIDTH)

    def row_block(k):
        return lax.dynamic_index_in_dim(dw, head_group ^ k, 0, keepdims=False)

    w0 = row_block(0)
    w1 = sflip(row_block(1), YO)
    w2 = sflip(row_block(2), ZO)
    w3 = sflip(row_block(3), ZO | YO)
    dw = in_order(in_order(w0, w1, y0), in_order(w2, w3, y0), z0).reshape(HEAD_GROUPS, block, 3, GROUP_WIDTH)
    dw = dw.astype(jnp.float32).transpose(2, 1, 0, 3).reshape(3, block, width)
    dquery_weight, dkey_weight, dvalue_weight = dw[0, :out_rows], dw[1, :out_rows], dw[2, :out_rows]
    dquery_bias = lax.dynamic_slice_in_dim(dw[0, out_rows], me * out_rows, out_rows)
    dvalue_bias = lax.dynamic_slice_in_dim(dw[2, out_rows], me * out_rows, out_rows)

    return (
        layer_out.astype(bf16).reshape(2, rows, width),
        dtokens.astype(bf16),
        dquery_weight,
        dquery_bias,
        dkey_weight,
        dvalue_weight,
        dvalue_bias,
        doutput_weight,
        doutput_bias,
        dfirst_gain,
        dfirst_shift,
        dinner_weight,
        dinner_bias,
        douter_weight,
        douter_bias,
        dsecond_gain,
        dsecond_shift,
    )


def solution(mesh):
    in_specs = (
        P("grp", "seq", None),
        P("grp"),
        P(("grp", "seq"), None),
        P(("grp", "seq")),
        P(("grp", "seq"), None),
        P(("grp", "seq"), None),
        P(("grp", "seq")),
        P(("grp", "seq"), None),
        P(("grp", "seq")),
        P(("grp", "seq")),
        P(("grp", "seq")),
        P(("grp", "seq"), None),
        P(("grp", "seq")),
        P(("grp", "seq"), None),
        P(("grp", "seq")),
        P(("grp", "seq")),
        P(("grp", "seq")),
        P("grp", "seq", None),
    )
    out_specs = (
        P("grp", "seq", None),
        P("grp", "seq", None),
        P("seq", None),
        P("seq"),
        P("seq", None),
        P("seq", None),
        P("seq"),
        P("seq", None),
        P("seq"),
        P("seq"),
        P("seq"),
        P("seq", None),
        P("seq"),
        P("seq", None),
        P("seq"),
        P("seq"),
        P("seq"),
    )
    body = partial(per_device, mesh.shape["seq"], mesh.shape["grp"])
    return jax.shard_map(
        body, mesh=mesh, in_specs=in_specs, out_specs=out_specs, check_vma=False
    )
```

```python
from functools import partial

import jax
import jax.numpy as jnp
from jax import lax
from jax.experimental import pallas as pl
from jax.experimental.pallas import tpu as pltpu
from jax.sharding import PartitionSpec as P

HEADS = 12
HEAD = 64
HEAD_GROUPS = 4
GROUP_WIDTH = HEADS * HEAD // HEAD_GROUPS
NH = HEADS // HEAD_GROUPS
BF16 = jnp.bfloat16
F32 = jnp.float32

score_scale = 0.125
epsilon = 1e-12
masked_score = -1e30


def log2_of(size):
    return size.bit_length() - 1


def flip(value, axis, size, mask):
    return lax.ppermute(value, axis, [(i, i ^ mask) for i in range(size)])


def in_order(mine, theirs, bit):
    return jnp.where(bit == 0, jnp.stack([mine, theirs]), jnp.stack([theirs, mine]))


def pick(pair, bit):
    return jnp.where(bit == 0, pair[0], pair[1])


def layer_norm(hidden, norm_gain, norm_shift):
    centred = hidden - jnp.mean(hidden, axis=-1, keepdims=True)
    spread = jnp.mean(centred * centred, axis=-1, keepdims=True)
    return centred * lax.rsqrt(spread + epsilon) * norm_gain + norm_shift


def dot(left, right):
    return jnp.dot(left, right, preferred_element_type=jnp.float32)


def dot_t(left, right):
    return lax.dot_general(left, right, (((1,), (1,)), ((), ())), preferred_element_type=jnp.float32)


def t_dot(left, right):
    return lax.dot_general(left, right, (((0,), (0,)), ((), ())), preferred_element_type=jnp.float32)


def column_sums(matrix):
    return jnp.sum(matrix.astype(jnp.float32), axis=0)


def thirds(x):
    hi=x.astype(BF16)
    r=x-hi.astype(F32)
    mid=r.astype(BF16)
    lo=(r-mid.astype(F32)).astype(BF16)
    return hi,mid,lo

def fwd_body(q_ref, kv_ref, kb_ref, c_ref, cf_ref, st_ref, kt, va, oacc, lacc, *, bq):
    i=pl.program_id(0); h=pl.program_id(1)
    W=NH*HEAD
    @pl.when((i==0)&(h==0))
    def _():
        tail=kb_ref[:,HEAD:]
        for g in range(NH):
            ka=jnp.concatenate([kv_ref[:,g*HEAD:(g+1)*HEAD],tail],axis=1)
            kt[g]=ka.T
            va[g]=jnp.concatenate([kv_ref[:,W+g*HEAD:W+(g+1)*HEAD],tail],axis=1)
    one=jnp.where(lax.broadcasted_iota(jnp.int32,(bq,HEAD),1)==0,1.0,0.0).astype(BF16)
    def head(g):
        qa=jnp.concatenate([q_ref[:,g*HEAD:(g+1)*HEAD],one],axis=1)
        s=dot(qa,kt[g])
        m=jnp.max(s,axis=1,keepdims=True)
        p=jnp.exp(s-m).astype(BF16)
        o=dot(p,va[g])
        l=o[:,HEAD+1:HEAD+2]
        oacc[g]=o/l
        lacc[g]=jnp.broadcast_to(m+jnp.log(l),(bq,128))
    for g in range(NH):
        @pl.when(h==g)
        def _(): head(g)
    @pl.when(h==NH-1)
    def _():
        c=jnp.concatenate([oacc[g][:,:HEAD] for g in range(NH)],axis=1)
        c_ref[...]=c.astype(BF16)
        cf_ref[...]=c
        lane=lax.broadcasted_iota(jnp.int32,(bq,128),1)
        st=lacc[0]
        for g in range(1,NH): st=jnp.where(lane==g,lacc[g],st)
        st_ref[...]=st

def attend_forward(q,kv,kb,bq=256):
    n,W=q.shape; L=kv.shape[0]
    return pl.pallas_call(partial(fwd_body,bq=bq),
        grid=(n//bq,NH),
        in_specs=[pl.BlockSpec((bq,W),lambda i,h:(i,0)),pl.BlockSpec((L,2*W),lambda i,h:(0,0)),pl.BlockSpec((L,128),lambda i,h:(0,0))],
        out_specs=[pl.BlockSpec((bq,W),lambda i,h:(i,0)),pl.BlockSpec((bq,W),lambda i,h:(i,0)),pl.BlockSpec((bq,128),lambda i,h:(i,0))],
        out_shape=[jax.ShapeDtypeStruct((n,W),BF16),jax.ShapeDtypeStruct((n,W),F32),jax.ShapeDtypeStruct((n,128),F32)],
        scratch_shapes=[pltpu.VMEM((NH,128,L),BF16),pltpu.VMEM((NH,L,128),BF16),pltpu.VMEM((NH,bq,128),F32),pltpu.VMEM((NH,bq,128),F32)],
        cost_estimate=pl.CostEstimate(flops=16*n*L*W, transcendentals=NH*n*L, bytes_accessed=4*n*L),
        name="attend_forward",
    )(q,kv,kb)

def bwd_body(bit_ref, q_ref, kv_ref, kb_ref, cf_ref, st_ref, dc_ref, dq_ref, sent_ref, kept_ref, qt, qn, dct, dcn, dqt, dk, dv, *, nk):
    j=pl.program_id(0); h=pl.program_id(1)
    W=NH*HEAD
    n=q_ref.shape[0]
    @pl.when((j==0)&(h==0))
    def _():
        pad=jnp.zeros((n,256-W),BF16)
        row=lax.broadcasted_iota(jnp.int32,(16,n),0)
        lane=lax.broadcasted_iota(jnp.int32,(8,W),1)
        head_row=lax.broadcasted_iota(jnp.int32,(8,W),0)
        pick=jnp.where((lane>=head_row*HEAD)&(lane<head_row*HEAD+HEAD),1.0,0.0).astype(BF16)
        prod=dc_ref[...].astype(F32)*cf_ref[...]
        hi,mid,lo=thirds(prod)
        deltas=dot_t(pick,hi)+dot_t(pick,mid)+dot_t(pick,lo)
        stats=st_ref[...].T
        q_t=jnp.concatenate([q_ref[...],pad],axis=1).T
        d_t=jnp.concatenate([dc_ref[...],pad],axis=1).T
        def tail(x,first):
            hi,mid,lo=(v.astype(F32) for v in thirds(-x))
            z=jnp.where(row==1,hi,jnp.where(row==2,mid,jnp.where(row==3,lo,0.0)))
            return jnp.where(row==0,first,z).astype(BF16)
        rest=jnp.zeros((HEAD-16,n),BF16)
        for g in range(NH):
            cols=slice(g*HEAD,(g+1)*HEAD)
            for t,x,first,dst in ((q_t,stats,1.0,qt),(d_t,deltas,0.0,dct)):
                dst[g,:HEAD]=t[cols]
                dst[g,HEAD:HEAD+16]=tail(x[g:g+1],first)
                dst[g,HEAD+16:]=rest
            qn[g]=q_ref[:,cols]
            dcn[g]=dc_ref[:,cols]
        dqt[...]=jnp.zeros_like(dqt)
    key_tail=kb_ref[:,HEAD:]
    def head(g):
        k=kv_ref[:,g*HEAD:(g+1)*HEAD]
        ka=jnp.concatenate([k,key_tail],axis=1)
        va=jnp.concatenate([kv_ref[:,W+g*HEAD:W+(g+1)*HEAD],key_tail],axis=1)
        p=jnp.exp(dot(ka,qt[g]))
        dp=dot(va,dct[g])
        ds=(p*dp).astype(BF16)
        dv[g]=dot(p.astype(BF16),dcn[g])
        dk[g]=dot(ds,qn[g])
        dqt[g]=dqt[g]+t_dot(ka,ds)[:HEAD]
    for g in range(NH):
        @pl.when(h==g)
        def _(): head(g)
    @pl.when(h==NH-1)
    def _():
        dkv=jnp.concatenate([dk[g] for g in range(NH)]+[dv[g] for g in range(NH)],axis=1)
        @pl.when(j<nk//2)
        def _():
            sent_ref[...]=dkv.astype(BF16)
        @pl.when(j>=nk//2)
        def _():
            kept_ref[...]=dkv
    @pl.when((h==NH-1)&(j==nk-1))
    def _():
        for g in range(NH):
            dq_ref[:,g*HEAD:(g+1)*HEAD]=(dqt[g].T*0.125).astype(BF16)

def attend_backward(q,kv,kb,cf,st,dc,bit,bk=768):
    n,W=q.shape; L=kv.shape[0]; nk=L//bk; half=nk//2
    full=lambda a: pl.BlockSpec(a.shape,lambda j,h,b:(0,0))
    key=lambda j,h,b:(jnp.where(j<half,(1-b[0])*half+j,b[0]*half+j-half),0)
    return pl.pallas_call(partial(bwd_body,nk=nk),
        grid_spec=pltpu.PrefetchScalarGridSpec(
            num_scalar_prefetch=1,
            grid=(nk,NH),
            in_specs=[full(q),pl.BlockSpec((bk,2*W),key),pl.BlockSpec((bk,128),key),full(cf),full(st),full(dc)],
            out_specs=[pl.BlockSpec((n,W),lambda j,h,b:(0,0)),
                pl.BlockSpec((bk,2*W),lambda j,h,b:(jnp.minimum(j,half-1),0)),
                pl.BlockSpec((bk,2*W),lambda j,h,b:(jnp.maximum(j-half,0),0))],
            scratch_shapes=[pltpu.VMEM((NH,2*HEAD,n),BF16),pltpu.VMEM((NH,n,HEAD),BF16),pltpu.VMEM((NH,2*HEAD,n),BF16),pltpu.VMEM((NH,n,HEAD),BF16),
                pltpu.VMEM((NH,HEAD,n),F32),pltpu.VMEM((NH,bk,HEAD),F32),pltpu.VMEM((NH,bk,HEAD),F32)]),
        out_shape=[jax.ShapeDtypeStruct((n,W),BF16),jax.ShapeDtypeStruct((L//2,2*W),BF16),jax.ShapeDtypeStruct((L//2,2*W),F32)],
        name="attend_backward",
    )(bit,q,kv,kb,cf,st,dc)


def feed_grads_body(y_ref, dz_ref, a_ref, do_ref, out_ref, *, chips):
    width = y_ref.shape[1]
    r_in, r_out = width // chips, a_ref.shape[1] // chips
    half = chips // 2
    for j in range(2):
        grad = t_dot(y_ref[...], dz_ref[:, j * width : (j + 1) * width]).astype(BF16)
        for q in range(chips):
            out_ref[q, j * r_in : (j + 1) * r_in] = grad[q * r_in : (q + 1) * r_in]
        grad = t_dot(a_ref[:, j * width : (j + 1) * width], do_ref[...]).astype(BF16)
        for q in range(half):
            out_ref[j * half + q, 2 * r_in :] = grad[q * r_out : (q + 1) * r_out]


def feed_grads(y, dz, a, do, chips):
    width = y.shape[1]
    return pl.pallas_call(
        partial(feed_grads_body, chips=chips),
        out_shape=jax.ShapeDtypeStruct((chips, (2 * width + a.shape[1]) // chips, width), BF16),
        cost_estimate=pl.CostEstimate(
            flops=4 * width * y.shape[0] * dz.shape[1], transcendentals=0, bytes_accessed=10 * width * width * 2
        ),
        name="feed_grads",
    )(y, dz, a, do)


def other_grads_body(dz_ref, ctx_ref, da_ref, do_ref, vec_ref, out_ref, *, chips):
    width = da_ref.shape[1]
    r_ctx = ctx_ref.shape[1] // chips
    grad = t_dot(ctx_ref[...], da_ref[...]).astype(BF16)
    n = do_ref.shape[0]
    ones = jnp.ones((16, da_ref.shape[0]), BF16)
    sums = [dot(ones[:, :n], da_ref[:n])[:1], dot(ones[:, :n], do_ref[...])[:1]]
    sums += [dot(ones, dz_ref[:, j * width : (j + 1) * width])[:1] for j in range(2)]
    small = jnp.concatenate([vec_ref[...]] + sums, axis=0).astype(BF16)
    for q in range(chips):
        out_ref[q, :r_ctx] = grad[q * r_ctx : (q + 1) * r_ctx]
        out_ref[q, r_ctx:] = small


def other_grads(dz, ctx, da, do, vec, chips):
    width = da.shape[1]
    return pl.pallas_call(
        partial(other_grads_body, chips=chips),
        out_shape=jax.ShapeDtypeStruct((chips, ctx.shape[1] // chips + vec.shape[0] + 4, width), BF16),
        cost_estimate=pl.CostEstimate(
            flops=2 * width * ctx.shape[0] * ctx.shape[1], transcendentals=0, bytes_accessed=5 * width * width * 2
        ),
        name="other_grads",
    )(dz, ctx, da, do, vec)


def per_device(
    seq_size,
    grp_size,
    tokens,
    valid_len,
    query_weight,
    query_bias,
    key_weight,
    value_weight,
    value_bias,
    output_weight,
    output_bias,
    first_gain,
    first_shift,
    inner_weight,
    inner_bias,
    outer_weight,
    outer_bias,
    second_gain,
    second_shift,
    grad_out,
):
    bf16 = jnp.bfloat16
    rows, width = tokens.shape[1:]
    feed = inner_weight.shape[1]
    shard = query_weight.shape[0]
    HI, ZO, YO = seq_size // 2, seq_size // 4, 2
    extra_bits = [1 << b for b in range(2, log2_of(ZO))]
    part_bits = [1] + extra_bits
    me = lax.axis_index("seq")
    grp = lax.axis_index("grp")
    z1 = me // HI
    z0 = (me // ZO) % 2
    y0 = (me // YO) % 2
    head_group = 2 * z0 + y0
    my_part = me % 2 + 2 * ((me // 4) % max(ZO // 4, 1))
    n_parts = seq_size // 8

    def sflip(value, mask):
        return flip(value, "seq", seq_size, mask)

    chips = seq_size // 2
    x_mine = pick(tokens, z1)
    x_sent = pick(tokens, 1 - z1)
    half_width = width // 2
    x_theirs = sflip(x_sent, HI)
    x_pair = in_order(x_mine, x_theirs, z1)
    xa, xb = x_pair[:, :, :half_width], x_pair[:, :, half_width:]
    ra, rb = sflip(xa, YO), sflip(xb, ZO)
    xa, xb = in_order(xa, ra, y0), in_order(xb, rb, z0)
    ra, rb = sflip(xa, ZO), sflip(xb, YO)
    xa, xb = in_order(xa, ra, z0), in_order(xb, rb, y0)
    x_all = jnp.concatenate([xa.transpose(2, 0, 1, 3, 4), xb.transpose(2, 1, 0, 3, 4)], axis=-1)
    x_all = x_all.reshape(8 * rows, width)

    core = me % 2
    chips = seq_size // 2
    piece = feed // seq_size
    n_dev = grp_size * seq_size
    half_feed = feed // 2
    split = inner_weight.reshape(shard, chips, 2, piece)
    split = [split[:, :, i].reshape(shard, 2, width).transpose(1, 0, 2).reshape(2 * shard, width) for i in range(2)]
    near = jnp.concatenate([pick(split, 1 - core), output_weight], axis=0)
    far = sflip(near, 1)
    outer_far = lax.ppermute(
        outer_weight,
        ("grp", "seq"),
        [(d, d ^ (1 | grp_size) if d % 2 != (d // grp_size) % 2 else d) for d in range(n_dev)],
    )
    inner_pair = in_order(pick(split, core).reshape(2, shard, width), far[: 2 * shard].reshape(2, shard, width), core)
    packed = jnp.concatenate(
        [
            inner_pair.transpose(1, 0, 2, 3).reshape(4 * shard, width),
            in_order(output_weight, far[2 * shard :], core).reshape(2 * shard, width),
            outer_far,
        ],
        axis=0,
    )
    chip_groups = [[2 * q + i for q in range(chips)] for i in range(2)]
    gathered = lax.all_gather(packed, "seq", axis=0, tiled=False, axis_index_groups=chip_groups)
    first_end = 6 * shard
    gathered = [gathered]
    for b in range(log2_of(grp_size)):
        gathered += [flip(part, "grp", grp_size, 1 << b) for part in gathered]

    def gathered_rows(start, stop):
        parts = [x[:, start:stop] for x in gathered]
        stacks = {i: x[None] for i, x in enumerate(parts)}
        for b in range(log2_of(grp_size)):
            bit = (grp >> b) % 2
            merged = {}
            for i in range(len(stacks) // 2):
                low, high = stacks[2 * i], stacks[2 * i + 1]
                merged[i] = jnp.where(bit == 0, jnp.concatenate([low, high]), jnp.concatenate([high, low]))
            stacks = merged
        return stacks[0].reshape((-1,) + parts[0].shape[1:])

    smalls = jnp.concatenate(
        [query_bias, value_bias, output_bias, first_gain, first_shift, outer_bias, second_gain, second_shift, inner_bias]
    )
    small_rows = 32 - shard if shard == 24 else 8
    grouped = jnp.stack([query_weight, key_weight, value_weight]).reshape(3, shard, HEAD_GROUPS, GROUP_WIDTH)
    grouped = grouped.transpose(2, 1, 0, 3).reshape(HEAD_GROUPS, shard, 3 * GROUP_WIDTH)
    small_block = jnp.zeros((small_rows * 3 * GROUP_WIDTH,), bf16).at[: smalls.shape[0]].set(smalls)
    small_block = jnp.broadcast_to(small_block.reshape(1, small_rows, -1), (HEAD_GROUPS, small_rows, 3 * GROUP_WIDTH))
    grouped = jnp.concatenate([grouped, small_block], axis=1)
    grouped, _ = lax.optimization_barrier((grouped, x_theirs))

    def group_block(k):
        return lax.dynamic_index_in_dim(grouped, head_group ^ k, 0, keepdims=False)

    w0 = group_block(0)
    w1 = sflip(group_block(1), YO)
    w2 = sflip(group_block(2), ZO)
    w3 = sflip(group_block(3), ZO | YO)
    w_all = in_order(in_order(w0, w1, y0), in_order(w2, w3, y0), z0)
    w_all = in_order(w_all, sflip(w_all, HI), z1)
    names = ["z1", "z0", "y0"]
    for b in extra_bits:
        w_all = in_order(w_all, sflip(w_all, b), (me // b) % 2)
        names = ["e%d" % b] + names
    for b in range(log2_of(grp_size)):
        w_all = in_order(w_all, flip(w_all, "grp", grp_size, 1 << b), (grp >> b) % 2)
        names = ["g%d" % b] + names
    w_all = in_order(w_all, sflip(w_all, 1), me % 2)
    names = ["c"] + names
    wanted = ["g%d" % b for b in reversed(range(log2_of(grp_size)))] + ["z1", "z0"]
    wanted += ["e%d" % b for b in reversed(extra_bits)] + ["y0", "c"]
    n = len(names)
    w_all = w_all.transpose(*[names.index(w) for w in wanted], n, n + 1)
    w_all = w_all.reshape(grp_size * seq_size, shard + small_rows, 3 * GROUP_WIDTH)
    small_all = w_all[:, shard:].reshape(grp_size * seq_size, -1)[:, : smalls.shape[0]]
    vectors = [small_all[:, i * shard : (i + 1) * shard].reshape(-1).astype(jnp.float32) for i in range(8)]
    q_bias, v_bias, o_bias, gain1, shift1, out_bias, gain2, shift2 = vectors
    in_bias = small_all[:, 8 * shard :].reshape(-1).astype(jnp.float32)
    w_all = w_all[:, :shard].reshape(width, 3 * GROUP_WIDTH)

    def own_columns(vector):
        return lax.dynamic_slice_in_dim(vector, head_group * GROUP_WIDTH, GROUP_WIDTH)

    qkv_bias = jnp.concatenate([own_columns(q_bias), jnp.zeros((GROUP_WIDTH,), jnp.float32), own_columns(v_bias)])
    qkv = dot(x_all, w_all) + qkv_bias
    queries = (qkv[:, :GROUP_WIDTH] * score_scale).astype(bf16)
    kv = qkv[:, GROUP_WIDTH:].astype(bf16)[None]
    for b in part_bits:
        bit = (me // b) % 2
        theirs = sflip(kv, b)
        kv = jnp.where(bit == 0, jnp.concatenate([kv, theirs]), jnp.concatenate([theirs, kv]))
    kv = kv.reshape(-1, 2 * GROUP_WIDTH)

    part = jnp.arange(n_parts, dtype=jnp.int32)
    part_device = part % 2 + 4 * (part // 2)
    member = jnp.arange(8, dtype=jnp.int32)
    member_device = (member // 4) * HI + ((member // 2) % 2) * ZO + (member % 2) * YO
    device = part_device[:, None] + member_device[None, :]
    position = (device[:, :, None] * rows + jnp.arange(rows, dtype=jnp.int32)).reshape(-1)
    bias = jnp.where(position < pick(valid_len, z1), 0.0, masked_score)[:, None]
    lane = jnp.arange(128, dtype=jnp.int32)[None, :]
    key_tail = jnp.where(lane == HEAD, bias, jnp.where((lane > HEAD) & (lane < HEAD + 4), 1.0, 0.0)).astype(bf16)

    context, context_full, stats = attend_forward(queries, kv, key_tail)

    teams = [
        [a * HI + b * ZO + c * YO + q for a in range(2) for b in range(2) for c in range(2)]
        for q in [i % 2 + 4 * (i // 2) for i in range(n_parts)]
    ]

    def exchange(blocks):
        return lax.all_to_all(blocks, "seq", 0, 0, axis_index_groups=teams, tiled=True)

    context = exchange(context.reshape(8, rows, GROUP_WIDTH))
    context = context.reshape(2, HEAD_GROUPS, rows, GROUP_WIDTH).transpose(0, 2, 1, 3).reshape(2 * rows, width)

    inner_lo = gathered_rows(0, 2 * shard).reshape(width, width)
    inner_hi = gathered_rows(2 * shard, 4 * shard).reshape(width, width)
    output_all = gathered_rows(4 * shard, first_end).reshape(width, width)
    outer_all = gathered_rows(first_end, first_end + outer_weight.shape[0])
    outer_all = outer_all.reshape(-1, 2, grp_size // 2, outer_weight.shape[0], width)
    outer_all = outer_all.transpose(0, 2, 1, 3, 4).reshape(half_feed, width)

    in_bias = pick(in_bias.reshape(chips, 2, piece).transpose(1, 0, 2).reshape(2, half_feed), core)

    home = tokens.reshape(2 * rows, width)
    cotangent = grad_out.reshape(2 * rows, width)
    hidden_one = home.astype(jnp.float32) + dot(context, output_all) + o_bias
    norm_one, norm_back_one = jax.vjp(layer_norm, hidden_one, gain1, shift1)
    first_out = norm_one.astype(bf16)
    n_own = 2 * rows
    both_first = jnp.concatenate([first_out, sflip(first_out, 1)], axis=0)

    def gelu_pair(pre):
        full, back = jax.vjp(partial(jax.nn.gelu, approximate=False), pre)
        return full.astype(bf16), back(jnp.ones_like(pre))[0]

    inner_all = jnp.concatenate([inner_lo, inner_hi], axis=1)
    active, slope = gelu_pair(dot(both_first, inner_all) + in_bias)
    outer_part = dot(active, outer_all)
    outer_sum = outer_part[:n_own] + sflip(outer_part[n_own:].astype(bf16), 1).astype(jnp.float32)
    hidden_two = first_out.astype(jnp.float32) + outer_sum + out_bias
    layer_out, norm_back_two = jax.vjp(layer_norm, hidden_two, gain2, shift2)
    dhidden_two, dsecond_gain, dsecond_shift = norm_back_two(cotangent.astype(jnp.float32))
    douter = dhidden_two.astype(bf16)
    both_douter = jnp.concatenate([douter, sflip(douter, 1)], axis=0)

    def over_chips(blocks):
        return lax.psum_scatter(blocks, "seq", scatter_dimension=0, tiled=False, axis_index_groups=chip_groups)

    def over_groups(blocks):
        for b in range(log2_of(grp_size)):
            blocks = (blocks.astype(jnp.float32) + flip(blocks, "grp", grp_size, 1 << b).astype(jnp.float32)).astype(bf16)
        return blocks

    dinner = (dot_t(both_douter, outer_all) * slope).astype(bf16)
    feed_blocks, dinner = lax.optimization_barrier(
        (feed_grads(both_first, dinner, active, both_douter, chips), dinner)
    )
    feed_sums = over_chips(feed_blocks)
    dfirst_part = dot_t(dinner, inner_all)
    dfirst = dhidden_two + dfirst_part[:n_own] + sflip(dfirst_part[n_own:].astype(bf16), 1).astype(jnp.float32)
    dhidden_one, dfirst_gain, dfirst_shift = norm_back_one(dfirst)
    dattend = dhidden_one.astype(bf16)
    dcontext = dot_t(dattend, output_all).astype(bf16)
    dcontext = dcontext.reshape(2, rows, HEAD_GROUPS, GROUP_WIDTH).transpose(0, 2, 1, 3)
    dcontext = exchange(dcontext.reshape(8, rows, GROUP_WIDTH)).reshape(8 * rows, GROUP_WIDTH)

    out_rows = width // seq_size
    ctx_split = context.reshape(n_own, chips, 2, out_rows)
    ctx_split = [ctx_split[:, :, i].reshape(n_own, width // 2) for i in range(2)]
    both_ctx = jnp.concatenate([pick(ctx_split, core), sflip(pick(ctx_split, 1 - core), 1)], axis=0)
    both_dattend = jnp.concatenate([dattend, sflip(dattend, 1)], axis=0)
    vectors = jnp.stack([dfirst_gain, dfirst_shift, dsecond_gain, dsecond_shift])
    other_blocks = other_grads(dinner, both_ctx, both_dattend, douter, vectors, chips)
    other_blocks, dcontext = lax.optimization_barrier((other_blocks, dcontext))

    last = part_bits[-1]
    dqueries, sent, kept = attend_backward(
        queries, kv, key_tail, context_full, stats, dcontext, ((me // last) % 2).astype(jnp.int32).reshape(1)
    )
    sent, feed_sums, other_blocks = lax.optimization_barrier((sent, feed_sums, other_blocks))
    other_sums = over_chips(other_blocks)
    dkv = (kept + sflip(sent, last).astype(jnp.float32)).reshape(n_parts // 2, 8 * rows, 2 * GROUP_WIDTH)
    for b in reversed(part_bits[:-1]):
        bit = (me // b) % 2
        n_now = dkv.shape[0] // 2
        low, high = dkv[:n_now], dkv[n_now:]
        sent = jnp.where(bit == 0, high, low).astype(bf16)
        dkv = jnp.where(bit == 0, low, high) + sflip(sent, b).astype(jnp.float32)
    dqkv = jnp.concatenate([dqueries, dkv[0].astype(bf16)], axis=1)

    dx = dot_t(dqkv, w_all).reshape(2, 2, 2, rows, width)
    da, db = dx[..., :half_width], dx[..., half_width:]

    def halve(low, high, bit, mask):
        sent = jnp.where(bit == 0, high, low).astype(bf16)
        return jnp.where(bit == 0, low, high) + sflip(sent, mask).astype(jnp.float32)

    da = halve(da[:, :, 0], da[:, :, 1], y0, YO)
    db = halve(db[:, 0], db[:, 1], z0, ZO)
    da = halve(da[:, 0], da[:, 1], z0, ZO)
    db = halve(db[:, 0], db[:, 1], y0, YO)
    dx = jnp.concatenate([da, db], axis=-1)
    dx, other_sums = lax.optimization_barrier((dx, other_sums))
    mine = pick(dx, z1)
    theirs = sflip(pick(dx, 1 - z1).astype(bf16), HI).astype(jnp.float32)
    dtokens = dhidden_one.reshape(2, rows, width) + in_order(mine, theirs, z1)

    feed_sums, other_sums = over_groups(feed_sums), over_groups(other_sums)
    r1 = 4 * out_rows
    inner_grad = feed_sums[:r1].reshape(2, 2, out_rows, width)
    inner_grad = [inner_grad[:, i] for i in range(2)]
    far = sflip(jnp.concatenate([pick(inner_grad, 1 - core).reshape(2 * out_rows, width), other_sums[out_rows:]], axis=0), 1)
    dinner_weight = in_order(pick(inner_grad, core), far[: 2 * out_rows].reshape(2, out_rows, width), core)
    dinner_weight = dinner_weight.transpose(2, 0, 1, 3).reshape(out_rows, 2, chips, piece).transpose(0, 2, 1, 3)
    dinner_weight = dinner_weight.reshape(out_rows, feed).astype(jnp.float32)
    douter_weight = feed_sums[r1:].astype(jnp.float32)
    doutput_weight = other_sums[:out_rows].astype(jnp.float32)
    small = other_sums[out_rows:].astype(jnp.float32)
    both = lax.dynamic_slice_in_dim(small + far[2 * out_rows :].astype(jnp.float32), me * out_rows, out_rows, axis=1)
    dfirst_gain, dfirst_shift, dsecond_gain, dsecond_shift, doutput_bias, douter_bias = (both[i] for i in range(6))
    dinner_bias = lax.dynamic_slice_in_dim(small[6:8].reshape(half_feed), (me // 2) * piece, piece)

    dw = t_dot(x_all, dqkv)
    dbias = column_sums(dqkv)
    dw = dw.reshape(seq_size, out_rows, 3 * GROUP_WIDTH)
    dw = jnp.concatenate([dw, jnp.broadcast_to(dbias, (seq_size, 8, 3 * GROUP_WIDTH))], axis=1)
    block = dw.shape[1]
    n_extra = 1 << len(extra_bits)
    dw = dw.reshape(2, 2, 2, n_extra, 2, 1, block, 3 * GROUP_WIDTH)[:, :, :, :, :, 0]
    dw = dw.reshape(2, 2, n_extra, 2, 2, block, 3 * GROUP_WIDTH)
    dw = halve(dw[:, :, :, :, 0], dw[:, :, :, :, 1], me % 2, 1)
    for b in reversed(extra_bits):
        m = dw.shape[2] // 2
        dw = halve(dw[:, :, :m], dw[:, :, m:], (me // b) % 2, b)
    dw = dw[:, :, 0]
    dw = halve(dw[0], dw[1], z1, HI)
    for b in range(log2_of(grp_size)):
        dw = dw + flip(dw.astype(bf16), "grp", grp_size, 1 << b).astype(jnp.float32)
    dw = dw.astype(bf16).reshape(HEAD_GROUPS, block, 3 * GROUP_WIDTH)

    def row_block(k):
        return lax.dynamic_index_in_dim(dw, head_group ^ k, 0, keepdims=False)

    w0 = row_block(0)
    w1 = sflip(row_block(1), YO)
    w2 = sflip(row_block(2), ZO)
    w3 = sflip(row_block(3), ZO | YO)
    dw = in_order(in_order(w0, w1, y0), in_order(w2, w3, y0), z0).reshape(HEAD_GROUPS, block, 3, GROUP_WIDTH)
    dw = dw.astype(jnp.float32).transpose(2, 1, 0, 3).reshape(3, block, width)
    dquery_weight, dkey_weight, dvalue_weight = dw[0, :out_rows], dw[1, :out_rows], dw[2, :out_rows]
    dquery_bias = lax.dynamic_slice_in_dim(dw[0, out_rows], me * out_rows, out_rows)
    dvalue_bias = lax.dynamic_slice_in_dim(dw[2, out_rows], me * out_rows, out_rows)

    return (
        layer_out.astype(bf16).reshape(2, rows, width),
        dtokens.astype(bf16),
        dquery_weight,
        dquery_bias,
        dkey_weight,
        dvalue_weight,
        dvalue_bias,
        doutput_weight,
        doutput_bias,
        dfirst_gain,
        dfirst_shift,
        dinner_weight,
        dinner_bias,
        douter_weight,
        douter_bias,
        dsecond_gain,
        dsecond_shift,
    )


def solution(mesh):
    in_specs = (
        P("grp", "seq", None),
        P("grp"),
        P(("grp", "seq"), None),
        P(("grp", "seq")),
        P(("grp", "seq"), None),
        P(("grp", "seq"), None),
        P(("grp", "seq")),
        P(("grp", "seq"), None),
        P(("grp", "seq")),
        P(("grp", "seq")),
        P(("grp", "seq")),
        P(("grp", "seq"), None),
        P(("grp", "seq")),
        P(("grp", "seq"), None),
        P(("grp", "seq")),
        P(("grp", "seq")),
        P(("grp", "seq")),
        P("grp", "seq", None),
    )
    out_specs = (
        P("grp", "seq", None),
        P("grp", "seq", None),
        P("seq", None),
        P("seq"),
        P("seq", None),
        P("seq", None),
        P("seq"),
        P("seq", None),
        P("seq"),
        P("seq"),
        P("seq"),
        P("seq", None),
        P("seq"),
        P("seq", None),
        P("seq"),
        P("seq"),
        P("seq"),
    )
    body = partial(per_device, mesh.shape["seq"], mesh.shape["grp"])
    return jax.shard_map(
        body, mesh=mesh, in_specs=in_specs, out_specs=out_specs, check_vma=False
    )
```

```python
from functools import partial

import jax
import jax.numpy as jnp
from jax import lax
from jax.experimental import pallas as pl
from jax.experimental.pallas import tpu as pltpu
from jax.sharding import PartitionSpec as P

HEADS = 12
HEAD = 64
HEAD_GROUPS = 4
GROUP_WIDTH = HEADS * HEAD // HEAD_GROUPS
NH = HEADS // HEAD_GROUPS
BF16 = jnp.bfloat16
F32 = jnp.float32

score_scale = 0.125
epsilon = 1e-12
masked_score = -1e30


def log2_of(size):
    return size.bit_length() - 1


def flip(value, axis, size, mask):
    return lax.ppermute(value, axis, [(i, i ^ mask) for i in range(size)])


def in_order(mine, theirs, bit):
    return jnp.where(bit == 0, jnp.stack([mine, theirs]), jnp.stack([theirs, mine]))


def pick(pair, bit):
    return jnp.where(bit == 0, pair[0], pair[1])


def layer_norm(hidden, norm_gain, norm_shift):
    centred = hidden - jnp.mean(hidden, axis=-1, keepdims=True)
    spread = jnp.mean(centred * centred, axis=-1, keepdims=True)
    return centred * lax.rsqrt(spread + epsilon) * norm_gain + norm_shift


def dot(left, right):
    return jnp.dot(left, right, preferred_element_type=jnp.float32)


def dot_t(left, right):
    return lax.dot_general(left, right, (((1,), (1,)), ((), ())), preferred_element_type=jnp.float32)


def t_dot(left, right):
    return lax.dot_general(left, right, (((0,), (0,)), ((), ())), preferred_element_type=jnp.float32)


def column_sums(matrix):
    return jnp.sum(matrix.astype(jnp.float32), axis=0)


def thirds(x):
    hi=x.astype(BF16)
    r=x-hi.astype(F32)
    mid=r.astype(BF16)
    lo=(r-mid.astype(F32)).astype(BF16)
    return hi,mid,lo

def fwd_body(q_ref, kv_ref, kb_ref, c_ref, cf_ref, st_ref, kt, va, oacc, lacc, *, bq):
    i=pl.program_id(0); h=pl.program_id(1)
    W=NH*HEAD
    @pl.when((i==0)&(h==0))
    def _():
        tail=kb_ref[:,HEAD:]
        for g in range(NH):
            ka=jnp.concatenate([kv_ref[:,g*HEAD:(g+1)*HEAD],tail],axis=1)
            kt[g]=ka.T
            va[g]=jnp.concatenate([kv_ref[:,W+g*HEAD:W+(g+1)*HEAD],tail],axis=1)
    one=jnp.where(lax.broadcasted_iota(jnp.int32,(bq,HEAD),1)==0,1.0,0.0).astype(BF16)
    def head(g):
        qa=jnp.concatenate([q_ref[:,g*HEAD:(g+1)*HEAD],one],axis=1)
        s=dot(qa,kt[g])
        m=jnp.max(s,axis=1,keepdims=True)
        p=jnp.exp(s-m).astype(BF16)
        o=dot(p,va[g])
        l=o[:,HEAD+1:HEAD+2]
        oacc[g]=o/l
        lacc[g]=jnp.broadcast_to(m+jnp.log(l),(bq,128))
    for g in range(NH):
        @pl.when(h==g)
        def _(): head(g)
    @pl.when(h==NH-1)
    def _():
        c=jnp.concatenate([oacc[g][:,:HEAD] for g in range(NH)],axis=1)
        c_ref[...]=c.astype(BF16)
        cf_ref[...]=c
        lane=lax.broadcasted_iota(jnp.int32,(bq,128),1)
        st=lacc[0]
        for g in range(1,NH): st=jnp.where(lane==g,lacc[g],st)
        st_ref[...]=st

def attend_forward(q,kv,kb,bq=256):
    n,W=q.shape; L=kv.shape[0]
    return pl.pallas_call(partial(fwd_body,bq=bq),
        grid=(n//bq,NH),
        in_specs=[pl.BlockSpec((bq,W),lambda i,h:(i,0)),pl.BlockSpec((L,2*W),lambda i,h:(0,0)),pl.BlockSpec((L,128),lambda i,h:(0,0))],
        out_specs=[pl.BlockSpec((bq,W),lambda i,h:(i,0)),pl.BlockSpec((bq,W),lambda i,h:(i,0)),pl.BlockSpec((bq,128),lambda i,h:(i,0))],
        out_shape=[jax.ShapeDtypeStruct((n,W),BF16),jax.ShapeDtypeStruct((n,W),F32),jax.ShapeDtypeStruct((n,128),F32)],
        scratch_shapes=[pltpu.VMEM((NH,128,L),BF16),pltpu.VMEM((NH,L,128),BF16),pltpu.VMEM((NH,bq,128),F32),pltpu.VMEM((NH,bq,128),F32)],
        cost_estimate=pl.CostEstimate(flops=16*n*L*W, transcendentals=NH*n*L, bytes_accessed=4*n*L),
        name="attend_forward",
    )(q,kv,kb)

def bwd_body(bit_ref, q_ref, kv_ref, kb_ref, cf_ref, st_ref, dc_ref, dq_ref, sent_ref, kept_ref, qt, qn, dct, dcn, dqt, dk, dv, *, nk):
    j=pl.program_id(0); h=pl.program_id(1)
    W=NH*HEAD
    n=q_ref.shape[0]
    @pl.when((j==0)&(h==0))
    def _():
        pad=jnp.zeros((n,256-W),BF16)
        row=lax.broadcasted_iota(jnp.int32,(16,n),0)
        lane=lax.broadcasted_iota(jnp.int32,(8,W),1)
        head_row=lax.broadcasted_iota(jnp.int32,(8,W),0)
        pick=jnp.where((lane>=head_row*HEAD)&(lane<head_row*HEAD+HEAD),1.0,0.0).astype(BF16)
        prod=dc_ref[...].astype(F32)*cf_ref[...]
        hi,mid,lo=thirds(prod)
        deltas=dot_t(pick,hi)+dot_t(pick,mid)+dot_t(pick,lo)
        stats=st_ref[...].T
        q_t=jnp.concatenate([q_ref[...],pad],axis=1).T
        d_t=jnp.concatenate([dc_ref[...],pad],axis=1).T
        def tail(x,first):
            hi,mid,lo=(v.astype(F32) for v in thirds(-x))
            z=jnp.where(row==1,hi,jnp.where(row==2,mid,jnp.where(row==3,lo,0.0)))
            return jnp.where(row==0,first,z).astype(BF16)
        rest=jnp.zeros((HEAD-16,n),BF16)
        for g in range(NH):
            cols=slice(g*HEAD,(g+1)*HEAD)
            for t,x,first,dst in ((q_t,stats,1.0,qt),(d_t,deltas,0.0,dct)):
                dst[g,:HEAD]=t[cols]
                dst[g,HEAD:HEAD+16]=tail(x[g:g+1],first)
                dst[g,HEAD+16:]=rest
            qn[g]=q_ref[:,cols]
            dcn[g]=dc_ref[:,cols]
        dqt[...]=jnp.zeros_like(dqt)
    key_tail=kb_ref[:,HEAD:]
    def head(g):
        k=kv_ref[:,g*HEAD:(g+1)*HEAD]
        ka=jnp.concatenate([k,key_tail],axis=1)
        va=jnp.concatenate([kv_ref[:,W+g*HEAD:W+(g+1)*HEAD],key_tail],axis=1)
        p=jnp.exp(dot(ka,qt[g]))
        dp=dot(va,dct[g])
        ds=(p*dp).astype(BF16)
        dv[g]=dot(p.astype(BF16),dcn[g])
        dk[g]=dot(ds,qn[g])
        dqt[g]=dqt[g]+t_dot(ka,ds)[:HEAD]
    for g in range(NH):
        @pl.when(h==g)
        def _(): head(g)
    @pl.when(h==NH-1)
    def _():
        dkv=jnp.concatenate([dk[g] for g in range(NH)]+[dv[g] for g in range(NH)],axis=1)
        @pl.when(j<nk//2)
        def _():
            sent_ref[...]=dkv.astype(BF16)
        @pl.when(j>=nk//2)
        def _():
            kept_ref[...]=dkv
    @pl.when((h==NH-1)&(j==nk-1))
    def _():
        for g in range(NH):
            dq_ref[:,g*HEAD:(g+1)*HEAD]=(dqt[g].T*0.125).astype(BF16)

def attend_backward(q,kv,kb,cf,st,dc,bit,bk=768):
    n,W=q.shape; L=kv.shape[0]; nk=L//bk; half=nk//2
    full=lambda a: pl.BlockSpec(a.shape,lambda j,h,b:(0,0))
    key=lambda j,h,b:(jnp.where(j<half,(1-b[0])*half+j,b[0]*half+j-half),0)
    return pl.pallas_call(partial(bwd_body,nk=nk),
        grid_spec=pltpu.PrefetchScalarGridSpec(
            num_scalar_prefetch=1,
            grid=(nk,NH),
            in_specs=[full(q),pl.BlockSpec((bk,2*W),key),pl.BlockSpec((bk,128),key),full(cf),full(st),full(dc)],
            out_specs=[pl.BlockSpec((n,W),lambda j,h,b:(0,0)),
                pl.BlockSpec((bk,2*W),lambda j,h,b:(jnp.minimum(j,half-1),0)),
                pl.BlockSpec((bk,2*W),lambda j,h,b:(jnp.maximum(j-half,0),0))],
            scratch_shapes=[pltpu.VMEM((NH,2*HEAD,n),BF16),pltpu.VMEM((NH,n,HEAD),BF16),pltpu.VMEM((NH,2*HEAD,n),BF16),pltpu.VMEM((NH,n,HEAD),BF16),
                pltpu.VMEM((NH,HEAD,n),F32),pltpu.VMEM((NH,bk,HEAD),F32),pltpu.VMEM((NH,bk,HEAD),F32)]),
        out_shape=[jax.ShapeDtypeStruct((n,W),BF16),jax.ShapeDtypeStruct((L//2,2*W),BF16),jax.ShapeDtypeStruct((L//2,2*W),F32)],
        name="attend_backward",
    )(bit,q,kv,kb,cf,st,dc)


def feed_grads_body(y_ref, dz_ref, a_ref, do_ref, out_ref, *, chips):
    width = y_ref.shape[1]
    r_in, r_out = width // chips, a_ref.shape[1] // chips
    half = chips // 2
    for j in range(2):
        grad = t_dot(y_ref[...], dz_ref[:, j * width : (j + 1) * width]).astype(BF16)
        for q in range(chips):
            out_ref[q, j * r_in : (j + 1) * r_in] = grad[q * r_in : (q + 1) * r_in]
        grad = t_dot(a_ref[:, j * width : (j + 1) * width], do_ref[...]).astype(BF16)
        for q in range(half):
            out_ref[j * half + q, 2 * r_in :] = grad[q * r_out : (q + 1) * r_out]


def feed_grads(y, dz, a, do, chips):
    width = y.shape[1]
    return pl.pallas_call(
        partial(feed_grads_body, chips=chips),
        out_shape=jax.ShapeDtypeStruct((chips, (2 * width + a.shape[1]) // chips, width), BF16),
        cost_estimate=pl.CostEstimate(
            flops=4 * width * y.shape[0] * dz.shape[1], transcendentals=0, bytes_accessed=10 * width * width * 2
        ),
        name="feed_grads",
    )(y, dz, a, do)


def other_grads_body(dz_ref, ctx_ref, da_ref, do_ref, vec_ref, out_ref, *, chips):
    width = da_ref.shape[1]
    r_ctx = ctx_ref.shape[1] // chips
    grad = t_dot(ctx_ref[...], da_ref[...]).astype(BF16)
    n = do_ref.shape[0]
    ones = jnp.ones((16, da_ref.shape[0]), BF16)
    sums = [dot(ones[:, :n], da_ref[:n])[:1], dot(ones[:, :n], do_ref[...])[:1]]
    sums += [dot(ones, dz_ref[:, j * width : (j + 1) * width])[:1] for j in range(2)]
    small = jnp.concatenate([vec_ref[...]] + sums, axis=0).astype(BF16)
    for q in range(chips):
        out_ref[q, :r_ctx] = grad[q * r_ctx : (q + 1) * r_ctx]
        out_ref[q, r_ctx:] = small


def other_grads(dz, ctx, da, do, vec, chips):
    width = da.shape[1]
    return pl.pallas_call(
        partial(other_grads_body, chips=chips),
        out_shape=jax.ShapeDtypeStruct((chips, ctx.shape[1] // chips + vec.shape[0] + 4, width), BF16),
        cost_estimate=pl.CostEstimate(
            flops=2 * width * ctx.shape[0] * ctx.shape[1], transcendentals=0, bytes_accessed=5 * width * width * 2
        ),
        name="other_grads",
    )(dz, ctx, da, do, vec)


def per_device(
    seq_size,
    grp_size,
    tokens,
    valid_len,
    query_weight,
    query_bias,
    key_weight,
    value_weight,
    value_bias,
    output_weight,
    output_bias,
    first_gain,
    first_shift,
    inner_weight,
    inner_bias,
    outer_weight,
    outer_bias,
    second_gain,
    second_shift,
    grad_out,
):
    bf16 = jnp.bfloat16
    rows, width = tokens.shape[1:]
    feed = inner_weight.shape[1]
    shard = query_weight.shape[0]
    HI, ZO, YO = seq_size // 2, seq_size // 4, 2
    extra_bits = [1 << b for b in range(2, log2_of(ZO))]
    part_bits = [1] + extra_bits
    me = lax.axis_index("seq")
    grp = lax.axis_index("grp")
    z1 = me // HI
    z0 = (me // ZO) % 2
    y0 = (me // YO) % 2
    head_group = 2 * z0 + y0
    my_part = me % 2 + 2 * ((me // 4) % max(ZO // 4, 1))
    n_parts = seq_size // 8

    def sflip(value, mask):
        return flip(value, "seq", seq_size, mask)

    chips = seq_size // 2
    x_mine = pick(tokens, z1)
    x_sent = pick(tokens, 1 - z1)
    half_width = width // 2
    x_theirs = sflip(x_sent, HI)
    x_pair = in_order(x_mine, x_theirs, z1)
    xa, xb = x_pair[:, :, :half_width], x_pair[:, :, half_width:]
    ra, rb = sflip(xa, YO), sflip(xb, ZO)
    xa, xb = in_order(xa, ra, y0), in_order(xb, rb, z0)
    ra, rb = sflip(xa, ZO), sflip(xb, YO)
    xa, xb = in_order(xa, ra, z0), in_order(xb, rb, y0)
    x_all = jnp.concatenate([xa.transpose(2, 0, 1, 3, 4), xb.transpose(2, 1, 0, 3, 4)], axis=-1)
    x_all = x_all.reshape(8 * rows, width)

    core = me % 2
    chips = seq_size // 2
    piece = feed // seq_size
    n_dev = grp_size * seq_size
    half_feed = feed // 2
    split = inner_weight.reshape(shard, chips, 2, piece)
    split = [split[:, :, i].reshape(shard, 2, width).transpose(1, 0, 2).reshape(2 * shard, width) for i in range(2)]
    near = jnp.concatenate([pick(split, 1 - core), output_weight], axis=0)
    far = sflip(near, 1)
    outer_far = lax.ppermute(
        outer_weight,
        ("grp", "seq"),
        [(d, d ^ (1 | grp_size) if d % 2 != (d // grp_size) % 2 else d) for d in range(n_dev)],
    )
    inner_pair = in_order(pick(split, core).reshape(2, shard, width), far[: 2 * shard].reshape(2, shard, width), core)
    packed = jnp.concatenate(
        [
            inner_pair.transpose(1, 0, 2, 3).reshape(4 * shard, width),
            in_order(output_weight, far[2 * shard :], core).reshape(2 * shard, width),
            outer_far,
        ],
        axis=0,
    )
    chip_groups = [[2 * q + i for q in range(chips)] for i in range(2)]
    gathered = lax.all_gather(packed, "seq", axis=0, tiled=False, axis_index_groups=chip_groups)
    first_end = 6 * shard
    gathered = [gathered]
    for b in range(log2_of(grp_size)):
        gathered += [flip(part, "grp", grp_size, 1 << b) for part in gathered]

    def gathered_rows(start, stop):
        parts = [x[:, start:stop] for x in gathered]
        stacks = {i: x[None] for i, x in enumerate(parts)}
        for b in range(log2_of(grp_size)):
            bit = (grp >> b) % 2
            merged = {}
            for i in range(len(stacks) // 2):
                low, high = stacks[2 * i], stacks[2 * i + 1]
                merged[i] = jnp.where(bit == 0, jnp.concatenate([low, high]), jnp.concatenate([high, low]))
            stacks = merged
        return stacks[0].reshape((-1,) + parts[0].shape[1:])

    smalls = jnp.concatenate(
        [query_bias, value_bias, output_bias, first_gain, first_shift, outer_bias, second_gain, second_shift, inner_bias]
    )
    small_rows = 32 - shard if shard == 24 else 8
    grouped = jnp.stack([query_weight, key_weight, value_weight]).reshape(3, shard, HEAD_GROUPS, GROUP_WIDTH)
    grouped = grouped.transpose(2, 1, 0, 3).reshape(HEAD_GROUPS, shard, 3 * GROUP_WIDTH)
    small_block = jnp.zeros((small_rows * 3 * GROUP_WIDTH,), bf16).at[: smalls.shape[0]].set(smalls)
    small_block = jnp.broadcast_to(small_block.reshape(1, small_rows, -1), (HEAD_GROUPS, small_rows, 3 * GROUP_WIDTH))
    grouped = jnp.concatenate([grouped, small_block], axis=1)
    grouped, _ = lax.optimization_barrier((grouped, x_theirs))

    def group_block(k):
        return lax.dynamic_index_in_dim(grouped, head_group ^ k, 0, keepdims=False)

    w0 = group_block(0)
    w1 = sflip(group_block(1), YO)
    w2 = sflip(group_block(2), ZO)
    w3 = sflip(group_block(3), ZO | YO)
    w_all = in_order(in_order(w0, w1, y0), in_order(w2, w3, y0), z0)
    w_all = in_order(w_all, sflip(w_all, HI), z1)
    names = ["z1", "z0", "y0"]
    for b in extra_bits:
        w_all = in_order(w_all, sflip(w_all, b), (me // b) % 2)
        names = ["e%d" % b] + names
    for b in range(log2_of(grp_size)):
        w_all = in_order(w_all, flip(w_all, "grp", grp_size, 1 << b), (grp >> b) % 2)
        names = ["g%d" % b] + names
    w_all = in_order(w_all, sflip(w_all, 1), me % 2)
    names = ["c"] + names
    wanted = ["g%d" % b for b in reversed(range(log2_of(grp_size)))] + ["z1", "z0"]
    wanted += ["e%d" % b for b in reversed(extra_bits)] + ["y0", "c"]
    n = len(names)
    w_all = w_all.transpose(*[names.index(w) for w in wanted], n, n + 1)
    w_all = w_all.reshape(grp_size * seq_size, shard + small_rows, 3 * GROUP_WIDTH)
    small_all = w_all[:, shard:].reshape(grp_size * seq_size, -1)[:, : smalls.shape[0]]
    vectors = [small_all[:, i * shard : (i + 1) * shard].reshape(-1).astype(jnp.float32) for i in range(8)]
    q_bias, v_bias, o_bias, gain1, shift1, out_bias, gain2, shift2 = vectors
    in_bias = small_all[:, 8 * shard :].reshape(-1).astype(jnp.float32)
    w_all = w_all[:, :shard].reshape(width, 3 * GROUP_WIDTH)

    def own_columns(vector):
        return lax.dynamic_slice_in_dim(vector, head_group * GROUP_WIDTH, GROUP_WIDTH)

    qkv_bias = jnp.concatenate([own_columns(q_bias), jnp.zeros((GROUP_WIDTH,), jnp.float32), own_columns(v_bias)])
    qkv = dot(x_all, w_all) + qkv_bias
    queries = (qkv[:, :GROUP_WIDTH] * score_scale).astype(bf16)
    kv = qkv[:, GROUP_WIDTH:].astype(bf16)[None]
    for b in part_bits:
        bit = (me // b) % 2
        theirs = sflip(kv, b)
        kv = jnp.where(bit == 0, jnp.concatenate([kv, theirs]), jnp.concatenate([theirs, kv]))
    kv = kv.reshape(-1, 2 * GROUP_WIDTH)

    part = jnp.arange(n_parts, dtype=jnp.int32)
    part_device = part % 2 + 4 * (part // 2)
    member = jnp.arange(8, dtype=jnp.int32)
    member_device = (member // 4) * HI + ((member // 2) % 2) * ZO + (member % 2) * YO
    device = part_device[:, None] + member_device[None, :]
    position = (device[:, :, None] * rows + jnp.arange(rows, dtype=jnp.int32)).reshape(-1)
    bias = jnp.where(position < pick(valid_len, z1), 0.0, masked_score)[:, None]
    lane = jnp.arange(128, dtype=jnp.int32)[None, :]
    key_tail = jnp.where(lane == HEAD, bias, jnp.where((lane > HEAD) & (lane < HEAD + 4), 1.0, 0.0)).astype(bf16)

    context, context_full, stats = attend_forward(queries, kv, key_tail)

    teams = [
        [a * HI + b * ZO + c * YO + q for a in range(2) for b in range(2) for c in range(2)]
        for q in [i % 2 + 4 * (i // 2) for i in range(n_parts)]
    ]

    def exchange(blocks):
        return lax.all_to_all(blocks, "seq", 0, 0, axis_index_groups=teams, tiled=True)

    context = exchange(context.reshape(8, rows, GROUP_WIDTH))
    context = context.reshape(2, HEAD_GROUPS, rows, GROUP_WIDTH).transpose(0, 2, 1, 3).reshape(2 * rows, width)

    inner_lo = gathered_rows(0, 2 * shard).reshape(width, width)
    inner_hi = gathered_rows(2 * shard, 4 * shard).reshape(width, width)
    output_all = gathered_rows(4 * shard, first_end).reshape(width, width)
    outer_all = gathered_rows(first_end, first_end + outer_weight.shape[0])
    outer_all = outer_all.reshape(-1, 2, grp_size // 2, outer_weight.shape[0], width)
    outer_all = outer_all.transpose(0, 2, 1, 3, 4).reshape(half_feed, width)

    in_bias = pick(in_bias.reshape(chips, 2, piece).transpose(1, 0, 2).reshape(2, half_feed), core)

    home = tokens.reshape(2 * rows, width)
    cotangent = grad_out.reshape(2 * rows, width)
    hidden_one = home.astype(jnp.float32) + dot(context, output_all) + o_bias
    norm_one, norm_back_one = jax.vjp(layer_norm, hidden_one, gain1, shift1)
    first_out = norm_one.astype(bf16)
    n_own = 2 * rows
    both_first = jnp.concatenate([first_out, sflip(first_out, 1)], axis=0)

    def gelu_pair(pre):
        full, back = jax.vjp(partial(jax.nn.gelu, approximate=False), pre)
        return full.astype(bf16), back(jnp.ones_like(pre))[0]

    inner_all = jnp.concatenate([inner_lo, inner_hi], axis=1)
    active, slope = gelu_pair(dot(both_first, inner_all) + in_bias)
    outer_part = dot(active, outer_all)
    outer_sum = outer_part[:n_own] + sflip(outer_part[n_own:].astype(bf16), 1).astype(jnp.float32)
    hidden_two = first_out.astype(jnp.float32) + outer_sum + out_bias
    layer_out, norm_back_two = jax.vjp(layer_norm, hidden_two, gain2, shift2)
    dhidden_two, dsecond_gain, dsecond_shift = norm_back_two(cotangent.astype(jnp.float32))
    douter = dhidden_two.astype(bf16)
    both_douter = jnp.concatenate([douter, sflip(douter, 1)], axis=0)

    def over_chips(blocks):
        return lax.psum_scatter(blocks, "seq", scatter_dimension=0, tiled=False, axis_index_groups=chip_groups)

    def over_groups(blocks):
        for b in range(log2_of(grp_size)):
            blocks = (blocks.astype(jnp.float32) + flip(blocks, "grp", grp_size, 1 << b).astype(jnp.float32)).astype(bf16)
        return blocks

    dinner = (dot_t(both_douter, outer_all) * slope).astype(bf16)
    dfirst_part = dot_t(dinner, inner_all)
    dfirst = dhidden_two + dfirst_part[:n_own] + sflip(dfirst_part[n_own:].astype(bf16), 1).astype(jnp.float32)
    dhidden_one, dfirst_gain, dfirst_shift = norm_back_one(dfirst)
    dattend = dhidden_one.astype(bf16)
    dcontext = dot_t(dattend, output_all).astype(bf16)
    dcontext = dcontext.reshape(2, rows, HEAD_GROUPS, GROUP_WIDTH).transpose(0, 2, 1, 3)
    dcontext = exchange(dcontext.reshape(8, rows, GROUP_WIDTH)).reshape(8 * rows, GROUP_WIDTH)

    out_rows = width // seq_size
    ctx_split = context.reshape(n_own, chips, 2, out_rows)
    ctx_split = [ctx_split[:, :, i].reshape(n_own, width // 2) for i in range(2)]
    both_ctx = jnp.concatenate([pick(ctx_split, core), sflip(pick(ctx_split, 1 - core), 1)], axis=0)
    both_dattend = jnp.concatenate([dattend, sflip(dattend, 1)], axis=0)
    vectors = jnp.stack([dfirst_gain, dfirst_shift, dsecond_gain, dsecond_shift])
    other_blocks = other_grads(dinner, both_ctx, both_dattend, douter, vectors, chips)
    feed_blocks = feed_grads(both_first, dinner, active, both_douter, chips)
    feed_blocks, other_blocks, dcontext = lax.optimization_barrier((feed_blocks, other_blocks, dcontext))
    feed_sums = over_chips(feed_blocks)

    def halve(low, high, bit, mask):
        sent = jnp.where(bit == 0, high, low).astype(bf16)
        return jnp.where(bit == 0, low, high) + sflip(sent, mask).astype(jnp.float32)

    def halve_other(blocks, b):
        pairs = blocks.reshape((-1, 2) + blocks.shape[1:])
        return halve(pairs[:, 0], pairs[:, 1], (me >> (b + 1)) % 2, 2 << b)

    last = part_bits[-1]
    dqueries, sent, kept = attend_backward(
        queries, kv, key_tail, context_full, stats, dcontext, ((me // last) % 2).astype(jnp.int32).reshape(1)
    )
    dkv = (kept + sflip(sent, last).astype(jnp.float32)).reshape(n_parts // 2, 8 * rows, 2 * GROUP_WIDTH)
    for b in reversed(part_bits[:-1]):
        bit = (me // b) % 2
        n_now = dkv.shape[0] // 2
        low, high = dkv[:n_now], dkv[n_now:]
        sent = jnp.where(bit == 0, high, low).astype(bf16)
        dkv = jnp.where(bit == 0, low, high) + sflip(sent, b).astype(jnp.float32)
    dqkv = jnp.concatenate([dqueries, dkv[0].astype(bf16)], axis=1)
    other_sums = halve_other(other_blocks, 0)

    dx = dot_t(dqkv, w_all).reshape(2, 2, 2, rows, width)
    da, db = dx[..., :half_width], dx[..., half_width:]

    da = halve(da[:, :, 0], da[:, :, 1], y0, YO)
    db = halve(db[:, 0], db[:, 1], z0, ZO)
    da, db, other_sums = lax.optimization_barrier((da, db, halve_other(other_sums, 1)))
    da = halve(da[:, 0], da[:, 1], z0, ZO)
    db = halve(db[:, 0], db[:, 1], y0, YO)
    dx = jnp.concatenate([da, db], axis=-1)
    mine = pick(dx, z1)
    theirs = sflip(pick(dx, 1 - z1).astype(bf16), HI).astype(jnp.float32)
    dtokens = dhidden_one.reshape(2, rows, width) + in_order(mine, theirs, z1)

    for b in range(2, log2_of(chips)):
        other_sums = halve_other(other_sums, b)
    feed_sums, other_sums = over_groups(feed_sums), over_groups(other_sums[0].astype(bf16))
    r1 = 4 * out_rows
    inner_grad = feed_sums[:r1].reshape(2, 2, out_rows, width)
    inner_grad = [inner_grad[:, i] for i in range(2)]
    far = sflip(jnp.concatenate([pick(inner_grad, 1 - core).reshape(2 * out_rows, width), other_sums[out_rows:]], axis=0), 1)
    dinner_weight = in_order(pick(inner_grad, core), far[: 2 * out_rows].reshape(2, out_rows, width), core)
    dinner_weight = dinner_weight.transpose(2, 0, 1, 3).reshape(out_rows, 2, chips, piece).transpose(0, 2, 1, 3)
    dinner_weight = dinner_weight.reshape(out_rows, feed).astype(jnp.float32)
    douter_weight = feed_sums[r1:].astype(jnp.float32)
    doutput_weight = other_sums[:out_rows].astype(jnp.float32)
    small = other_sums[out_rows:].astype(jnp.float32)
    both = lax.dynamic_slice_in_dim(small + far[2 * out_rows :].astype(jnp.float32), me * out_rows, out_rows, axis=1)
    dfirst_gain, dfirst_shift, dsecond_gain, dsecond_shift, doutput_bias, douter_bias = (both[i] for i in range(6))
    dinner_bias = lax.dynamic_slice_in_dim(small[6:8].reshape(half_feed), (me // 2) * piece, piece)

    dw = t_dot(x_all, dqkv)
    dbias = column_sums(dqkv)
    dw = dw.reshape(seq_size, out_rows, 3 * GROUP_WIDTH)
    dw = jnp.concatenate([dw, jnp.broadcast_to(dbias, (seq_size, 8, 3 * GROUP_WIDTH))], axis=1)
    block = dw.shape[1]
    n_extra = 1 << len(extra_bits)
    dw = dw.reshape(2, 2, 2, n_extra, 2, 1, block, 3 * GROUP_WIDTH)[:, :, :, :, :, 0]
    dw = dw.reshape(2, 2, n_extra, 2, 2, block, 3 * GROUP_WIDTH)
    dw = halve(dw[:, :, :, :, 0], dw[:, :, :, :, 1], me % 2, 1)
    for b in reversed(extra_bits):
        m = dw.shape[2] // 2
        dw = halve(dw[:, :, :m], dw[:, :, m:], (me // b) % 2, b)
    dw = dw[:, :, 0]
    dw = halve(dw[0], dw[1], z1, HI)
    for b in range(log2_of(grp_size)):
        dw = dw + flip(dw.astype(bf16), "grp", grp_size, 1 << b).astype(jnp.float32)
    dw = dw.astype(bf16).reshape(HEAD_GROUPS, block, 3 * GROUP_WIDTH)

    def row_block(k):
        return lax.dynamic_index_in_dim(dw, head_group ^ k, 0, keepdims=False)

    w0 = row_block(0)
    w1 = sflip(row_block(1), YO)
    w2 = sflip(row_block(2), ZO)
    w3 = sflip(row_block(3), ZO | YO)
    dw = in_order(in_order(w0, w1, y0), in_order(w2, w3, y0), z0).reshape(HEAD_GROUPS, block, 3, GROUP_WIDTH)
    dw = dw.astype(jnp.float32).transpose(2, 1, 0, 3).reshape(3, block, width)
    dquery_weight, dkey_weight, dvalue_weight = dw[0, :out_rows], dw[1, :out_rows], dw[2, :out_rows]
    dquery_bias = lax.dynamic_slice_in_dim(dw[0, out_rows], me * out_rows, out_rows)
    dvalue_bias = lax.dynamic_slice_in_dim(dw[2, out_rows], me * out_rows, out_rows)

    return (
        layer_out.astype(bf16).reshape(2, rows, width),
        dtokens.astype(bf16),
        dquery_weight,
        dquery_bias,
        dkey_weight,
        dvalue_weight,
        dvalue_bias,
        doutput_weight,
        doutput_bias,
        dfirst_gain,
        dfirst_shift,
        dinner_weight,
        dinner_bias,
        douter_weight,
        douter_bias,
        dsecond_gain,
        dsecond_shift,
    )


def solution(mesh):
    in_specs = (
        P("grp", "seq", None),
        P("grp"),
        P(("grp", "seq"), None),
        P(("grp", "seq")),
        P(("grp", "seq"), None),
        P(("grp", "seq"), None),
        P(("grp", "seq")),
        P(("grp", "seq"), None),
        P(("grp", "seq")),
        P(("grp", "seq")),
        P(("grp", "seq")),
        P(("grp", "seq"), None),
        P(("grp", "seq")),
        P(("grp", "seq"), None),
        P(("grp", "seq")),
        P(("grp", "seq")),
        P(("grp", "seq")),
        P("grp", "seq", None),
    )
    out_specs = (
        P("grp", "seq", None),
        P("grp", "seq", None),
        P("seq", None),
        P("seq"),
        P("seq", None),
        P("seq", None),
        P("seq"),
        P("seq", None),
        P("seq"),
        P("seq"),
        P("seq"),
        P("seq", None),
        P("seq"),
        P("seq", None),
        P("seq"),
        P("seq"),
        P("seq"),
    )
    body = partial(per_device, mesh.shape["seq"], mesh.shape["grp"])
    return jax.shard_map(
        body, mesh=mesh, in_specs=in_specs, out_specs=out_specs, check_vma=False
    )
```

```python
from functools import partial

import jax
import jax.numpy as jnp
from jax import lax
from jax.experimental import pallas as pl
from jax.experimental.pallas import tpu as pltpu
from jax.sharding import PartitionSpec as P

HEADS = 12
HEAD = 64
HEAD_GROUPS = 4
GROUP_WIDTH = HEADS * HEAD // HEAD_GROUPS
NH = HEADS // HEAD_GROUPS
BF16 = jnp.bfloat16
F32 = jnp.float32

score_scale = 0.125
epsilon = 1e-12
masked_score = -1e30


def log2_of(size):
    return size.bit_length() - 1


def flip(value, axis, size, mask):
    return lax.ppermute(value, axis, [(i, i ^ mask) for i in range(size)])


def in_order(mine, theirs, bit):
    return jnp.where(bit == 0, jnp.stack([mine, theirs]), jnp.stack([theirs, mine]))


def pick(pair, bit):
    return jnp.where(bit == 0, pair[0], pair[1])


def layer_norm(hidden, norm_gain, norm_shift):
    centred = hidden - jnp.mean(hidden, axis=-1, keepdims=True)
    spread = jnp.mean(centred * centred, axis=-1, keepdims=True)
    return centred * lax.rsqrt(spread + epsilon) * norm_gain + norm_shift


def dot(left, right):
    return jnp.dot(left, right, preferred_element_type=jnp.float32)


def dot_t(left, right):
    return lax.dot_general(left, right, (((1,), (1,)), ((), ())), preferred_element_type=jnp.float32)


def t_dot(left, right):
    return lax.dot_general(left, right, (((0,), (0,)), ((), ())), preferred_element_type=jnp.float32)


def column_sums(matrix):
    return jnp.sum(matrix.astype(jnp.float32), axis=0)


def thirds(x):
    hi=x.astype(BF16)
    r=x-hi.astype(F32)
    mid=r.astype(BF16)
    lo=(r-mid.astype(F32)).astype(BF16)
    return hi,mid,lo

def fwd_body(q_ref, kv_ref, kb_ref, c_ref, cf_ref, st_ref, kt, va, oacc, lacc, *, bq):
    i=pl.program_id(0); h=pl.program_id(1)
    W=NH*HEAD
    @pl.when((i==0)&(h==0))
    def _():
        tail=kb_ref[:,HEAD:]
        for g in range(NH):
            ka=jnp.concatenate([kv_ref[:,g*HEAD:(g+1)*HEAD],tail],axis=1)
            kt[g]=ka.T
            va[g]=jnp.concatenate([kv_ref[:,W+g*HEAD:W+(g+1)*HEAD],tail],axis=1)
    one=jnp.where(lax.broadcasted_iota(jnp.int32,(bq,HEAD),1)==0,1.0,0.0).astype(BF16)
    def head(g):
        qa=jnp.concatenate([q_ref[:,g*HEAD:(g+1)*HEAD],one],axis=1)
        s=dot(qa,kt[g])
        m=jnp.max(s,axis=1,keepdims=True)
        p=jnp.exp(s-m).astype(BF16)
        o=dot(p,va[g])
        l=o[:,HEAD+1:HEAD+2]
        oacc[g]=o/l
        lacc[g]=jnp.broadcast_to(m+jnp.log(l),(bq,128))
    for g in range(NH):
        @pl.when(h==g)
        def _(): head(g)
    @pl.when(h==NH-1)
    def _():
        c=jnp.concatenate([oacc[g][:,:HEAD] for g in range(NH)],axis=1)
        c_ref[...]=c.astype(BF16)
        cf_ref[...]=c
        lane=lax.broadcasted_iota(jnp.int32,(bq,128),1)
        st=lacc[0]
        for g in range(1,NH): st=jnp.where(lane==g,lacc[g],st)
        st_ref[...]=st

def attend_forward(q,kv,kb,bq=256):
    n,W=q.shape; L=kv.shape[0]
    return pl.pallas_call(partial(fwd_body,bq=bq),
        grid=(n//bq,NH),
        in_specs=[pl.BlockSpec((bq,W),lambda i,h:(i,0)),pl.BlockSpec((L,2*W),lambda i,h:(0,0)),pl.BlockSpec((L,128),lambda i,h:(0,0))],
        out_specs=[pl.BlockSpec((bq,W),lambda i,h:(i,0)),pl.BlockSpec((bq,W),lambda i,h:(i,0)),pl.BlockSpec((bq,128),lambda i,h:(i,0))],
        out_shape=[jax.ShapeDtypeStruct((n,W),BF16),jax.ShapeDtypeStruct((n,W),F32),jax.ShapeDtypeStruct((n,128),F32)],
        scratch_shapes=[pltpu.VMEM((NH,128,L),BF16),pltpu.VMEM((NH,L,128),BF16),pltpu.VMEM((NH,bq,128),F32),pltpu.VMEM((NH,bq,128),F32)],
        cost_estimate=pl.CostEstimate(flops=16*n*L*W, transcendentals=NH*n*L, bytes_accessed=4*n*L),
        name="attend_forward",
    )(q,kv,kb)

def bwd_body(bit_ref, q_ref, kv_ref, kb_ref, cf_ref, st_ref, dc_ref, dq_ref, sent_ref, kept_ref, qt, qn, dct, dcn, dqt, dk, dv, *, nk):
    j=pl.program_id(0); h=pl.program_id(1)
    W=NH*HEAD
    n=q_ref.shape[0]
    @pl.when((j==0)&(h==0))
    def _():
        pad=jnp.zeros((n,256-W),BF16)
        row=lax.broadcasted_iota(jnp.int32,(16,n),0)
        lane=lax.broadcasted_iota(jnp.int32,(8,W),1)
        head_row=lax.broadcasted_iota(jnp.int32,(8,W),0)
        pick=jnp.where((lane>=head_row*HEAD)&(lane<head_row*HEAD+HEAD),1.0,0.0).astype(BF16)
        prod=dc_ref[...].astype(F32)*cf_ref[...]
        hi,mid,lo=thirds(prod)
        deltas=dot_t(pick,hi)+dot_t(pick,mid)+dot_t(pick,lo)
        stats=st_ref[...].T
        q_t=jnp.concatenate([q_ref[...],pad],axis=1).T
        d_t=jnp.concatenate([dc_ref[...],pad],axis=1).T
        def tail(x,first):
            hi,mid,lo=(v.astype(F32) for v in thirds(-x))
            z=jnp.where(row==1,hi,jnp.where(row==2,mid,jnp.where(row==3,lo,0.0)))
            return jnp.where(row==0,first,z).astype(BF16)
        rest=jnp.zeros((HEAD-16,n),BF16)
        for g in range(NH):
            cols=slice(g*HEAD,(g+1)*HEAD)
            for t,x,first,dst in ((q_t,stats,1.0,qt),(d_t,deltas,0.0,dct)):
                dst[g,:HEAD]=t[cols]
                dst[g,HEAD:HEAD+16]=tail(x[g:g+1],first)
                dst[g,HEAD+16:]=rest
            qn[g]=q_ref[:,cols]
            dcn[g]=dc_ref[:,cols]
        dqt[...]=jnp.zeros_like(dqt)
    key_tail=kb_ref[:,HEAD:]
    def head(g):
        k=kv_ref[:,g*HEAD:(g+1)*HEAD]
        ka=jnp.concatenate([k,key_tail],axis=1)
        va=jnp.concatenate([kv_ref[:,W+g*HEAD:W+(g+1)*HEAD],key_tail],axis=1)
        p=jnp.exp(dot(ka,qt[g]))
        dp=dot(va,dct[g])
        ds=(p*dp).astype(BF16)
        dv[g]=dot(p.astype(BF16),dcn[g])
        dk[g]=dot(ds,qn[g])
        dqt[g]=dqt[g]+t_dot(ka,ds)[:HEAD]
    for g in range(NH):
        @pl.when(h==g)
        def _(): head(g)
    @pl.when(h==NH-1)
    def _():
        dkv=jnp.concatenate([dk[g] for g in range(NH)]+[dv[g] for g in range(NH)],axis=1)
        @pl.when(j<nk//2)
        def _():
            sent_ref[...]=dkv.astype(BF16)
        @pl.when(j>=nk//2)
        def _():
            kept_ref[...]=dkv
    @pl.when((h==NH-1)&(j==nk-1))
    def _():
        for g in range(NH):
            dq_ref[:,g*HEAD:(g+1)*HEAD]=(dqt[g].T*0.125).astype(BF16)

def attend_backward(q,kv,kb,cf,st,dc,bit,bk=768):
    n,W=q.shape; L=kv.shape[0]; nk=L//bk; half=nk//2
    full=lambda a: pl.BlockSpec(a.shape,lambda j,h,b:(0,0))
    key=lambda j,h,b:(jnp.where(j<half,(1-b[0])*half+j,b[0]*half+j-half),0)
    return pl.pallas_call(partial(bwd_body,nk=nk),
        grid_spec=pltpu.PrefetchScalarGridSpec(
            num_scalar_prefetch=1,
            grid=(nk,NH),
            in_specs=[full(q),pl.BlockSpec((bk,2*W),key),pl.BlockSpec((bk,128),key),full(cf),full(st),full(dc)],
            out_specs=[pl.BlockSpec((n,W),lambda j,h,b:(0,0)),
                pl.BlockSpec((bk,2*W),lambda j,h,b:(jnp.minimum(j,half-1),0)),
                pl.BlockSpec((bk,2*W),lambda j,h,b:(jnp.maximum(j-half,0),0))],
            scratch_shapes=[pltpu.VMEM((NH,2*HEAD,n),BF16),pltpu.VMEM((NH,n,HEAD),BF16),pltpu.VMEM((NH,2*HEAD,n),BF16),pltpu.VMEM((NH,n,HEAD),BF16),
                pltpu.VMEM((NH,HEAD,n),F32),pltpu.VMEM((NH,bk,HEAD),F32),pltpu.VMEM((NH,bk,HEAD),F32)]),
        out_shape=[jax.ShapeDtypeStruct((n,W),BF16),jax.ShapeDtypeStruct((L//2,2*W),BF16),jax.ShapeDtypeStruct((L//2,2*W),F32)],
        name="attend_backward",
    )(bit,q,kv,kb,cf,st,dc)


def feed_grads_body(y_ref, dz_ref, a_ref, do_ref, out_ref, *, chips):
    width = y_ref.shape[1]
    r_in, r_out = width // chips, a_ref.shape[1] // chips
    half = chips // 2
    for j in range(2):
        grad = t_dot(y_ref[...], dz_ref[:, j * width : (j + 1) * width]).astype(BF16)
        for q in range(chips):
            out_ref[q, j * r_in : (j + 1) * r_in] = grad[q * r_in : (q + 1) * r_in]
        grad = t_dot(a_ref[:, j * width : (j + 1) * width], do_ref[...]).astype(BF16)
        for q in range(half):
            out_ref[j * half + q, 2 * r_in :] = grad[q * r_out : (q + 1) * r_out]


def feed_grads(y, dz, a, do, chips):
    width = y.shape[1]
    return pl.pallas_call(
        partial(feed_grads_body, chips=chips),
        out_shape=jax.ShapeDtypeStruct((chips, (2 * width + a.shape[1]) // chips, width), BF16),
        cost_estimate=pl.CostEstimate(
            flops=4 * width * y.shape[0] * dz.shape[1], transcendentals=0, bytes_accessed=10 * width * width * 2
        ),
        name="feed_grads",
    )(y, dz, a, do)


def other_grads_body(dz_ref, ctx_ref, da_ref, do_ref, vec_ref, out_ref, *, chips):
    width = da_ref.shape[1]
    r_ctx = ctx_ref.shape[1] // chips
    grad = t_dot(ctx_ref[...], da_ref[...]).astype(BF16)
    n = do_ref.shape[0]
    ones = jnp.ones((16, da_ref.shape[0]), BF16)
    sums = [dot(ones[:, :n], da_ref[:n])[:1], dot(ones[:, :n], do_ref[...])[:1]]
    sums += [dot(ones, dz_ref[:, j * width : (j + 1) * width])[:1] for j in range(2)]
    small = jnp.concatenate([vec_ref[...]] + sums, axis=0).astype(BF16)
    for q in range(chips):
        out_ref[q, :r_ctx] = grad[q * r_ctx : (q + 1) * r_ctx]
        out_ref[q, r_ctx:] = small


def other_grads(dz, ctx, da, do, vec, chips):
    width = da.shape[1]
    return pl.pallas_call(
        partial(other_grads_body, chips=chips),
        out_shape=jax.ShapeDtypeStruct((chips, ctx.shape[1] // chips + vec.shape[0] + 4, width), BF16),
        cost_estimate=pl.CostEstimate(
            flops=2 * width * ctx.shape[0] * ctx.shape[1], transcendentals=0, bytes_accessed=5 * width * width * 2
        ),
        name="other_grads",
    )(dz, ctx, da, do, vec)


def per_device(
    seq_size,
    grp_size,
    tokens,
    valid_len,
    query_weight,
    query_bias,
    key_weight,
    value_weight,
    value_bias,
    output_weight,
    output_bias,
    first_gain,
    first_shift,
    inner_weight,
    inner_bias,
    outer_weight,
    outer_bias,
    second_gain,
    second_shift,
    grad_out,
):
    bf16 = jnp.bfloat16
    rows, width = tokens.shape[1:]
    feed = inner_weight.shape[1]
    shard = query_weight.shape[0]
    HI, ZO, YO = seq_size // 2, seq_size // 4, 2
    extra_bits = [1 << b for b in range(2, log2_of(ZO))]
    part_bits = [1] + extra_bits
    me = lax.axis_index("seq")
    grp = lax.axis_index("grp")
    z1 = me // HI
    z0 = (me // ZO) % 2
    y0 = (me // YO) % 2
    head_group = 2 * z0 + y0
    my_part = me % 2 + 2 * ((me // 4) % max(ZO // 4, 1))
    n_parts = seq_size // 8

    def sflip(value, mask):
        return flip(value, "seq", seq_size, mask)

    chips = seq_size // 2
    x_mine = pick(tokens, z1)
    x_sent = pick(tokens, 1 - z1)
    half_width = width // 2
    x_theirs = sflip(x_sent, HI)
    x_pair = in_order(x_mine, x_theirs, z1)
    xa, xb = x_pair[:, :, :half_width], x_pair[:, :, half_width:]
    ra, rb = sflip(xa, YO), sflip(xb, ZO)
    xa, xb = in_order(xa, ra, y0), in_order(xb, rb, z0)
    ra, rb = sflip(xa, ZO), sflip(xb, YO)
    xa, xb = in_order(xa, ra, z0), in_order(xb, rb, y0)
    x_all = jnp.concatenate([xa.transpose(2, 0, 1, 3, 4), xb.transpose(2, 1, 0, 3, 4)], axis=-1)
    x_all = x_all.reshape(8 * rows, width)

    core = me % 2
    chips = seq_size // 2
    piece = feed // seq_size
    n_dev = grp_size * seq_size
    half_feed = feed // 2
    split = inner_weight.reshape(shard, chips, 2, piece)
    split = [split[:, :, i].reshape(shard, 2, width).transpose(1, 0, 2).reshape(2 * shard, width) for i in range(2)]
    near = jnp.concatenate([pick(split, 1 - core), output_weight], axis=0)
    far = sflip(near, 1)
    outer_far = lax.ppermute(
        outer_weight,
        ("grp", "seq"),
        [(d, d ^ (1 | grp_size) if d % 2 != (d // grp_size) % 2 else d) for d in range(n_dev)],
    )
    inner_pair = in_order(pick(split, core).reshape(2, shard, width), far[: 2 * shard].reshape(2, shard, width), core)
    packed = jnp.concatenate(
        [
            inner_pair.transpose(1, 0, 2, 3).reshape(4 * shard, width),
            in_order(output_weight, far[2 * shard :], core).reshape(2 * shard, width),
            outer_far,
        ],
        axis=0,
    )
    chip_groups = [[2 * q + i for q in range(chips)] for i in range(2)]
    gathered = lax.all_gather(packed, "seq", axis=0, tiled=False, axis_index_groups=chip_groups)
    first_end = 6 * shard
    gathered = [gathered]
    for b in range(log2_of(grp_size)):
        gathered += [flip(part, "grp", grp_size, 1 << b) for part in gathered]

    def gathered_rows(start, stop):
        parts = [x[:, start:stop] for x in gathered]
        stacks = {i: x[None] for i, x in enumerate(parts)}
        for b in range(log2_of(grp_size)):
            bit = (grp >> b) % 2
            merged = {}
            for i in range(len(stacks) // 2):
                low, high = stacks[2 * i], stacks[2 * i + 1]
                merged[i] = jnp.where(bit == 0, jnp.concatenate([low, high]), jnp.concatenate([high, low]))
            stacks = merged
        return stacks[0].reshape((-1,) + parts[0].shape[1:])

    smalls = jnp.concatenate(
        [query_bias, value_bias, output_bias, first_gain, first_shift, outer_bias, second_gain, second_shift, inner_bias]
    )
    small_rows = 32 - shard if shard == 24 else 8
    grouped = jnp.stack([query_weight, key_weight, value_weight]).reshape(3, shard, HEAD_GROUPS, GROUP_WIDTH)
    grouped = grouped.transpose(2, 1, 0, 3).reshape(HEAD_GROUPS, shard, 3 * GROUP_WIDTH)
    small_block = jnp.zeros((small_rows * 3 * GROUP_WIDTH,), bf16).at[: smalls.shape[0]].set(smalls)
    small_block = jnp.broadcast_to(small_block.reshape(1, small_rows, -1), (HEAD_GROUPS, small_rows, 3 * GROUP_WIDTH))
    grouped = jnp.concatenate([grouped, small_block], axis=1)
    grouped, _ = lax.optimization_barrier((grouped, x_theirs))

    def group_block(k):
        return lax.dynamic_index_in_dim(grouped, head_group ^ k, 0, keepdims=False)

    w0 = group_block(0)
    w1 = sflip(group_block(1), YO)
    w2 = sflip(group_block(2), ZO)
    w3 = sflip(group_block(3), ZO | YO)
    w_all = in_order(in_order(w0, w1, y0), in_order(w2, w3, y0), z0)
    w_all = in_order(w_all, sflip(w_all, HI), z1)
    names = ["z1", "z0", "y0"]
    for b in extra_bits:
        w_all = in_order(w_all, sflip(w_all, b), (me // b) % 2)
        names = ["e%d" % b] + names
    for b in range(log2_of(grp_size)):
        w_all = in_order(w_all, flip(w_all, "grp", grp_size, 1 << b), (grp >> b) % 2)
        names = ["g%d" % b] + names
    w_all = in_order(w_all, sflip(w_all, 1), me % 2)
    names = ["c"] + names
    wanted = ["g%d" % b for b in reversed(range(log2_of(grp_size)))] + ["z1", "z0"]
    wanted += ["e%d" % b for b in reversed(extra_bits)] + ["y0", "c"]
    n = len(names)
    w_all = w_all.transpose(*[names.index(w) for w in wanted], n, n + 1)
    w_all = w_all.reshape(grp_size * seq_size, shard + small_rows, 3 * GROUP_WIDTH)
    small_all = w_all[:, shard:].reshape(grp_size * seq_size, -1)[:, : smalls.shape[0]]
    vectors = [small_all[:, i * shard : (i + 1) * shard].reshape(-1).astype(jnp.float32) for i in range(8)]
    q_bias, v_bias, o_bias, gain1, shift1, out_bias, gain2, shift2 = vectors
    in_bias = small_all[:, 8 * shard :].reshape(-1).astype(jnp.float32)
    w_all = w_all[:, :shard].reshape(width, 3 * GROUP_WIDTH)

    def own_columns(vector):
        return lax.dynamic_slice_in_dim(vector, head_group * GROUP_WIDTH, GROUP_WIDTH)

    qkv_bias = jnp.concatenate([own_columns(q_bias), jnp.zeros((GROUP_WIDTH,), jnp.float32), own_columns(v_bias)])
    qkv = dot(x_all, w_all) + qkv_bias
    queries = (qkv[:, :GROUP_WIDTH] * score_scale).astype(bf16)
    kv = qkv[:, GROUP_WIDTH:].astype(bf16)[None]
    for b in part_bits:
        bit = (me // b) % 2
        theirs = sflip(kv, b)
        kv = jnp.where(bit == 0, jnp.concatenate([kv, theirs]), jnp.concatenate([theirs, kv]))
    kv = kv.reshape(-1, 2 * GROUP_WIDTH)

    part = jnp.arange(n_parts, dtype=jnp.int32)
    part_device = part % 2 + 4 * (part // 2)
    member = jnp.arange(8, dtype=jnp.int32)
    member_device = (member // 4) * HI + ((member // 2) % 2) * ZO + (member % 2) * YO
    device = part_device[:, None] + member_device[None, :]
    position = (device[:, :, None] * rows + jnp.arange(rows, dtype=jnp.int32)).reshape(-1)
    bias = jnp.where(position < pick(valid_len, z1), 0.0, masked_score)[:, None]
    lane = jnp.arange(128, dtype=jnp.int32)[None, :]
    key_tail = jnp.where(lane == HEAD, bias, jnp.where((lane > HEAD) & (lane < HEAD + 4), 1.0, 0.0)).astype(bf16)

    context, context_full, stats = attend_forward(queries, kv, key_tail)

    teams = [
        [a * HI + b * ZO + c * YO + q for a in range(2) for b in range(2) for c in range(2)]
        for q in [i % 2 + 4 * (i // 2) for i in range(n_parts)]
    ]

    def exchange(blocks):
        return lax.all_to_all(blocks, "seq", 0, 0, axis_index_groups=teams, tiled=True)

    context = exchange(context.reshape(8, rows, GROUP_WIDTH))
    context = context.reshape(2, HEAD_GROUPS, rows, GROUP_WIDTH).transpose(0, 2, 1, 3).reshape(2 * rows, width)

    inner_lo = gathered_rows(0, 2 * shard).reshape(width, width)
    inner_hi = gathered_rows(2 * shard, 4 * shard).reshape(width, width)
    output_all = gathered_rows(4 * shard, first_end).reshape(width, width)
    outer_all = gathered_rows(first_end, first_end + outer_weight.shape[0])
    outer_all = outer_all.reshape(-1, 2, grp_size // 2, outer_weight.shape[0], width)
    outer_all = outer_all.transpose(0, 2, 1, 3, 4).reshape(half_feed, width)

    in_bias = pick(in_bias.reshape(chips, 2, piece).transpose(1, 0, 2).reshape(2, half_feed), core)

    home = tokens.reshape(2 * rows, width)
    cotangent = grad_out.reshape(2 * rows, width)
    hidden_one = home.astype(jnp.float32) + dot(context, output_all) + o_bias
    norm_one, norm_back_one = jax.vjp(layer_norm, hidden_one, gain1, shift1)
    first_out = norm_one.astype(bf16)
    n_own = 2 * rows
    both_first = jnp.concatenate([first_out, sflip(first_out, 1)], axis=0)

    def gelu_pair(pre):
        full, back = jax.vjp(partial(jax.nn.gelu, approximate=False), pre)
        return full.astype(bf16), back(jnp.ones_like(pre))[0]

    inner_all = jnp.concatenate([inner_lo, inner_hi], axis=1)
    active, slope = gelu_pair(dot(both_first, inner_all) + in_bias)
    outer_part = dot(active, outer_all)
    outer_sum = outer_part[:n_own] + sflip(outer_part[n_own:].astype(bf16), 1).astype(jnp.float32)
    hidden_two = first_out.astype(jnp.float32) + outer_sum + out_bias
    layer_out, norm_back_two = jax.vjp(layer_norm, hidden_two, gain2, shift2)
    dhidden_two, dsecond_gain, dsecond_shift = norm_back_two(cotangent.astype(jnp.float32))
    douter = dhidden_two.astype(bf16)
    both_douter = jnp.concatenate([douter, sflip(douter, 1)], axis=0)

    def over_chips(blocks):
        return lax.psum_scatter(blocks, "seq", scatter_dimension=0, tiled=False, axis_index_groups=chip_groups)

    def over_groups(blocks):
        for b in range(log2_of(grp_size)):
            blocks = (blocks.astype(jnp.float32) + flip(blocks, "grp", grp_size, 1 << b).astype(jnp.float32)).astype(bf16)
        return blocks

    dinner = (dot_t(both_douter, outer_all) * slope).astype(bf16)
    dfirst_part = dot_t(dinner, inner_all)
    dfirst = dhidden_two + dfirst_part[:n_own] + sflip(dfirst_part[n_own:].astype(bf16), 1).astype(jnp.float32)
    dhidden_one, dfirst_gain, dfirst_shift = norm_back_one(dfirst)
    dattend = dhidden_one.astype(bf16)
    dcontext = dot_t(dattend, output_all).astype(bf16)
    dcontext = dcontext.reshape(2, rows, HEAD_GROUPS, GROUP_WIDTH).transpose(0, 2, 1, 3)
    dcontext, late_context = lax.optimization_barrier((dcontext.reshape(8, rows, GROUP_WIDTH), context))
    dcontext = exchange(dcontext).reshape(8 * rows, GROUP_WIDTH)

    out_rows = width // seq_size
    ctx_split = late_context.reshape(n_own, chips, 2, out_rows)
    ctx_split = [ctx_split[:, :, i].reshape(n_own, width // 2) for i in range(2)]
    both_ctx = jnp.concatenate([pick(ctx_split, core), sflip(pick(ctx_split, 1 - core), 1)], axis=0)
    both_dattend = jnp.concatenate([dattend, sflip(dattend, 1)], axis=0)
    vectors = jnp.stack([dfirst_gain, dfirst_shift, dsecond_gain, dsecond_shift])
    other_blocks = other_grads(dinner, both_ctx, both_dattend, douter, vectors, chips)
    feed_blocks = feed_grads(both_first, dinner, active, both_douter, chips)
    feed_blocks, other_blocks, dcontext = lax.optimization_barrier((feed_blocks, other_blocks, dcontext))
    feed_sums = over_chips(feed_blocks)

    def halve(low, high, bit, mask):
        sent = jnp.where(bit == 0, high, low).astype(bf16)
        return jnp.where(bit == 0, low, high) + sflip(sent, mask).astype(jnp.float32)

    def halve_other(blocks, b):
        pairs = blocks.reshape((-1, 2) + blocks.shape[1:])
        return halve(pairs[:, 0], pairs[:, 1], (me >> (b + 1)) % 2, 2 << b)

    last = part_bits[-1]
    dqueries, sent, kept = attend_backward(
        queries, kv, key_tail, context_full, stats, dcontext, ((me // last) % 2).astype(jnp.int32).reshape(1)
    )
    dkv = (kept + sflip(sent, last).astype(jnp.float32)).reshape(n_parts // 2, 8 * rows, 2 * GROUP_WIDTH)
    for b in reversed(part_bits[:-1]):
        bit = (me // b) % 2
        n_now = dkv.shape[0] // 2
        low, high = dkv[:n_now], dkv[n_now:]
        sent = jnp.where(bit == 0, high, low).astype(bf16)
        dkv = jnp.where(bit == 0, low, high) + sflip(sent, b).astype(jnp.float32)
    dqkv = jnp.concatenate([dqueries, dkv[0].astype(bf16)], axis=1)
    other_sums = halve_other(other_blocks, 0)

    dx, late_x = lax.optimization_barrier((dot_t(dqkv, w_all).reshape(2, 2, 2, rows, width), x_all))
    da, db = dx[..., :half_width], dx[..., half_width:]

    da = halve(da[:, :, 0], da[:, :, 1], y0, YO)
    db = halve(db[:, 0], db[:, 1], z0, ZO)
    other_sums = halve_other(other_sums, 1)
    da, db, other_sums, feed_sums = lax.optimization_barrier((da, db, other_sums, feed_sums))
    feed_sums = over_groups(feed_sums)
    da = halve(da[:, 0], da[:, 1], z0, ZO)
    db = halve(db[:, 0], db[:, 1], y0, YO)
    dx = jnp.concatenate([da, db], axis=-1)
    dx, feed_sums = lax.optimization_barrier((dx, feed_sums))
    mine = pick(dx, z1)
    theirs = sflip(pick(dx, 1 - z1).astype(bf16), HI).astype(jnp.float32)
    dtokens = dhidden_one.reshape(2, rows, width) + in_order(mine, theirs, z1)

    for b in range(2, log2_of(chips)):
        other_sums = halve_other(other_sums, b)
    other_sums = over_groups(other_sums[0].astype(bf16))
    r1 = 4 * out_rows
    inner_grad = feed_sums[:r1].reshape(2, 2, out_rows, width)
    inner_grad = [inner_grad[:, i] for i in range(2)]
    far = sflip(jnp.concatenate([pick(inner_grad, 1 - core).reshape(2 * out_rows, width), other_sums[out_rows:]], axis=0), 1)
    dinner_weight = in_order(pick(inner_grad, core), far[: 2 * out_rows].reshape(2, out_rows, width), core)
    dinner_weight = dinner_weight.transpose(2, 0, 1, 3).reshape(out_rows, 2, chips, piece).transpose(0, 2, 1, 3)
    dinner_weight = dinner_weight.reshape(out_rows, feed).astype(jnp.float32)
    douter_weight = feed_sums[r1:].astype(jnp.float32)
    doutput_weight = other_sums[:out_rows].astype(jnp.float32)
    small = other_sums[out_rows:].astype(jnp.float32)
    both = lax.dynamic_slice_in_dim(small + far[2 * out_rows :].astype(jnp.float32), me * out_rows, out_rows, axis=1)
    dfirst_gain, dfirst_shift, dsecond_gain, dsecond_shift, doutput_bias, douter_bias = (both[i] for i in range(6))
    dinner_bias = lax.dynamic_slice_in_dim(small[6:8].reshape(half_feed), (me // 2) * piece, piece)

    dw = t_dot(x_all, dqkv)
    dbias = column_sums(dqkv)
    dw = dw.reshape(seq_size, out_rows, 3 * GROUP_WIDTH)
    dw = jnp.concatenate([dw, jnp.broadcast_to(dbias, (seq_size, 8, 3 * GROUP_WIDTH))], axis=1)
    block = dw.shape[1]
    n_extra = 1 << len(extra_bits)
    dw = dw.reshape(2, 2, 2, n_extra, 2, 1, block, 3 * GROUP_WIDTH)[:, :, :, :, :, 0]
    dw = dw.reshape(2, 2, n_extra, 2, 2, block, 3 * GROUP_WIDTH)
    dw = halve(dw[:, :, :, :, 0], dw[:, :, :, :, 1], me % 2, 1)
    for b in reversed(extra_bits):
        m = dw.shape[2] // 2
        dw = halve(dw[:, :, :m], dw[:, :, m:], (me // b) % 2, b)
    dw = dw[:, :, 0]
    dw = halve(dw[0], dw[1], z1, HI)
    for b in range(log2_of(grp_size)):
        dw = dw + flip(dw.astype(bf16), "grp", grp_size, 1 << b).astype(jnp.float32)
    dw = dw.astype(bf16).reshape(HEAD_GROUPS, block, 3 * GROUP_WIDTH)

    def row_block(k):
        return lax.dynamic_index_in_dim(dw, head_group ^ k, 0, keepdims=False)

    w0 = row_block(0)
    w1 = sflip(row_block(1), YO)
    w2 = sflip(row_block(2), ZO)
    w3 = sflip(row_block(3), ZO | YO)
    dw = in_order(in_order(w0, w1, y0), in_order(w2, w3, y0), z0).reshape(HEAD_GROUPS, block, 3, GROUP_WIDTH)
    dw = dw.astype(jnp.float32).transpose(2, 1, 0, 3).reshape(3, block, width)
    dquery_weight, dkey_weight, dvalue_weight = dw[0, :out_rows], dw[1, :out_rows], dw[2, :out_rows]
    dquery_bias = lax.dynamic_slice_in_dim(dw[0, out_rows], me * out_rows, out_rows)
    dvalue_bias = lax.dynamic_slice_in_dim(dw[2, out_rows], me * out_rows, out_rows)

    return (
        layer_out.astype(bf16).reshape(2, rows, width),
        dtokens.astype(bf16),
        dquery_weight,
        dquery_bias,
        dkey_weight,
        dvalue_weight,
        dvalue_bias,
        doutput_weight,
        doutput_bias,
        dfirst_gain,
        dfirst_shift,
        dinner_weight,
        dinner_bias,
        douter_weight,
        douter_bias,
        dsecond_gain,
        dsecond_shift,
    )


def solution(mesh):
    in_specs = (
        P("grp", "seq", None),
        P("grp"),
        P(("grp", "seq"), None),
        P(("grp", "seq")),
        P(("grp", "seq"), None),
        P(("grp", "seq"), None),
        P(("grp", "seq")),
        P(("grp", "seq"), None),
        P(("grp", "seq")),
        P(("grp", "seq")),
        P(("grp", "seq")),
        P(("grp", "seq"), None),
        P(("grp", "seq")),
        P(("grp", "seq"), None),
        P(("grp", "seq")),
        P(("grp", "seq")),
        P(("grp", "seq")),
        P("grp", "seq", None),
    )
    out_specs = (
        P("grp", "seq", None),
        P("grp", "seq", None),
        P("seq", None),
        P("seq"),
        P("seq", None),
        P("seq", None),
        P("seq"),
        P("seq", None),
        P("seq"),
        P("seq"),
        P("seq"),
        P("seq", None),
        P("seq"),
        P("seq", None),
        P("seq"),
        P("seq"),
        P("seq"),
    )
    body = partial(per_device, mesh.shape["seq"], mesh.shape["grp"])
    return jax.shard_map(
        body, mesh=mesh, in_specs=in_specs, out_specs=out_specs, check_vma=False
    )
```

```python
from functools import partial

import jax
import jax.numpy as jnp
from jax import lax
from jax.experimental import pallas as pl
from jax.experimental.pallas import tpu as pltpu
from jax.sharding import PartitionSpec as P

HEADS = 12
HEAD = 64
HEAD_GROUPS = 4
GROUP_WIDTH = HEADS * HEAD // HEAD_GROUPS
NH = HEADS // HEAD_GROUPS
BF16 = jnp.bfloat16
F32 = jnp.float32

score_scale = 0.125
epsilon = 1e-12
masked_score = -1e30


def log2_of(size):
    return size.bit_length() - 1


def flip(value, axis, size, mask):
    return lax.ppermute(value, axis, [(i, i ^ mask) for i in range(size)])


def in_order(mine, theirs, bit):
    return jnp.where(bit == 0, jnp.stack([mine, theirs]), jnp.stack([theirs, mine]))


def pick(pair, bit):
    return jnp.where(bit == 0, pair[0], pair[1])


def layer_norm(hidden, norm_gain, norm_shift):
    centred = hidden - jnp.mean(hidden, axis=-1, keepdims=True)
    spread = jnp.mean(centred * centred, axis=-1, keepdims=True)
    return centred * lax.rsqrt(spread + epsilon) * norm_gain + norm_shift


def dot(left, right):
    return jnp.dot(left, right, preferred_element_type=jnp.float32)


def dot_t(left, right):
    return lax.dot_general(left, right, (((1,), (1,)), ((), ())), preferred_element_type=jnp.float32)


def t_dot(left, right):
    return lax.dot_general(left, right, (((0,), (0,)), ((), ())), preferred_element_type=jnp.float32)


def column_sums(matrix):
    return jnp.sum(matrix.astype(jnp.float32), axis=0)


def thirds(x):
    hi=x.astype(BF16)
    r=x-hi.astype(F32)
    mid=r.astype(BF16)
    lo=(r-mid.astype(F32)).astype(BF16)
    return hi,mid,lo

def fwd_body(q_ref, kv_ref, kb_ref, c_ref, cf_ref, st_ref, kt, va, oacc, lacc, *, bq):
    i=pl.program_id(0); h=pl.program_id(1)
    W=NH*HEAD
    @pl.when((i==0)&(h==0))
    def _():
        tail=kb_ref[:,HEAD:]
        for g in range(NH):
            ka=jnp.concatenate([kv_ref[:,g*HEAD:(g+1)*HEAD],tail],axis=1)
            kt[g]=ka.T
            va[g]=jnp.concatenate([kv_ref[:,W+g*HEAD:W+(g+1)*HEAD],tail],axis=1)
    one=jnp.where(lax.broadcasted_iota(jnp.int32,(bq,HEAD),1)==0,1.0,0.0).astype(BF16)
    def head(g):
        qa=jnp.concatenate([q_ref[:,g*HEAD:(g+1)*HEAD],one],axis=1)
        s=dot(qa,kt[g])
        m=jnp.max(s,axis=1,keepdims=True)
        p=jnp.exp(s-m).astype(BF16)
        o=dot(p,va[g])
        l=o[:,HEAD+1:HEAD+2]
        oacc[g]=o/l
        lacc[g]=jnp.broadcast_to(m+jnp.log(l),(bq,128))
    for g in range(NH):
        @pl.when(h==g)
        def _(): head(g)
    @pl.when(h==NH-1)
    def _():
        c=jnp.concatenate([oacc[g][:,:HEAD] for g in range(NH)],axis=1)
        c_ref[...]=c.astype(BF16)
        cf_ref[...]=c
        lane=lax.broadcasted_iota(jnp.int32,(bq,128),1)
        st=lacc[0]
        for g in range(1,NH): st=jnp.where(lane==g,lacc[g],st)
        st_ref[...]=st

def attend_forward(q,kv,kb,bq=256):
    n,W=q.shape; L=kv.shape[0]
    return pl.pallas_call(partial(fwd_body,bq=bq),
        grid=(n//bq,NH),
        in_specs=[pl.BlockSpec((bq,W),lambda i,h:(i,0)),pl.BlockSpec((L,2*W),lambda i,h:(0,0)),pl.BlockSpec((L,128),lambda i,h:(0,0))],
        out_specs=[pl.BlockSpec((bq,W),lambda i,h:(i,0)),pl.BlockSpec((bq,W),lambda i,h:(i,0)),pl.BlockSpec((bq,128),lambda i,h:(i,0))],
        out_shape=[jax.ShapeDtypeStruct((n,W),BF16),jax.ShapeDtypeStruct((n,W),F32),jax.ShapeDtypeStruct((n,128),F32)],
        scratch_shapes=[pltpu.VMEM((NH,128,L),BF16),pltpu.VMEM((NH,L,128),BF16),pltpu.VMEM((NH,bq,128),F32),pltpu.VMEM((NH,bq,128),F32)],
        cost_estimate=pl.CostEstimate(flops=16*n*L*W, transcendentals=NH*n*L, bytes_accessed=4*n*L),
        name="attend_forward",
    )(q,kv,kb)

def bwd_body(bit_ref, q_ref, kv_ref, kb_ref, cf_ref, st_ref, dc_ref, dq_ref, sent_ref, kept_ref, qt, qn, dct, dcn, dqt, dk, dv, *, nk):
    j=pl.program_id(0); h=pl.program_id(1)
    W=NH*HEAD
    n=q_ref.shape[0]
    @pl.when((j==0)&(h==0))
    def _():
        pad=jnp.zeros((n,256-W),BF16)
        row=lax.broadcasted_iota(jnp.int32,(16,n),0)
        lane=lax.broadcasted_iota(jnp.int32,(8,W),1)
        head_row=lax.broadcasted_iota(jnp.int32,(8,W),0)
        pick=jnp.where((lane>=head_row*HEAD)&(lane<head_row*HEAD+HEAD),1.0,0.0).astype(BF16)
        prod=dc_ref[...].astype(F32)*cf_ref[...]
        hi,mid,lo=thirds(prod)
        deltas=dot_t(pick,hi)+dot_t(pick,mid)+dot_t(pick,lo)
        stats=st_ref[...].T
        q_t=jnp.concatenate([q_ref[...],pad],axis=1).T
        d_t=jnp.concatenate([dc_ref[...],pad],axis=1).T
        def tail(x,first):
            hi,mid,lo=(v.astype(F32) for v in thirds(-x))
            z=jnp.where(row==1,hi,jnp.where(row==2,mid,jnp.where(row==3,lo,0.0)))
            return jnp.where(row==0,first,z).astype(BF16)
        rest=jnp.zeros((HEAD-16,n),BF16)
        for g in range(NH):
            cols=slice(g*HEAD,(g+1)*HEAD)
            for t,x,first,dst in ((q_t,stats,1.0,qt),(d_t,deltas,0.0,dct)):
                dst[g,:HEAD]=t[cols]
                dst[g,HEAD:HEAD+16]=tail(x[g:g+1],first)
                dst[g,HEAD+16:]=rest
            qn[g]=q_ref[:,cols]
            dcn[g]=dc_ref[:,cols]
        dqt[...]=jnp.zeros_like(dqt)
    key_tail=kb_ref[:,HEAD:]
    def head(g):
        k=kv_ref[:,g*HEAD:(g+1)*HEAD]
        ka=jnp.concatenate([k,key_tail],axis=1)
        va=jnp.concatenate([kv_ref[:,W+g*HEAD:W+(g+1)*HEAD],key_tail],axis=1)
        p=jnp.exp(dot(ka,qt[g]))
        dp=dot(va,dct[g])
        ds=(p*dp).astype(BF16)
        dv[g]=dot(p.astype(BF16),dcn[g])
        dk[g]=dot(ds,qn[g])
        dqt[g]=dqt[g]+t_dot(ka,ds)[:HEAD]
    for g in range(NH):
        @pl.when(h==g)
        def _(): head(g)
    @pl.when(h==NH-1)
    def _():
        dkv=jnp.concatenate([dk[g] for g in range(NH)]+[dv[g] for g in range(NH)],axis=1)
        @pl.when(j<nk//2)
        def _():
            sent_ref[...]=dkv.astype(BF16)
        @pl.when(j>=nk//2)
        def _():
            kept_ref[...]=dkv
    @pl.when((h==NH-1)&(j==nk-1))
    def _():
        for g in range(NH):
            dq_ref[:,g*HEAD:(g+1)*HEAD]=(dqt[g].T*0.125).astype(BF16)

def attend_backward(q,kv,kb,cf,st,dc,bit,bk=768):
    n,W=q.shape; L=kv.shape[0]; nk=L//bk; half=nk//2
    full=lambda a: pl.BlockSpec(a.shape,lambda j,h,b:(0,0))
    key=lambda j,h,b:(jnp.where(j<half,(1-b[0])*half+j,b[0]*half+j-half),0)
    return pl.pallas_call(partial(bwd_body,nk=nk),
        grid_spec=pltpu.PrefetchScalarGridSpec(
            num_scalar_prefetch=1,
            grid=(nk,NH),
            in_specs=[full(q),pl.BlockSpec((bk,2*W),key),pl.BlockSpec((bk,128),key),full(cf),full(st),full(dc)],
            out_specs=[pl.BlockSpec((n,W),lambda j,h,b:(0,0)),
                pl.BlockSpec((bk,2*W),lambda j,h,b:(jnp.minimum(j,half-1),0)),
                pl.BlockSpec((bk,2*W),lambda j,h,b:(jnp.maximum(j-half,0),0))],
            scratch_shapes=[pltpu.VMEM((NH,2*HEAD,n),BF16),pltpu.VMEM((NH,n,HEAD),BF16),pltpu.VMEM((NH,2*HEAD,n),BF16),pltpu.VMEM((NH,n,HEAD),BF16),
                pltpu.VMEM((NH,HEAD,n),F32),pltpu.VMEM((NH,bk,HEAD),F32),pltpu.VMEM((NH,bk,HEAD),F32)]),
        out_shape=[jax.ShapeDtypeStruct((n,W),BF16),jax.ShapeDtypeStruct((L//2,2*W),BF16),jax.ShapeDtypeStruct((L//2,2*W),F32)],
        name="attend_backward",
    )(bit,q,kv,kb,cf,st,dc)


def feed_grads_body(y_ref, dz_ref, a_ref, do_ref, out_ref, *, chips):
    width = y_ref.shape[1]
    r_in, r_out = width // chips, a_ref.shape[1] // chips
    half = chips // 2
    for j in range(2):
        grad = t_dot(y_ref[...], dz_ref[:, j * width : (j + 1) * width]).astype(BF16)
        for q in range(chips):
            out_ref[q, j * r_in : (j + 1) * r_in] = grad[q * r_in : (q + 1) * r_in]
        grad = t_dot(a_ref[:, j * width : (j + 1) * width], do_ref[...]).astype(BF16)
        for q in range(half):
            out_ref[j * half + q, 2 * r_in :] = grad[q * r_out : (q + 1) * r_out]


def feed_grads(y, dz, a, do, chips):
    width = y.shape[1]
    return pl.pallas_call(
        partial(feed_grads_body, chips=chips),
        out_shape=jax.ShapeDtypeStruct((chips, (2 * width + a.shape[1]) // chips, width), BF16),
        cost_estimate=pl.CostEstimate(
            flops=4 * width * y.shape[0] * dz.shape[1], transcendentals=0, bytes_accessed=10 * width * width * 2
        ),
        name="feed_grads",
    )(y, dz, a, do)


def other_grads_body(dz_ref, ctx_ref, da_ref, do_ref, vec_ref, out_ref, *, chips):
    width = da_ref.shape[1]
    r_ctx = ctx_ref.shape[1] // chips
    grad = t_dot(ctx_ref[...], da_ref[...]).astype(BF16)
    n = do_ref.shape[0]
    ones = jnp.ones((16, da_ref.shape[0]), BF16)
    sums = [dot(ones[:, :n], da_ref[:n])[:1], dot(ones[:, :n], do_ref[...])[:1]]
    sums += [dot(ones, dz_ref[:, j * width : (j + 1) * width])[:1] for j in range(2)]
    small = jnp.concatenate([vec_ref[...]] + sums, axis=0).astype(BF16)
    for q in range(chips):
        out_ref[q, :r_ctx] = grad[q * r_ctx : (q + 1) * r_ctx]
        out_ref[q, r_ctx:] = small


def other_grads(dz, ctx, da, do, vec, chips):
    width = da.shape[1]
    return pl.pallas_call(
        partial(other_grads_body, chips=chips),
        out_shape=jax.ShapeDtypeStruct((chips, ctx.shape[1] // chips + vec.shape[0] + 4, width), BF16),
        cost_estimate=pl.CostEstimate(
            flops=2 * width * ctx.shape[0] * ctx.shape[1], transcendentals=0, bytes_accessed=5 * width * width * 2
        ),
        name="other_grads",
    )(dz, ctx, da, do, vec)


def per_device(
    seq_size,
    grp_size,
    tokens,
    valid_len,
    query_weight,
    query_bias,
    key_weight,
    value_weight,
    value_bias,
    output_weight,
    output_bias,
    first_gain,
    first_shift,
    inner_weight,
    inner_bias,
    outer_weight,
    outer_bias,
    second_gain,
    second_shift,
    grad_out,
):
    bf16 = jnp.bfloat16
    rows, width = tokens.shape[1:]
    feed = inner_weight.shape[1]
    shard = query_weight.shape[0]
    HI, ZO, YO = seq_size // 2, seq_size // 4, 2
    extra_bits = [1 << b for b in range(2, log2_of(ZO))]
    part_bits = [1] + extra_bits
    me = lax.axis_index("seq")
    grp = lax.axis_index("grp")
    z1 = me // HI
    z0 = (me // ZO) % 2
    y0 = (me // YO) % 2
    head_group = 2 * z0 + y0
    my_part = me % 2 + 2 * ((me // 4) % max(ZO // 4, 1))
    n_parts = seq_size // 8

    def sflip(value, mask):
        return flip(value, "seq", seq_size, mask)

    chips = seq_size // 2
    x_mine = pick(tokens, z1)
    x_sent = pick(tokens, 1 - z1)
    half_width = width // 2
    x_theirs = sflip(x_sent, HI)
    x_pair = in_order(x_mine, x_theirs, z1)
    xa, xb = x_pair[:, :, :half_width], x_pair[:, :, half_width:]
    ra, rb = sflip(xa, YO), sflip(xb, ZO)
    xa, xb = in_order(xa, ra, y0), in_order(xb, rb, z0)
    ra, rb = sflip(xa, ZO), sflip(xb, YO)
    xa, xb = in_order(xa, ra, z0), in_order(xb, rb, y0)
    x_all = jnp.concatenate([xa.transpose(2, 0, 1, 3, 4), xb.transpose(2, 1, 0, 3, 4)], axis=-1)
    x_all = x_all.reshape(8 * rows, width)

    core = me % 2
    chips = seq_size // 2
    piece = feed // seq_size
    n_dev = grp_size * seq_size
    half_feed = feed // 2
    split = inner_weight.reshape(shard, chips, 2, piece)
    split = [split[:, :, i].reshape(shard, 2, width).transpose(1, 0, 2).reshape(2 * shard, width) for i in range(2)]
    near = jnp.concatenate([pick(split, 1 - core), output_weight], axis=0)
    far = sflip(near, 1)
    outer_far = lax.ppermute(
        outer_weight,
        ("grp", "seq"),
        [(d, d ^ (1 | grp_size) if d % 2 != (d // grp_size) % 2 else d) for d in range(n_dev)],
    )
    inner_pair = in_order(pick(split, core).reshape(2, shard, width), far[: 2 * shard].reshape(2, shard, width), core)
    packed = jnp.concatenate(
        [
            inner_pair.transpose(1, 0, 2, 3).reshape(4 * shard, width),
            in_order(output_weight, far[2 * shard :], core).reshape(2 * shard, width),
            outer_far,
        ],
        axis=0,
    )
    chip_groups = [[2 * q + i for q in range(chips)] for i in range(2)]
    gathered = lax.all_gather(packed, "seq", axis=0, tiled=False, axis_index_groups=chip_groups)
    first_end = 6 * shard
    gathered = [gathered]
    for b in range(log2_of(grp_size)):
        gathered += [flip(part, "grp", grp_size, 1 << b) for part in gathered]

    def gathered_rows(start, stop):
        parts = [x[:, start:stop] for x in gathered]
        stacks = {i: x[None] for i, x in enumerate(parts)}
        for b in range(log2_of(grp_size)):
            bit = (grp >> b) % 2
            merged = {}
            for i in range(len(stacks) // 2):
                low, high = stacks[2 * i], stacks[2 * i + 1]
                merged[i] = jnp.where(bit == 0, jnp.concatenate([low, high]), jnp.concatenate([high, low]))
            stacks = merged
        return stacks[0].reshape((-1,) + parts[0].shape[1:])

    smalls = jnp.concatenate(
        [query_bias, value_bias, output_bias, first_gain, first_shift, outer_bias, second_gain, second_shift, inner_bias]
    )
    small_rows = 32 - shard if shard == 24 else 8
    grouped = jnp.stack([query_weight, key_weight, value_weight]).reshape(3, shard, HEAD_GROUPS, GROUP_WIDTH)
    grouped = grouped.transpose(2, 1, 0, 3).reshape(HEAD_GROUPS, shard, 3 * GROUP_WIDTH)
    small_block = jnp.zeros((small_rows * 3 * GROUP_WIDTH,), bf16).at[: smalls.shape[0]].set(smalls)
    small_block = jnp.broadcast_to(small_block.reshape(1, small_rows, -1), (HEAD_GROUPS, small_rows, 3 * GROUP_WIDTH))
    grouped = jnp.concatenate([grouped, small_block], axis=1)
    grouped, _ = lax.optimization_barrier((grouped, x_theirs))

    def group_block(k):
        return lax.dynamic_index_in_dim(grouped, head_group ^ k, 0, keepdims=False)

    w0 = group_block(0)
    w1 = sflip(group_block(1), YO)
    w2 = sflip(group_block(2), ZO)
    w3 = sflip(group_block(3), ZO | YO)
    w_all = in_order(in_order(w0, w1, y0), in_order(w2, w3, y0), z0)
    w_all = in_order(w_all, sflip(w_all, HI), z1)
    names = ["z1", "z0", "y0"]
    for b in extra_bits:
        w_all = in_order(w_all, sflip(w_all, b), (me // b) % 2)
        names = ["e%d" % b] + names
    for b in range(log2_of(grp_size)):
        w_all = in_order(w_all, flip(w_all, "grp", grp_size, 1 << b), (grp >> b) % 2)
        names = ["g%d" % b] + names
    w_all = in_order(w_all, sflip(w_all, 1), me % 2)
    names = ["c"] + names
    wanted = ["g%d" % b for b in reversed(range(log2_of(grp_size)))] + ["z1", "z0"]
    wanted += ["e%d" % b for b in reversed(extra_bits)] + ["y0", "c"]
    n = len(names)
    w_all = w_all.transpose(*[names.index(w) for w in wanted], n, n + 1)
    w_all = w_all.reshape(grp_size * seq_size, shard + small_rows, 3 * GROUP_WIDTH)
    small_all = w_all[:, shard:].reshape(grp_size * seq_size, -1)[:, : smalls.shape[0]]
    vectors = [small_all[:, i * shard : (i + 1) * shard].reshape(-1).astype(jnp.float32) for i in range(8)]
    q_bias, v_bias, o_bias, gain1, shift1, out_bias, gain2, shift2 = vectors
    in_bias = small_all[:, 8 * shard :].reshape(-1).astype(jnp.float32)
    w_all = w_all[:, :shard].reshape(width, 3 * GROUP_WIDTH)

    def own_columns(vector):
        return lax.dynamic_slice_in_dim(vector, head_group * GROUP_WIDTH, GROUP_WIDTH)

    qkv_bias = jnp.concatenate([own_columns(q_bias), jnp.zeros((GROUP_WIDTH,), jnp.float32), own_columns(v_bias)])
    qkv = dot(x_all, w_all) + qkv_bias
    queries = (qkv[:, :GROUP_WIDTH] * score_scale).astype(bf16)
    kv = qkv[:, GROUP_WIDTH:].astype(bf16)[None]
    for b in part_bits:
        bit = (me // b) % 2
        theirs = sflip(kv, b)
        kv = jnp.where(bit == 0, jnp.concatenate([kv, theirs]), jnp.concatenate([theirs, kv]))
    kv = kv.reshape(-1, 2 * GROUP_WIDTH)

    part = jnp.arange(n_parts, dtype=jnp.int32)
    part_device = part % 2 + 4 * (part // 2)
    member = jnp.arange(8, dtype=jnp.int32)
    member_device = (member // 4) * HI + ((member // 2) % 2) * ZO + (member % 2) * YO
    device = part_device[:, None] + member_device[None, :]
    position = (device[:, :, None] * rows + jnp.arange(rows, dtype=jnp.int32)).reshape(-1)
    bias = jnp.where(position < pick(valid_len, z1), 0.0, masked_score)[:, None]
    lane = jnp.arange(128, dtype=jnp.int32)[None, :]
    key_tail = jnp.where(lane == HEAD, bias, jnp.where((lane > HEAD) & (lane < HEAD + 4), 1.0, 0.0)).astype(bf16)

    context, context_full, stats = attend_forward(queries, kv, key_tail)

    teams = [
        [a * HI + b * ZO + c * YO + q for a in range(2) for b in range(2) for c in range(2)]
        for q in [i % 2 + 4 * (i // 2) for i in range(n_parts)]
    ]

    def exchange(blocks):
        return lax.all_to_all(blocks, "seq", 0, 0, axis_index_groups=teams, tiled=True)

    context = exchange(context.reshape(8, rows, GROUP_WIDTH))
    context = context.reshape(2, HEAD_GROUPS, rows, GROUP_WIDTH).transpose(0, 2, 1, 3).reshape(2 * rows, width)

    inner_lo = gathered_rows(0, 2 * shard).reshape(width, width)
    inner_hi = gathered_rows(2 * shard, 4 * shard).reshape(width, width)
    output_all = gathered_rows(4 * shard, first_end).reshape(width, width)
    outer_all = gathered_rows(first_end, first_end + outer_weight.shape[0])
    outer_all = outer_all.reshape(-1, 2, grp_size // 2, outer_weight.shape[0], width)
    outer_all = outer_all.transpose(0, 2, 1, 3, 4).reshape(half_feed, width)

    in_bias = pick(in_bias.reshape(chips, 2, piece).transpose(1, 0, 2).reshape(2, half_feed), core)

    home = tokens.reshape(2 * rows, width)
    cotangent = grad_out.reshape(2 * rows, width)
    hidden_one = home.astype(jnp.float32) + dot(context, output_all) + o_bias
    norm_one, norm_back_one = jax.vjp(layer_norm, hidden_one, gain1, shift1)
    first_out = norm_one.astype(bf16)
    n_own = 2 * rows
    both_first = jnp.concatenate([first_out, sflip(first_out, 1)], axis=0)

    def gelu_pair(pre):
        full, back = jax.vjp(partial(jax.nn.gelu, approximate=False), pre)
        return full.astype(bf16), back(jnp.ones_like(pre))[0]

    inner_all = jnp.concatenate([inner_lo, inner_hi], axis=1)
    active, slope = gelu_pair(dot(both_first, inner_all) + in_bias)
    outer_part = dot(active, outer_all)
    outer_sum = outer_part[:n_own] + sflip(outer_part[n_own:].astype(bf16), 1).astype(jnp.float32)
    hidden_two = first_out.astype(jnp.float32) + outer_sum + out_bias
    layer_out, norm_back_two = jax.vjp(layer_norm, hidden_two, gain2, shift2)
    dhidden_two, dsecond_gain, dsecond_shift = norm_back_two(cotangent.astype(jnp.float32))
    douter = dhidden_two.astype(bf16)
    both_douter = jnp.concatenate([douter, sflip(douter, 1)], axis=0)

    def over_chips(blocks):
        return lax.psum_scatter(blocks, "seq", scatter_dimension=0, tiled=False, axis_index_groups=chip_groups)

    def over_groups(blocks):
        for b in range(log2_of(grp_size)):
            blocks = (blocks.astype(jnp.float32) + flip(blocks, "grp", grp_size, 1 << b).astype(jnp.float32)).astype(bf16)
        return blocks

    dinner = (dot_t(both_douter, outer_all) * slope).astype(bf16)
    dfirst_part = dot_t(dinner, inner_all)
    dfirst = dhidden_two + dfirst_part[:n_own] + sflip(dfirst_part[n_own:].astype(bf16), 1).astype(jnp.float32)
    dhidden_one, dfirst_gain, dfirst_shift = norm_back_one(dfirst)
    dattend = dhidden_one.astype(bf16)
    dcontext = dot_t(dattend, output_all).astype(bf16)
    dcontext = dcontext.reshape(2, rows, HEAD_GROUPS, GROUP_WIDTH).transpose(0, 2, 1, 3)
    dcontext, late_context = lax.optimization_barrier((dcontext.reshape(8, rows, GROUP_WIDTH), context))
    dcontext = exchange(dcontext).reshape(8 * rows, GROUP_WIDTH)

    out_rows = width // seq_size
    ctx_split = late_context.reshape(n_own, chips, 2, out_rows)
    ctx_split = [ctx_split[:, :, i].reshape(n_own, width // 2) for i in range(2)]
    both_ctx = jnp.concatenate([pick(ctx_split, core), sflip(pick(ctx_split, 1 - core), 1)], axis=0)
    both_dattend = jnp.concatenate([dattend, sflip(dattend, 1)], axis=0)
    vectors = jnp.stack([dfirst_gain, dfirst_shift, dsecond_gain, dsecond_shift])
    other_blocks = other_grads(dinner, both_ctx, both_dattend, douter, vectors, chips)
    feed_blocks = feed_grads(both_first, dinner, active, both_douter, chips)
    feed_blocks, other_blocks, dcontext = lax.optimization_barrier((feed_blocks, other_blocks, dcontext))
    feed_sums = over_chips(feed_blocks)

    def halve(low, high, bit, mask):
        sent = jnp.where(bit == 0, high, low).astype(bf16)
        return jnp.where(bit == 0, low, high) + sflip(sent, mask).astype(jnp.float32)

    def halve_other(blocks, b):
        pairs = blocks.reshape((-1, 2) + blocks.shape[1:])
        return halve(pairs[:, 0], pairs[:, 1], (me >> (b + 1)) % 2, 2 << b)

    last = part_bits[-1]
    dqueries, sent, kept = attend_backward(
        queries, kv, key_tail, context_full, stats, dcontext, ((me // last) % 2).astype(jnp.int32).reshape(1)
    )
    dkv = (kept + sflip(sent, last).astype(jnp.float32)).reshape(n_parts // 2, 8 * rows, 2 * GROUP_WIDTH)
    for b in reversed(part_bits[:-1]):
        bit = (me // b) % 2
        n_now = dkv.shape[0] // 2
        low, high = dkv[:n_now], dkv[n_now:]
        sent = jnp.where(bit == 0, high, low).astype(bf16)
        dkv = jnp.where(bit == 0, low, high) + sflip(sent, b).astype(jnp.float32)
    dqkv = jnp.concatenate([dqueries, dkv[0].astype(bf16)], axis=1)
    other_sums = halve_other(other_blocks, 0)

    dx, late_x = lax.optimization_barrier((dot_t(dqkv, w_all).reshape(2, 2, 2, rows, width), x_all))
    da, db = dx[..., :half_width], dx[..., half_width:]

    da = halve(da[:, :, 0], da[:, :, 1], y0, YO)
    db = halve(db[:, 0], db[:, 1], z0, ZO)
    other_sums = halve_other(other_sums, 1)
    da, db, other_sums, feed_sums = lax.optimization_barrier((da, db, other_sums, feed_sums))
    feed_sums = over_groups(feed_sums)
    da = halve(da[:, 0], da[:, 1], z0, ZO)
    db = halve(db[:, 0], db[:, 1], y0, YO)
    dx = jnp.concatenate([da, db], axis=-1)
    dx, other_sums = lax.optimization_barrier((dx, other_sums))
    mine = pick(dx, z1)
    theirs = sflip(pick(dx, 1 - z1).astype(bf16), HI).astype(jnp.float32)
    for b in range(2, log2_of(chips)):
        other_sums = halve_other(other_sums, b)
    other_sums = over_groups(other_sums[0].astype(bf16))
    r1 = 4 * out_rows
    inner_grad = feed_sums[:r1].reshape(2, 2, out_rows, width)
    inner_grad = [inner_grad[:, i] for i in range(2)]
    far = sflip(jnp.concatenate([pick(inner_grad, 1 - core).reshape(2 * out_rows, width), other_sums[out_rows:]], axis=0), 1)
    dinner_weight = in_order(pick(inner_grad, core), far[: 2 * out_rows].reshape(2, out_rows, width), core)
    dinner_weight = dinner_weight.transpose(2, 0, 1, 3).reshape(out_rows, 2, chips, piece).transpose(0, 2, 1, 3)
    dinner_weight = dinner_weight.reshape(out_rows, feed).astype(jnp.float32)
    douter_weight = feed_sums[r1:].astype(jnp.float32)
    doutput_weight = other_sums[:out_rows].astype(jnp.float32)
    small = other_sums[out_rows:].astype(jnp.float32)
    both = lax.dynamic_slice_in_dim(small + far[2 * out_rows :].astype(jnp.float32), me * out_rows, out_rows, axis=1)
    dfirst_gain, dfirst_shift, dsecond_gain, dsecond_shift, doutput_bias, douter_bias = (both[i] for i in range(6))
    dinner_bias = lax.dynamic_slice_in_dim(small[6:8].reshape(half_feed), (me // 2) * piece, piece)

    dw = t_dot(x_all, dqkv)
    dbias = column_sums(dqkv)
    dw = dw.reshape(seq_size, out_rows, 3 * GROUP_WIDTH)
    dw = jnp.concatenate([dw, jnp.broadcast_to(dbias, (seq_size, 8, 3 * GROUP_WIDTH))], axis=1)
    block = dw.shape[1]
    n_extra = 1 << len(extra_bits)
    dw = dw.reshape(2, 2, 2, n_extra, 2, 1, block, 3 * GROUP_WIDTH)[:, :, :, :, :, 0]
    dw = dw.reshape(2, 2, n_extra, 2, 2, block, 3 * GROUP_WIDTH)
    dw = halve(dw[:, :, :, :, 0], dw[:, :, :, :, 1], me % 2, 1)
    for b in reversed(extra_bits):
        m = dw.shape[2] // 2
        dw = halve(dw[:, :, :m], dw[:, :, m:], (me // b) % 2, b)
    dw = dw[:, :, 0]
    dw = halve(dw[0], dw[1], z1, HI)
    for b in range(log2_of(grp_size)):
        dw = dw + flip(dw.astype(bf16), "grp", grp_size, 1 << b).astype(jnp.float32)
    dw = dw.astype(bf16).reshape(HEAD_GROUPS, block, 3 * GROUP_WIDTH)

    def row_block(k):
        return lax.dynamic_index_in_dim(dw, head_group ^ k, 0, keepdims=False)

    w0 = row_block(0)
    w1 = sflip(row_block(1), YO)
    w2 = sflip(row_block(2), ZO)
    w3 = sflip(row_block(3), ZO | YO)
    w0, w1, w2, w3, mine = lax.optimization_barrier((w0, w1, w2, w3, mine))
    dw = in_order(in_order(w0, w1, y0), in_order(w2, w3, y0), z0).reshape(HEAD_GROUPS, block, 3, GROUP_WIDTH)
    dw = dw.astype(jnp.float32).transpose(2, 1, 0, 3).reshape(3, block, width)
    dtokens = dhidden_one.reshape(2, rows, width) + in_order(mine, theirs, z1)
    dquery_weight, dkey_weight, dvalue_weight = dw[0, :out_rows], dw[1, :out_rows], dw[2, :out_rows]
    dquery_bias = lax.dynamic_slice_in_dim(dw[0, out_rows], me * out_rows, out_rows)
    dvalue_bias = lax.dynamic_slice_in_dim(dw[2, out_rows], me * out_rows, out_rows)

    return (
        layer_out.astype(bf16).reshape(2, rows, width),
        dtokens.astype(bf16),
        dquery_weight,
        dquery_bias,
        dkey_weight,
        dvalue_weight,
        dvalue_bias,
        doutput_weight,
        doutput_bias,
        dfirst_gain,
        dfirst_shift,
        dinner_weight,
        dinner_bias,
        douter_weight,
        douter_bias,
        dsecond_gain,
        dsecond_shift,
    )


def solution(mesh):
    in_specs = (
        P("grp", "seq", None),
        P("grp"),
        P(("grp", "seq"), None),
        P(("grp", "seq")),
        P(("grp", "seq"), None),
        P(("grp", "seq"), None),
        P(("grp", "seq")),
        P(("grp", "seq"), None),
        P(("grp", "seq")),
        P(("grp", "seq")),
        P(("grp", "seq")),
        P(("grp", "seq"), None),
        P(("grp", "seq")),
        P(("grp", "seq"), None),
        P(("grp", "seq")),
        P(("grp", "seq")),
        P(("grp", "seq")),
        P("grp", "seq", None),
    )
    out_specs = (
        P("grp", "seq", None),
        P("grp", "seq", None),
        P("seq", None),
        P("seq"),
        P("seq", None),
        P("seq", None),
        P("seq"),
        P("seq", None),
        P("seq"),
        P("seq"),
        P("seq"),
        P("seq", None),
        P("seq"),
        P("seq", None),
        P("seq"),
        P("seq"),
        P("seq"),
    )
    body = partial(per_device, mesh.shape["seq"], mesh.shape["grp"])
    return jax.shard_map(
        body, mesh=mesh, in_specs=in_specs, out_specs=out_specs, check_vma=False
    )
```

```python
from functools import partial

import jax
import jax.numpy as jnp
from jax import lax
from jax.experimental import pallas as pl
from jax.experimental.pallas import tpu as pltpu
from jax.sharding import PartitionSpec as P

HEADS = 12
HEAD = 64
HEAD_GROUPS = 4
GROUP_WIDTH = HEADS * HEAD // HEAD_GROUPS
NH = HEADS // HEAD_GROUPS
BF16 = jnp.bfloat16
F32 = jnp.float32

score_scale = 0.125
epsilon = 1e-12
masked_score = -1e30


def log2_of(size):
    return size.bit_length() - 1


def flip(value, axis, size, mask):
    return lax.ppermute(value, axis, [(i, i ^ mask) for i in range(size)])


def in_order(mine, theirs, bit):
    return jnp.where(bit == 0, jnp.stack([mine, theirs]), jnp.stack([theirs, mine]))


def pick(pair, bit):
    return jnp.where(bit == 0, pair[0], pair[1])


def layer_norm(hidden, norm_gain, norm_shift):
    centred = hidden - jnp.mean(hidden, axis=-1, keepdims=True)
    spread = jnp.mean(centred * centred, axis=-1, keepdims=True)
    return centred * lax.rsqrt(spread + epsilon) * norm_gain + norm_shift


def dot(left, right):
    return jnp.dot(left, right, preferred_element_type=jnp.float32)


def dot_t(left, right):
    return lax.dot_general(left, right, (((1,), (1,)), ((), ())), preferred_element_type=jnp.float32)


def t_dot(left, right):
    return lax.dot_general(left, right, (((0,), (0,)), ((), ())), preferred_element_type=jnp.float32)


def column_sums(matrix):
    return jnp.sum(matrix.astype(jnp.float32), axis=0)


def thirds(x):
    hi=x.astype(BF16)
    r=x-hi.astype(F32)
    mid=r.astype(BF16)
    lo=(r-mid.astype(F32)).astype(BF16)
    return hi,mid,lo

def fwd_body(q_ref, kv_ref, kb_ref, c_ref, cf_ref, st_ref, kt, va, oacc, lacc, *, bq):
    i=pl.program_id(0); h=pl.program_id(1)
    W=NH*HEAD
    @pl.when((i==0)&(h==0))
    def _():
        tail=kb_ref[:,HEAD:]
        for g in range(NH):
            ka=jnp.concatenate([kv_ref[:,g*HEAD:(g+1)*HEAD],tail],axis=1)
            kt[g]=ka.T
            va[g]=jnp.concatenate([kv_ref[:,W+g*HEAD:W+(g+1)*HEAD],tail],axis=1)
    one=jnp.where(lax.broadcasted_iota(jnp.int32,(bq,HEAD),1)==0,1.0,0.0).astype(BF16)
    def head(g):
        qa=jnp.concatenate([q_ref[:,g*HEAD:(g+1)*HEAD],one],axis=1)
        s=dot(qa,kt[g])
        m=jnp.max(s,axis=1,keepdims=True)
        p=jnp.exp(s-m).astype(BF16)
        o=dot(p,va[g])
        l=o[:,HEAD+1:HEAD+2]
        oacc[g]=o/l
        lacc[g]=jnp.broadcast_to(m+jnp.log(l),(bq,128))
    for g in range(NH):
        @pl.when(h==g)
        def _(): head(g)
    @pl.when(h==NH-1)
    def _():
        c=jnp.concatenate([oacc[g][:,:HEAD] for g in range(NH)],axis=1)
        c_ref[...]=c.astype(BF16)
        cf_ref[...]=c
        lane=lax.broadcasted_iota(jnp.int32,(bq,128),1)
        st=lacc[0]
        for g in range(1,NH): st=jnp.where(lane==g,lacc[g],st)
        st_ref[...]=st

def attend_forward(q,kv,kb,bq=256):
    n,W=q.shape; L=kv.shape[0]
    return pl.pallas_call(partial(fwd_body,bq=bq),
        grid=(n//bq,NH),
        in_specs=[pl.BlockSpec((bq,W),lambda i,h:(i,0)),pl.BlockSpec((L,2*W),lambda i,h:(0,0)),pl.BlockSpec((L,128),lambda i,h:(0,0))],
        out_specs=[pl.BlockSpec((bq,W),lambda i,h:(i,0)),pl.BlockSpec((bq,W),lambda i,h:(i,0)),pl.BlockSpec((bq,128),lambda i,h:(i,0))],
        out_shape=[jax.ShapeDtypeStruct((n,W),BF16),jax.ShapeDtypeStruct((n,W),F32),jax.ShapeDtypeStruct((n,128),F32)],
        scratch_shapes=[pltpu.VMEM((NH,128,L),BF16),pltpu.VMEM((NH,L,128),BF16),pltpu.VMEM((NH,bq,128),F32),pltpu.VMEM((NH,bq,128),F32)],
        cost_estimate=pl.CostEstimate(flops=16*n*L*W, transcendentals=NH*n*L, bytes_accessed=4*n*L),
        name="attend_forward",
    )(q,kv,kb)

def bwd_body(bit_ref, q_ref, kv_ref, kb_ref, cf_ref, st_ref, dc_ref, dq_ref, sent_ref, kept_ref, qt, qn, dct, dcn, dqt, dk, dv, *, nk):
    j=pl.program_id(0); h=pl.program_id(1)
    W=NH*HEAD
    n=q_ref.shape[0]
    @pl.when((j==0)&(h==0))
    def _():
        pad=jnp.zeros((n,256-W),BF16)
        row=lax.broadcasted_iota(jnp.int32,(16,n),0)
        lane=lax.broadcasted_iota(jnp.int32,(8,W),1)
        head_row=lax.broadcasted_iota(jnp.int32,(8,W),0)
        pick=jnp.where((lane>=head_row*HEAD)&(lane<head_row*HEAD+HEAD),1.0,0.0).astype(BF16)
        prod=dc_ref[...].astype(F32)*cf_ref[...]
        hi,mid,lo=thirds(prod)
        deltas=dot_t(pick,hi)+dot_t(pick,mid)+dot_t(pick,lo)
        stats=st_ref[...].T
        q_t=jnp.concatenate([q_ref[...],pad],axis=1).T
        d_t=jnp.concatenate([dc_ref[...],pad],axis=1).T
        def tail(x,first):
            hi,mid,lo=(v.astype(F32) for v in thirds(-x))
            z=jnp.where(row==1,hi,jnp.where(row==2,mid,jnp.where(row==3,lo,0.0)))
            return jnp.where(row==0,first,z).astype(BF16)
        rest=jnp.zeros((HEAD-16,n),BF16)
        for g in range(NH):
            cols=slice(g*HEAD,(g+1)*HEAD)
            for t,x,first,dst in ((q_t,stats,1.0,qt),(d_t,deltas,0.0,dct)):
                dst[g,:HEAD]=t[cols]
                dst[g,HEAD:HEAD+16]=tail(x[g:g+1],first)
                dst[g,HEAD+16:]=rest
            qn[g]=q_ref[:,cols]
            dcn[g]=dc_ref[:,cols]
        dqt[...]=jnp.zeros_like(dqt)
    key_tail=kb_ref[:,HEAD:]
    def head(g):
        k=kv_ref[:,g*HEAD:(g+1)*HEAD]
        ka=jnp.concatenate([k,key_tail],axis=1)
        va=jnp.concatenate([kv_ref[:,W+g*HEAD:W+(g+1)*HEAD],key_tail],axis=1)
        p=jnp.exp(dot(ka,qt[g]))
        dp=dot(va,dct[g])
        ds=(p*dp).astype(BF16)
        dv[g]=dot(p.astype(BF16),dcn[g])
        dk[g]=dot(ds,qn[g])
        dqt[g]=dqt[g]+t_dot(ka,ds)[:HEAD]
    for g in range(NH):
        @pl.when(h==g)
        def _(): head(g)
    @pl.when(h==NH-1)
    def _():
        dkv=jnp.concatenate([dk[g] for g in range(NH)]+[dv[g] for g in range(NH)],axis=1)
        @pl.when(j<nk//2)
        def _():
            sent_ref[...]=dkv.astype(BF16)
        @pl.when(j>=nk//2)
        def _():
            kept_ref[...]=dkv
    @pl.when((h==NH-1)&(j==nk-1))
    def _():
        for g in range(NH):
            dq_ref[:,g*HEAD:(g+1)*HEAD]=(dqt[g].T*0.125).astype(BF16)

def attend_backward(q,kv,kb,cf,st,dc,bit,bk=768):
    n,W=q.shape; L=kv.shape[0]; nk=L//bk; half=nk//2
    full=lambda a: pl.BlockSpec(a.shape,lambda j,h,b:(0,0))
    key=lambda j,h,b:(jnp.where(j<half,(1-b[0])*half+j,b[0]*half+j-half),0)
    return pl.pallas_call(partial(bwd_body,nk=nk),
        grid_spec=pltpu.PrefetchScalarGridSpec(
            num_scalar_prefetch=1,
            grid=(nk,NH),
            in_specs=[full(q),pl.BlockSpec((bk,2*W),key),pl.BlockSpec((bk,128),key),full(cf),full(st),full(dc)],
            out_specs=[pl.BlockSpec((n,W),lambda j,h,b:(0,0)),
                pl.BlockSpec((bk,2*W),lambda j,h,b:(jnp.minimum(j,half-1),0)),
                pl.BlockSpec((bk,2*W),lambda j,h,b:(jnp.maximum(j-half,0),0))],
            scratch_shapes=[pltpu.VMEM((NH,2*HEAD,n),BF16),pltpu.VMEM((NH,n,HEAD),BF16),pltpu.VMEM((NH,2*HEAD,n),BF16),pltpu.VMEM((NH,n,HEAD),BF16),
                pltpu.VMEM((NH,HEAD,n),F32),pltpu.VMEM((NH,bk,HEAD),F32),pltpu.VMEM((NH,bk,HEAD),F32)]),
        out_shape=[jax.ShapeDtypeStruct((n,W),BF16),jax.ShapeDtypeStruct((L//2,2*W),BF16),jax.ShapeDtypeStruct((L//2,2*W),F32)],
        name="attend_backward",
    )(bit,q,kv,kb,cf,st,dc)


def feed_grads_body(y_ref, dz_ref, a_ref, do_ref, out_ref, *, chips):
    width = y_ref.shape[1]
    r_in, r_out = width // chips, a_ref.shape[1] // chips
    half = chips // 2
    for j in range(2):
        grad = t_dot(y_ref[...], dz_ref[:, j * width : (j + 1) * width]).astype(BF16)
        for q in range(chips):
            out_ref[q, j * r_in : (j + 1) * r_in] = grad[q * r_in : (q + 1) * r_in]
        grad = t_dot(a_ref[:, j * width : (j + 1) * width], do_ref[...]).astype(BF16)
        for q in range(half):
            out_ref[j * half + q, 2 * r_in :] = grad[q * r_out : (q + 1) * r_out]


def feed_grads(y, dz, a, do, chips):
    width = y.shape[1]
    return pl.pallas_call(
        partial(feed_grads_body, chips=chips),
        out_shape=jax.ShapeDtypeStruct((chips, (2 * width + a.shape[1]) // chips, width), BF16),
        cost_estimate=pl.CostEstimate(
            flops=4 * width * y.shape[0] * dz.shape[1], transcendentals=0, bytes_accessed=10 * width * width * 2
        ),
        name="feed_grads",
    )(y, dz, a, do)


def other_grads_body(dz_ref, ctx_ref, da_ref, do_ref, vec_ref, out_ref, *, chips):
    width = da_ref.shape[1]
    r_ctx = ctx_ref.shape[1] // chips
    grad = t_dot(ctx_ref[...], da_ref[...]).astype(BF16)
    n = do_ref.shape[0]
    ones = jnp.ones((16, da_ref.shape[0]), BF16)
    sums = [dot(ones[:, :n], da_ref[:n])[:1], dot(ones[:, :n], do_ref[...])[:1]]
    sums += [dot(ones, dz_ref[:, j * width : (j + 1) * width])[:1] for j in range(2)]
    small = jnp.concatenate([vec_ref[...]] + sums, axis=0).astype(BF16)
    for q in range(chips):
        out_ref[q, :r_ctx] = grad[q * r_ctx : (q + 1) * r_ctx]
        out_ref[q, r_ctx:] = small


def other_grads(dz, ctx, da, do, vec, chips):
    width = da.shape[1]
    return pl.pallas_call(
        partial(other_grads_body, chips=chips),
        out_shape=jax.ShapeDtypeStruct((chips, ctx.shape[1] // chips + vec.shape[0] + 4, width), BF16),
        cost_estimate=pl.CostEstimate(
            flops=2 * width * ctx.shape[0] * ctx.shape[1], transcendentals=0, bytes_accessed=5 * width * width * 2
        ),
        name="other_grads",
    )(dz, ctx, da, do, vec)


def per_device(
    seq_size,
    grp_size,
    tokens,
    valid_len,
    query_weight,
    query_bias,
    key_weight,
    value_weight,
    value_bias,
    output_weight,
    output_bias,
    first_gain,
    first_shift,
    inner_weight,
    inner_bias,
    outer_weight,
    outer_bias,
    second_gain,
    second_shift,
    grad_out,
):
    bf16 = jnp.bfloat16
    rows, width = tokens.shape[1:]
    feed = inner_weight.shape[1]
    shard = query_weight.shape[0]
    HI, ZO, YO = seq_size // 2, seq_size // 4, 2
    extra_bits = [1 << b for b in range(2, log2_of(ZO))]
    part_bits = [1] + extra_bits
    me = lax.axis_index("seq")
    grp = lax.axis_index("grp")
    z1 = me // HI
    z0 = (me // ZO) % 2
    y0 = (me // YO) % 2
    head_group = 2 * z0 + y0
    my_part = me % 2 + 2 * ((me // 4) % max(ZO // 4, 1))
    n_parts = seq_size // 8

    def sflip(value, mask):
        return flip(value, "seq", seq_size, mask)

    chips = seq_size // 2
    x_mine = pick(tokens, z1)
    x_sent = pick(tokens, 1 - z1)
    half_width = width // 2
    x_theirs = sflip(x_sent, HI)
    x_pair = in_order(x_mine, x_theirs, z1)
    xa, xb = x_pair[:, :, :half_width], x_pair[:, :, half_width:]
    ra, rb = sflip(xa, YO), sflip(xb, ZO)
    xa, xb = in_order(xa, ra, y0), in_order(xb, rb, z0)
    ra, rb = sflip(xa, ZO), sflip(xb, YO)
    xa, xb = in_order(xa, ra, z0), in_order(xb, rb, y0)
    x_all = jnp.concatenate([xa.transpose(2, 0, 1, 3, 4), xb.transpose(2, 1, 0, 3, 4)], axis=-1)
    x_all = x_all.reshape(8 * rows, width)

    core = me % 2
    chips = seq_size // 2
    piece = feed // seq_size
    n_dev = grp_size * seq_size
    half_feed = feed // 2
    split = inner_weight.reshape(shard, chips, 2, piece)
    split = [split[:, :, i].reshape(shard, 2, width).transpose(1, 0, 2).reshape(2 * shard, width) for i in range(2)]
    near = jnp.concatenate([pick(split, 1 - core), output_weight], axis=0)
    far = sflip(near, 1)
    outer_far = lax.ppermute(
        outer_weight,
        ("grp", "seq"),
        [(d, d ^ (1 | grp_size) if d % 2 != (d // grp_size) % 2 else d) for d in range(n_dev)],
    )
    inner_pair = in_order(pick(split, core).reshape(2, shard, width), far[: 2 * shard].reshape(2, shard, width), core)
    packed = jnp.concatenate(
        [
            inner_pair.transpose(1, 0, 2, 3).reshape(4 * shard, width),
            in_order(output_weight, far[2 * shard :], core).reshape(2 * shard, width),
            outer_far,
        ],
        axis=0,
    )
    chip_groups = [[2 * q + i for q in range(chips)] for i in range(2)]
    gathered = lax.all_gather(packed, "seq", axis=0, tiled=False, axis_index_groups=chip_groups)
    first_end = 6 * shard
    gathered = [gathered]
    for b in range(log2_of(grp_size)):
        gathered += [flip(part, "grp", grp_size, 1 << b) for part in gathered]

    def gathered_rows(start, stop):
        parts = [x[:, start:stop] for x in gathered]
        stacks = {i: x[None] for i, x in enumerate(parts)}
        for b in range(log2_of(grp_size)):
            bit = (grp >> b) % 2
            merged = {}
            for i in range(len(stacks) // 2):
                low, high = stacks[2 * i], stacks[2 * i + 1]
                merged[i] = jnp.where(bit == 0, jnp.concatenate([low, high]), jnp.concatenate([high, low]))
            stacks = merged
        return stacks[0].reshape((-1,) + parts[0].shape[1:])

    smalls = jnp.concatenate(
        [query_bias, value_bias, output_bias, first_gain, first_shift, outer_bias, second_gain, second_shift, inner_bias]
    )
    small_rows = 32 - shard if shard == 24 else 8
    grouped = jnp.stack([query_weight, key_weight, value_weight]).reshape(3, shard, HEAD_GROUPS, GROUP_WIDTH)
    grouped = grouped.transpose(2, 1, 0, 3).reshape(HEAD_GROUPS, shard, 3 * GROUP_WIDTH)
    small_block = jnp.zeros((small_rows * 3 * GROUP_WIDTH,), bf16).at[: smalls.shape[0]].set(smalls)
    small_block = jnp.broadcast_to(small_block.reshape(1, small_rows, -1), (HEAD_GROUPS, small_rows, 3 * GROUP_WIDTH))
    grouped = jnp.concatenate([grouped, small_block], axis=1)
    grouped, _ = lax.optimization_barrier((grouped, x_theirs))

    def group_block(k):
        return lax.dynamic_index_in_dim(grouped, head_group ^ k, 0, keepdims=False)

    w0 = group_block(0)
    w1 = sflip(group_block(1), YO)
    w2 = sflip(group_block(2), ZO)
    w3 = sflip(group_block(3), ZO | YO)
    w_all = in_order(in_order(w0, w1, y0), in_order(w2, w3, y0), z0)
    w_all = in_order(w_all, sflip(w_all, HI), z1)
    names = ["z1", "z0", "y0"]
    for b in extra_bits:
        w_all = in_order(w_all, sflip(w_all, b), (me // b) % 2)
        names = ["e%d" % b] + names
    for b in range(log2_of(grp_size)):
        w_all = in_order(w_all, flip(w_all, "grp", grp_size, 1 << b), (grp >> b) % 2)
        names = ["g%d" % b] + names
    w_all = in_order(w_all, sflip(w_all, 1), me % 2)
    names = ["c"] + names
    wanted = ["g%d" % b for b in reversed(range(log2_of(grp_size)))] + ["z1", "z0"]
    wanted += ["e%d" % b for b in reversed(extra_bits)] + ["y0", "c"]
    n = len(names)
    w_all = w_all.transpose(*[names.index(w) for w in wanted], n, n + 1)
    w_all = w_all.reshape(grp_size * seq_size, shard + small_rows, 3 * GROUP_WIDTH)
    small_all = w_all[:, shard:].reshape(grp_size * seq_size, -1)[:, : smalls.shape[0]]
    vectors = [small_all[:, i * shard : (i + 1) * shard].reshape(-1).astype(jnp.float32) for i in range(8)]
    q_bias, v_bias, o_bias, gain1, shift1, out_bias, gain2, shift2 = vectors
    in_bias = small_all[:, 8 * shard :].reshape(-1).astype(jnp.float32)
    w_all = w_all[:, :shard].reshape(width, 3 * GROUP_WIDTH)

    def own_columns(vector):
        return lax.dynamic_slice_in_dim(vector, head_group * GROUP_WIDTH, GROUP_WIDTH)

    qkv_bias = jnp.concatenate([own_columns(q_bias), jnp.zeros((GROUP_WIDTH,), jnp.float32), own_columns(v_bias)])
    qkv = dot(x_all, w_all) + qkv_bias
    queries = (qkv[:, :GROUP_WIDTH] * score_scale).astype(bf16)
    kv = qkv[:, GROUP_WIDTH:].astype(bf16)[None]
    for b in part_bits:
        bit = (me // b) % 2
        theirs = sflip(kv, b)
        kv = jnp.where(bit == 0, jnp.concatenate([kv, theirs]), jnp.concatenate([theirs, kv]))
    kv = kv.reshape(-1, 2 * GROUP_WIDTH)

    part = jnp.arange(n_parts, dtype=jnp.int32)
    part_device = part % 2 + 4 * (part // 2)
    member = jnp.arange(8, dtype=jnp.int32)
    member_device = (member // 4) * HI + ((member // 2) % 2) * ZO + (member % 2) * YO
    device = part_device[:, None] + member_device[None, :]
    position = (device[:, :, None] * rows + jnp.arange(rows, dtype=jnp.int32)).reshape(-1)
    bias = jnp.where(position < pick(valid_len, z1), 0.0, masked_score)[:, None]
    lane = jnp.arange(128, dtype=jnp.int32)[None, :]
    key_tail = jnp.where(lane == HEAD, bias, jnp.where((lane > HEAD) & (lane < HEAD + 4), 1.0, 0.0)).astype(bf16)

    context, context_full, stats = attend_forward(queries, kv, key_tail)

    teams = [
        [a * HI + b * ZO + c * YO + q for a in range(2) for b in range(2) for c in range(2)]
        for q in [i % 2 + 4 * (i // 2) for i in range(n_parts)]
    ]

    def exchange(blocks):
        return lax.all_to_all(blocks, "seq", 0, 0, axis_index_groups=teams, tiled=True)

    context = exchange(context.reshape(8, rows, GROUP_WIDTH))
    context = context.reshape(2, HEAD_GROUPS, rows, GROUP_WIDTH).transpose(0, 2, 1, 3).reshape(2 * rows, width)

    inner_lo = gathered_rows(0, 2 * shard).reshape(width, width)
    inner_hi = gathered_rows(2 * shard, 4 * shard).reshape(width, width)
    output_all = gathered_rows(4 * shard, first_end).reshape(width, width)
    outer_all = gathered_rows(first_end, first_end + outer_weight.shape[0])
    outer_all = outer_all.reshape(-1, 2, grp_size // 2, outer_weight.shape[0], width)
    outer_all = outer_all.transpose(0, 2, 1, 3, 4).reshape(half_feed, width)

    in_bias = pick(in_bias.reshape(chips, 2, piece).transpose(1, 0, 2).reshape(2, half_feed), core)

    home = tokens.reshape(2 * rows, width)
    cotangent = grad_out.reshape(2 * rows, width)
    hidden_one = home.astype(jnp.float32) + dot(context, output_all) + o_bias
    norm_one, norm_back_one = jax.vjp(layer_norm, hidden_one, gain1, shift1)
    first_out = norm_one.astype(bf16)
    n_own = 2 * rows
    both_first = jnp.concatenate([first_out, sflip(first_out, 1)], axis=0)

    def gelu_pair(pre):
        full, back = jax.vjp(partial(jax.nn.gelu, approximate=False), pre)
        return full.astype(bf16), back(jnp.ones_like(pre))[0]

    inner_all = jnp.concatenate([inner_lo, inner_hi], axis=1)
    active, slope = gelu_pair(dot(both_first, inner_all) + in_bias)
    outer_part = dot(active, outer_all)
    outer_sum = outer_part[:n_own] + sflip(outer_part[n_own:].astype(bf16), 1).astype(jnp.float32)
    hidden_two = first_out.astype(jnp.float32) + outer_sum + out_bias
    layer_out, norm_back_two = jax.vjp(layer_norm, hidden_two, gain2, shift2)
    dhidden_two, dsecond_gain, dsecond_shift = norm_back_two(cotangent.astype(jnp.float32))
    douter = dhidden_two.astype(bf16)
    both_douter = jnp.concatenate([douter, sflip(douter, 1)], axis=0)

    def over_chips(blocks):
        return lax.psum_scatter(blocks, "seq", scatter_dimension=0, tiled=False, axis_index_groups=chip_groups)

    def over_groups(blocks):
        for b in range(log2_of(grp_size)):
            blocks = (blocks.astype(jnp.float32) + flip(blocks, "grp", grp_size, 1 << b).astype(jnp.float32)).astype(bf16)
        return blocks

    dinner = (dot_t(both_douter, outer_all) * slope).astype(bf16)
    dfirst_part = dot_t(dinner, inner_all)
    dfirst = dhidden_two + dfirst_part[:n_own] + sflip(dfirst_part[n_own:].astype(bf16), 1).astype(jnp.float32)
    dhidden_one, dfirst_gain, dfirst_shift = norm_back_one(dfirst)
    dattend = dhidden_one.astype(bf16)
    dcontext = dot_t(dattend, output_all).astype(bf16)
    dcontext = dcontext.reshape(2, rows, HEAD_GROUPS, GROUP_WIDTH).transpose(0, 2, 1, 3)
    dcontext, late_context = lax.optimization_barrier((dcontext.reshape(8, rows, GROUP_WIDTH), context))
    dcontext = exchange(dcontext).reshape(8 * rows, GROUP_WIDTH)

    out_rows = width // seq_size
    ctx_split = late_context.reshape(n_own, chips, 2, out_rows)
    ctx_split = [ctx_split[:, :, i].reshape(n_own, width // 2) for i in range(2)]
    both_ctx = jnp.concatenate([pick(ctx_split, core), sflip(pick(ctx_split, 1 - core), 1)], axis=0)
    both_dattend = jnp.concatenate([dattend, sflip(dattend, 1)], axis=0)
    vectors = jnp.stack([dfirst_gain, dfirst_shift, dsecond_gain, dsecond_shift])
    other_blocks = other_grads(dinner, both_ctx, both_dattend, douter, vectors, chips)
    feed_blocks = feed_grads(both_first, dinner, active, both_douter, chips)
    feed_blocks, other_blocks, dcontext = lax.optimization_barrier((feed_blocks, other_blocks, dcontext))
    feed_sums = over_chips(feed_blocks)

    def halve(low, high, bit, mask):
        sent = jnp.where(bit == 0, high, low).astype(bf16)
        return jnp.where(bit == 0, low, high) + sflip(sent, mask).astype(jnp.float32)

    def halve_other(blocks, b):
        pairs = blocks.reshape((-1, 2) + blocks.shape[1:])
        return halve(pairs[:, 0], pairs[:, 1], (me >> (b + 1)) % 2, 2 << b)

    last = part_bits[-1]
    dqueries, sent, kept = attend_backward(
        queries, kv, key_tail, context_full, stats, dcontext, ((me // last) % 2).astype(jnp.int32).reshape(1)
    )
    dkv = (kept + sflip(sent, last).astype(jnp.float32)).reshape(n_parts // 2, 8 * rows, 2 * GROUP_WIDTH)
    for b in reversed(part_bits[:-1]):
        bit = (me // b) % 2
        n_now = dkv.shape[0] // 2
        low, high = dkv[:n_now], dkv[n_now:]
        sent = jnp.where(bit == 0, high, low).astype(bf16)
        dkv = jnp.where(bit == 0, low, high) + sflip(sent, b).astype(jnp.float32)
    dqkv = jnp.concatenate([dqueries, dkv[0].astype(bf16)], axis=1)
    other_sums = halve_other(other_blocks, 0)

    dx, late_x = lax.optimization_barrier((dot_t(dqkv, w_all).reshape(2, 2, 2, rows, width), x_all))
    da, db = dx[..., :half_width], dx[..., half_width:]

    da = halve(da[:, :, 0], da[:, :, 1], y0, YO)
    db = halve(db[:, 0], db[:, 1], z0, ZO)
    other_sums = halve_other(other_sums, 1)
    da, db, other_sums, feed_sums = lax.optimization_barrier((da, db, other_sums, feed_sums))
    feed_sums = over_groups(feed_sums)
    da = halve(da[:, 0], da[:, 1], z0, ZO)
    db = halve(db[:, 0], db[:, 1], y0, YO)
    dx = jnp.concatenate([da, db], axis=-1)
    mine = pick(dx, z1)
    theirs = sflip(pick(dx, 1 - z1).astype(bf16), HI).astype(jnp.float32)
    dtokens = dhidden_one.reshape(2, rows, width) + in_order(mine, theirs, z1)

    for b in range(2, log2_of(chips)):
        other_sums = halve_other(other_sums, b)
    other_sums = over_groups(other_sums[0].astype(bf16))
    r1 = 4 * out_rows
    inner_grad = feed_sums[:r1].reshape(2, 2, out_rows, width)
    inner_grad = [inner_grad[:, i] for i in range(2)]
    far = sflip(jnp.concatenate([pick(inner_grad, 1 - core).reshape(2 * out_rows, width), other_sums[out_rows:]], axis=0), 1)
    dinner_weight = in_order(pick(inner_grad, core), far[: 2 * out_rows].reshape(2, out_rows, width), core)
    dinner_weight = dinner_weight.transpose(2, 0, 1, 3).reshape(out_rows, 2, chips, piece).transpose(0, 2, 1, 3)
    dinner_weight = dinner_weight.reshape(out_rows, feed).astype(jnp.float32)
    douter_weight = feed_sums[r1:].astype(jnp.float32)
    doutput_weight = other_sums[:out_rows].astype(jnp.float32)
    small = other_sums[out_rows:].astype(jnp.float32)
    both = lax.dynamic_slice_in_dim(small + far[2 * out_rows :].astype(jnp.float32), me * out_rows, out_rows, axis=1)
    dfirst_gain, dfirst_shift, dsecond_gain, dsecond_shift, doutput_bias, douter_bias = (both[i] for i in range(6))
    dinner_bias = lax.dynamic_slice_in_dim(small[6:8].reshape(half_feed), (me // 2) * piece, piece)

    dw = t_dot(x_all, dqkv)
    dbias = column_sums(dqkv)
    dw = dw.reshape(seq_size, out_rows, 3 * GROUP_WIDTH)
    dw = jnp.concatenate([dw, jnp.broadcast_to(dbias, (seq_size, 8, 3 * GROUP_WIDTH))], axis=1)
    block = dw.shape[1]
    n_extra = 1 << len(extra_bits)
    dw = dw.reshape(2, 2, 2, n_extra, 2, 1, block, 3 * GROUP_WIDTH)[:, :, :, :, :, 0]
    dw = dw.reshape(2, 2, n_extra, 2, 2, block, 3 * GROUP_WIDTH)
    dw = halve(dw[:, :, :, :, 0], dw[:, :, :, :, 1], me % 2, 1)
    for b in reversed(extra_bits):
        m = dw.shape[2] // 2
        dw = halve(dw[:, :, :m], dw[:, :, m:], (me // b) % 2, b)
    dw = dw[:, :, 0]
    dw = halve(dw[0], dw[1], z1, HI)
    for b in range(log2_of(grp_size)):
        dw = dw + flip(dw.astype(bf16), "grp", grp_size, 1 << b).astype(jnp.float32)
    dw = dw.astype(bf16).reshape(HEAD_GROUPS, block, 3 * GROUP_WIDTH)

    def row_block(k):
        return lax.dynamic_index_in_dim(dw, head_group ^ k, 0, keepdims=False)

    w0 = row_block(0)
    w1 = sflip(row_block(1), YO)
    w2 = sflip(row_block(2), ZO)
    w3 = sflip(row_block(3), ZO | YO)
    dw = in_order(in_order(w0, w1, y0), in_order(w2, w3, y0), z0).reshape(HEAD_GROUPS, block, 3, GROUP_WIDTH)
    dw = dw.astype(jnp.float32).transpose(2, 1, 0, 3).reshape(3, block, width)
    dquery_weight, dkey_weight, dvalue_weight = dw[0, :out_rows], dw[1, :out_rows], dw[2, :out_rows]
    dquery_bias = lax.dynamic_slice_in_dim(dw[0, out_rows], me * out_rows, out_rows)
    dvalue_bias = lax.dynamic_slice_in_dim(dw[2, out_rows], me * out_rows, out_rows)

    return (
        layer_out.astype(bf16).reshape(2, rows, width),
        dtokens.astype(bf16),
        dquery_weight,
        dquery_bias,
        dkey_weight,
        dvalue_weight,
        dvalue_bias,
        doutput_weight,
        doutput_bias,
        dfirst_gain,
        dfirst_shift,
        dinner_weight,
        dinner_bias,
        douter_weight,
        douter_bias,
        dsecond_gain,
        dsecond_shift,
    )


def solution(mesh):
    in_specs = (
        P("grp", "seq", None),
        P("grp"),
        P(("grp", "seq"), None),
        P(("grp", "seq")),
        P(("grp", "seq"), None),
        P(("grp", "seq"), None),
        P(("grp", "seq")),
        P(("grp", "seq"), None),
        P(("grp", "seq")),
        P(("grp", "seq")),
        P(("grp", "seq")),
        P(("grp", "seq"), None),
        P(("grp", "seq")),
        P(("grp", "seq"), None),
        P(("grp", "seq")),
        P(("grp", "seq")),
        P(("grp", "seq")),
        P("grp", "seq", None),
    )
    out_specs = (
        P("grp", "seq", None),
        P("grp", "seq", None),
        P("seq", None),
        P("seq"),
        P("seq", None),
        P("seq", None),
        P("seq"),
        P("seq", None),
        P("seq"),
        P("seq"),
        P("seq"),
        P("seq", None),
        P("seq"),
        P("seq", None),
        P("seq"),
        P("seq"),
        P("seq"),
    )
    body = partial(per_device, mesh.shape["seq"], mesh.shape["grp"])
    return jax.shard_map(
        body, mesh=mesh, in_specs=in_specs, out_specs=out_specs, check_vma=False
    )
```
